32 devices in a mesh: groups: 2 (over x), tm: 16 (over z, y, core).
Axes of the slice: x: 2, y: 2, z: 4, core: 2. Of those that a mesh axis runs over, the one named last changes fastest.
Arguments:
- loglik: float32 [4, 1024, 512], P('groups', None, 'tm'), parts along dimension 0, may hold values from -105 to 105
- trans_weight: float32 [256, 256], replicated, may hold values from 0 to 1, as said below
- block_mask: int32 [4, 4], replicated, may hold values from 0 to 1, as said below
- init_weight: float32 [256], replicated, may hold values from 0.01 to 1
- lengths: int32 [4], P('groups'), parts along dimension 0, may hold values from 512 to 1024, as said below
- pdf_map: int32 [256], replicated, may hold values from 0 to 511
Outputs:
- log_forward: float32 [4, 1024, 256], P('groups', 'tm'), parts along dimension 0
- log_gain: float32 [4, 1024], P('groups', 'tm'), parts along dimension 0
The draws below stay inside these ranges and needn't reach their ends.
There are 2 independent parts, one for each index of `groups`. The reference program is written for one: setup_inputs(seed, part) draws one part's arguments, and reference() takes and returns one part's arrays. A program takes and returns all parts, laid end to end along the dimension named above; an argument that names none is the same for every part. Nothing has to cross between parts.
Inputs may be any that keep to these rules, and one draw needn't show every extreme that they name: `block_mask`: the diagonal blocks are always allowed. `lengths`: some utterance has all 1024 frames. `trans_weight`: every entry is positive.
All inputs are finite; a program needn't handle non-finite values.
Results may differ from the reference program's by a relative error of at most 0.0003.
Values sent between devices are 32-bit elements; how exact they have to be, the bound alone decides.
No kernel may reach another device: no remote copies, remote signals or barrier semaphores. Data moves between devices by JAX's collectives and lax.ppermute only.
A program may use at most 128 MiB of HBM per device.

```python
import math
import jax
import jax.numpy as jnp
from jax import lax

S = 256
BLK = 64
NB = 4
P_SIZE = 512
UTT = 2
T_SIZE = 1024


def draw_block_mask(key, part):
    others = jax.random.randint(key, (NB, NB), 0, 2).astype(jnp.int32)
    return jnp.maximum(others, jnp.eye(NB, dtype=jnp.int32)).astype(jnp.int32)


def draw_lengths(key, part):
    spread = jax.random.randint(key, (UTT,), T_SIZE // 2, T_SIZE + 1).astype(jnp.int32)
    chosen = jax.random.randint(jax.random.fold_in(key, 7), (), 0, UTT)
    return spread.at[chosen].set(T_SIZE).astype(jnp.int32)


def spread_log(key, index, shape, low, high):
    fraction = jax.random.uniform(jax.random.fold_in(key, index), shape, jnp.float32, 0.0, 1.0)
    return jnp.exp(math.log(low) + fraction * (math.log(high) - math.log(low)))


def draw_trans_weight(key, part):
    source = jnp.arange(S, dtype=jnp.int32)[:, None]
    target = jnp.arange(S, dtype=jnp.int32)[None, :]
    inside = source // BLK == target // BLK
    ahead = (target % BLK - source % BLK) % BLK
    stay = spread_log(key, 1, (S, S), 0.3, 1.0)
    onward = spread_log(key, 2, (S, S), 0.1, 0.6)
    jump = spread_log(key, 3, (S, S), 0.01, 0.1)
    faint = spread_log(key, 4, (S, S), 1e-05, 0.0001)
    rates = spread_log(key, 5, (NB,), 1e-05, 0.03)
    row_rate = jnp.repeat(rates, BLK)[:, None]
    leak = row_rate * spread_log(key, 6, (S, S), 0.3, 1.0) / BLK
    local = jnp.where(ahead == 0, stay, jnp.where(ahead == 1, onward, jnp.where(ahead == 2, jump, faint)))
    return jnp.where(inside, local, leak).astype(jnp.float32)


def draw_loglik(key, part):
    noise_key = jax.random.fold_in(key, 11)
    shift_key = jax.random.fold_in(key, 12)
    noise = jnp.clip(jax.random.normal(noise_key, (UTT, T_SIZE, P_SIZE), jnp.float32), -4.0, 4.0)
    shift = jax.random.uniform(shift_key, (UTT, T_SIZE, 1), jnp.float32, -40.0, 40.0)
    return (shift + 0.2 * noise).astype(jnp.float32)


def with_ends(entries, own_key, low, top_value):
    extent = entries.shape
    spot = [jax.random.randint(jax.random.fold_in(own_key, axis), (), 0, extent[axis]) for axis in range(len(extent))]
    entries = entries.at[tuple(spot)].set(low)
    longest = extent.index(max(extent))
    spot[longest] = (spot[longest] + 1) % extent[longest]
    return entries.at[tuple(spot)].set(top_value)


def setup_inputs(seed: int = 0, part: int = 0) -> dict:
    key_of = jax.random.split(jax.random.key(seed), 7)
    part_splits = jax.random.split(jax.random.fold_in(key_of[6], part), 7)
    return {
        "loglik": draw_loglik(jax.random.fold_in(jax.random.fold_in(key_of[6], part), 71), part),
        "trans_weight": draw_trans_weight(jax.random.fold_in(key_of[6], 71), part),
        "block_mask": draw_block_mask(jax.random.fold_in(key_of[6], 71), part),
        "init_weight": jnp.clip(jnp.exp(jax.random.uniform(key_of[3], (S,), jnp.float32, math.log(0.01), math.log(1.0))), 0.01, 1.0),
        "lengths": draw_lengths(jax.random.fold_in(jax.random.fold_in(key_of[6], part), 71), part),
        "pdf_map": with_ends(jax.random.randint(key_of[5], (S,), 0, P_SIZE), jax.random.fold_in(key_of[5], 1), 0, P_SIZE - 1).astype(jnp.int32),
    }


def transitions(trans_weight, block_mask):
    expanded = jnp.repeat(jnp.repeat(block_mask, BLK, axis=0), BLK, axis=1).astype(jnp.float32)
    masked = trans_weight * expanded
    return masked / jnp.sum(masked, axis=1, keepdims=True)


def reference(loglik, trans_weight, block_mask, init_weight, lengths, pdf_map):
    trans = transitions(trans_weight, block_mask)
    start = init_weight / jnp.sum(init_weight)
    frames = jnp.take(loglik, pdf_map, axis=2)
    frames = jnp.moveaxis(frames, 1, 0)
    steps_all = jnp.arange(T_SIZE, dtype=jnp.int32)

    def advance(alpha, inputs):
        g_row, when = inputs
        top = jnp.max(g_row, axis=1, keepdims=True)
        factor = jnp.exp(g_row - top)
        v_new = jnp.dot(alpha, trans, precision=lax.Precision.HIGHEST) * factor
        total = jnp.sum(v_new, axis=1, keepdims=True)
        alive = when < lengths
        fresh = jnp.where(alive[:, None], v_new / total, alpha)
        gain = jnp.where(alive, jnp.log(total[:, 0]) + top[:, 0], jnp.float32(0.0))
        return fresh, (fresh, gain)

    first = jnp.broadcast_to(start, (loglik.shape[0], S)).astype(jnp.float32)
    _, (states, gains) = lax.scan(advance, first, (frames, steps_all))
    return jnp.log(jnp.moveaxis(states, 0, 1)), jnp.moveaxis(gains, 0, 1)
```

```python
import functools
import jax
import jax.numpy as jnp
from jax import lax
from jax.experimental import pallas as pl
from jax.experimental.pallas import tpu as pltpu
from jax.sharding import PartitionSpec as P

F32 = jnp.float32
BF16 = jnp.bfloat16
SUB = 8


def halves(x):
    high = x.astype(BF16)
    return high, (x - high.astype(F32)).astype(BF16)


def dot(a, b):
    return jnp.dot(a, b, preferred_element_type=F32)


def dot3(a_high, a_low, b_high, b_low):
    return dot(a_high, b_high) + dot(a_low, b_high) + dot(a_high, b_low)


def transfer_kernel(
    frames,
    lengths_ref,
    mask_ref,
    cols_ref,
    weight_ref,
    map_ref,
    chip_ref,
    pre_ref,
    e_ref,
    top_ref,
    th_ref,
    tl_ref,
    g_scr,
    e_scr,
    t_scr,
    ah,
    al,
    bh,
    bl,
):
    states = weight_ref.shape[0]
    half = frames // 2
    rows = states // 2
    blocks = half // SUB
    core = lax.axis_index("tm") % 2
    first_frame = (lax.axis_index("tm") // 2) * frames
    alive = lengths_ref[core] - first_frame

    nb = mask_ref.shape[0]
    width = states // nb
    lane = lax.broadcasted_iota(jnp.int32, (1, states), 1) // width
    for r in range(nb):
        row = jnp.zeros((1, states), F32)
        for c in range(nb):
            row = jnp.where(lane == c, mask_ref[r, c].astype(F32), row)
        part = weight_ref[r * width : (r + 1) * width, :] * row
        t_scr[r * width : (r + 1) * width, :] = part / jnp.sum(part, axis=1, keepdims=True)
    th, tl = halves(t_scr[...])
    th_ref[...] = th
    tl_ref[...] = tl

    cols = cols_ref[...].T
    pick = (lax.broadcasted_iota(jnp.int32, (cols.shape[1], states), 0) == map_ref[...]).astype(F32).astype(BF16)
    p1 = cols.astype(BF16)
    rest = cols - p1.astype(F32)
    p2, p3 = halves(rest)
    depth = 256
    pieces = cols.shape[1] // depth

    def gather(*accs):
        for k in range(pieces):
            cut = slice(k * depth, (k + 1) * depth)
            pltpu.matmul_push_rhs(pick[cut, :], 0, k % 2)
            pltpu.matmul_acc_lhs(accs[k % 2], p1[:, cut], 0)
            pltpu.matmul_acc_lhs(accs[k % 2], p2[:, cut], None)
            pltpu.matmul_acc_lhs(accs[k % 2], p3[:, cut], None)
        g_scr[...] = pltpu.matmul_pop(accs[0]) + pltpu.matmul_pop(accs[1])

    pl.run_scoped(gather, pltpu.ACC(0)((frames, states), F32), pltpu.ACC(1)((frames, states), F32))
    g = g_scr[...]
    top = jnp.max(g, axis=1, keepdims=True)
    e = jnp.exp(g - top)
    e_scr[...] = e
    for k in range(states // 128):
        e_ref[k] = e[:, k * 128 : (k + 1) * 128]
    top_ref[...] = jnp.broadcast_to(top, (frames, 128))

    eye = (
        lax.broadcasted_iota(jnp.int32, (states, states), 0) == lax.broadcasted_iota(jnp.int32, (states, states), 1)
    ).astype(F32)
    for mh, ml, off in ((ah, al, 0), (bh, bl, half)):
        h, l = halves(jnp.where(alive > off, t_scr[...] * e_scr[off : off + 1, :], eye))
        mh[0:states, :] = h
        ml[0:states, :] = l

    def body(a0, a1, b0, b1):
        accs = ((a0, a1), (b0, b1))
        mats = ((ah, al), (bh, bl))

        def issue_a(high_loaded):
            for m in range(2):
                sl = pl.ds(m * rows, rows)
                pltpu.matmul_acc_lhs(accs[0][m], ah[sl, :], high_loaded)
                pltpu.matmul_acc_lhs(accs[0][m], al[sl, :], None)
            for m in range(2):
                pltpu.matmul_push_rhs(tl_ref[...], 1, m)
            for m in range(2):
                pltpu.matmul_acc_lhs(accs[0][m], ah[pl.ds(m * rows, rows), :], 1)

        def issue_b():
            for m in range(2):
                pltpu.matmul_acc_lhs(accs[1][m], bh[pl.ds(m * rows, rows), :], None)
            for m in range(2):
                pltpu.matmul_push_rhs(th_ref[...], 0, m)
            for m in range(2):
                sl = pl.ds(m * rows, rows)
                pltpu.matmul_acc_lhs(accs[1][m], bh[sl, :], 0)
                pltpu.matmul_acc_lhs(accs[1][m], bl[sl, :], None)

        def post(k, s, peak):
            mh, ml = mats[k]
            frame = s + k * half
            er = e_scr[pl.ds(frame, 1), :] * (1.0 / jnp.max(peak.astype(F32), keepdims=True)[:, :1])
            base = jnp.where(frame < alive, 0, states)
            new = None
            for m in range(2):
                x = pltpu.matmul_pop(accs[k][m]) * er
                h, l = halves(x)
                at = pl.multiple_of(base + m * rows, rows)
                mh[pl.ds(at, rows), :] = h
                ml[pl.ds(at, rows), :] = l
                y = jnp.max(h.reshape(rows // 16, 16, states), axis=0)
                new = y if new is None else jnp.maximum(new, y)
            return new

        def keep(j):
            for k in range(2):
                for i in range(2):
                    pre_ref[k, j, i] = mats[k][i][0:states, :]

        for m in range(2):
            pltpu.matmul_push_rhs(th_ref[...], 0, m)
        issue_a(0)
        one = jnp.ones((16, states), BF16)

        def step(s, peaks, last=False):
            pa, pb = peaks
            issue_b()
            pa = post(0, s, pa)
            if not last:
                issue_a(None)
            pb = post(1, s, pb)
            return pa, pb

        def block(j, peaks):
            for r in range(1, SUB):
                peaks = step(j * SUB + r, peaks)
            keep(j)
            return step(j * SUB + SUB, peaks)

        peaks = lax.fori_loop(0, blocks - 1, block, (one, one))
        for r in range(1, SUB):
            peaks = step((blocks - 1) * SUB + r, peaks, r == SUB - 1)
        keep(blocks - 1)
        for m in range(2):
            sl = pl.ds(m * rows, rows)
            pltpu.matmul_push_rhs(bh[0:states, :], 0, m)
            pltpu.matmul_acc_lhs(accs[0][m], ah[sl, :], 0)
            pltpu.matmul_acc_lhs(accs[0][m], al[sl, :], None)
            pltpu.matmul_push_rhs(bl[0:states, :], 1, m)
            pltpu.matmul_acc_lhs(accs[0][m], ah[sl, :], 1)
        c = jnp.concatenate([pltpu.matmul_pop(accs[0][m]) for m in range(2)], axis=0)
        chip_ref[...] = c * (1.0 / jnp.max(c, keepdims=True)[:, :1])

    shape = (rows, states)
    pl.run_scoped(
        body,
        pltpu.ACC(0)(shape, F32),
        pltpu.ACC(1)(shape, F32),
        pltpu.ACC(0)(shape, F32),
        pltpu.ACC(1)(shape, F32),
    )


def vmem():
    return pl.BlockSpec(memory_space=pltpu.VMEM)


def smem():
    return pl.BlockSpec(memory_space=pltpu.SMEM)


def transfer(cols, weight, mask, lengths, pdf_map):
    columns, frames = cols.shape
    states = weight.shape[0]
    blocks = frames // 2 // SUB
    out = jax.ShapeDtypeStruct
    return pl.pallas_call(
        functools.partial(transfer_kernel, frames),
        out_shape=(
            out((states, states), F32),
            out((2, blocks, 2, states, states), BF16),
            out((states // 128, frames, 128), F32),
            out((frames, 128), F32),
            out((states, states), BF16),
            out((states, states), BF16),
        ),
        in_specs=[smem(), smem(), vmem(), vmem(), vmem()],
        out_specs=[vmem()] * 6,
        scratch_shapes=[pltpu.VMEM((frames, states), F32)] * 2
        + [pltpu.VMEM((states, states), F32)]
        + [pltpu.VMEM((2 * states, states), BF16)] * 4,
        compiler_params=pltpu.CompilerParams(vmem_limit_bytes=40 << 20),
        name="transfer",
    )(lengths, mask, cols, weight, pdf_map[None, :])


def row_dot(v, matrix_high, matrix_low):
    n = v.shape[0]
    vh, vl = halves(v)
    both = jnp.concatenate([vh, vl], axis=0)
    x = dot(both, matrix_high)
    return x[0:n] + x[n:] + dot(vh, matrix_low)


def unit(v):
    return v / jnp.sum(v, axis=1, keepdims=True)


def plane_kernel(own_ref, other_ref, init_ref, dh_ref, dl_ref, v_ref):
    chip = lax.axis_index("tm") // 2
    plane = chip // 2

    def product(left, right):
        d = dot3(*halves(left[...]), *halves(right[...]))
        h, l = halves(d * (1.0 / jnp.max(d, keepdims=True)[:, :1]))
        dh_ref[...] = h
        dl_ref[...] = l

    @pl.when(chip % 2 == 0)
    def _():
        product(own_ref, other_ref)

    @pl.when(chip % 2 == 1)
    def _():
        product(other_ref, own_ref)

    start = jnp.broadcast_to(unit(init_ref[...]), v_ref.shape)
    v_ref[...] = unit(row_dot(start, dh_ref[...], dl_ref[...]))


def plane_product(own, other, init):
    states = own.shape[0]
    out = jax.ShapeDtypeStruct
    return pl.pallas_call(
        plane_kernel,
        out_shape=(out((states, states), BF16), out((states, states), BF16), out((8, states), F32)),
        in_specs=[vmem()] * 3,
        out_specs=[vmem()] * 3,
        name="plane",
    )(own, other, init[None, :])


def hop_kernel(v_ref, dh_ref, dl_ref, out_ref):
    out_ref[...] = unit(row_dot(v_ref[...], dh_ref[...], dl_ref[...]))


def hop(v, dh, dl):
    return pl.pallas_call(
        hop_kernel,
        out_shape=jax.ShapeDtypeStruct(v.shape, F32),
        in_specs=[vmem()] * 3,
        out_specs=vmem(),
        name="hop",
    )(v, dh, dl)


def frames_kernel(
    frames,
    planes,
    lengths_ref,
    *refs,
):
    v_refs = refs[: planes - 1]
    init_ref, other_ref, pre_ref, e_ref, top_ref, th_ref, tl_ref, kept_ref, sent_ref, gain_ref, alpha_scr = refs[
        planes - 1 :
    ]
    states = th_ref.shape[0]
    half = frames // 2
    blocks = half // SUB
    subs = 2 * blocks
    index = lax.axis_index("tm")
    core = index % 2
    chip = index // 2
    alive = lengths_ref[core] - chip * frames

    v = jnp.broadcast_to(unit(init_ref[...]), (8, states))
    for g in range(1, planes):
        v = jnp.where(chip // 2 == g, v_refs[g - 1][...], v)
    oh, ol = halves(other_ref[...])
    v = jnp.where(chip % 2 == 1, unit(row_dot(v, oh, ol)), v)
    mid = unit(row_dot(v, pre_ref[0, blocks - 1, 0], pre_ref[0, blocks - 1, 1]))
    rows = [v[0:1]]
    for j in range(blocks - 1):
        rows.append(row_dot(v, pre_ref[0, j, 0], pre_ref[0, j, 1])[0:1])
    rows.append(mid[0:1])
    for j in range(blocks - 1):
        rows.append(row_dot(mid, pre_ref[1, j, 0], pre_ref[1, j, 1])[0:1])
    alpha = unit(jnp.concatenate(rows, axis=0))
    th, tl = th_ref[...], tl_ref[...]
    lane = lax.broadcasted_iota(jnp.int32, (subs, 128), 1)
    sub = lax.broadcasted_iota(jnp.int32, (subs, 128), 0)
    gains = jnp.zeros((subs, 128), F32)
    tiles = range(states // 128)
    for r in range(SUB):
        every = pl.ds(r, subs, stride=SUB)
        x = row_dot(alpha, th, tl) * jnp.concatenate([e_ref[k, every, :] for k in tiles], axis=1)
        total = jnp.sum(x, axis=1, keepdims=True)
        alpha = x / total
        for k in tiles:
            alpha_scr[k, every, :] = alpha[:, k * 128 : (k + 1) * 128]
        live = sub * SUB + r < alive
        gain = jnp.where(live, jnp.log(total) + top_ref[every, :], 0.0)
        gains = jnp.where(lane % SUB == r, gain, gains)
    end = pl.ds(jnp.clip(alive - 1, 0, frames - 1), 1)
    for which, ref in ((core, kept_ref), (1 - core, sent_ref)):
        at = pl.multiple_of(which * half, half)
        frame = at + lax.broadcasted_iota(jnp.int32, (half, 128), 0)
        for k in tiles:
            cut = slice(k * 128, (k + 1) * 128)
            final = jnp.where(alive > 0, alpha_scr[k, end, :], v[0:1, cut])
            ref[0:half, cut] = jnp.log(jnp.where(frame < alive, alpha_scr[k, pl.ds(at, half), :], final))
    picked = jnp.where(lane // SUB == sub % blocks, gains, 0.0)
    lines = [jnp.sum(picked[k * blocks : (k + 1) * blocks], axis=0, keepdims=True) for k in range(2)]
    gain_ref[...] = jnp.where(core == 0, lines[0], lines[1])
    line = jnp.where(core == 0, lines[1], lines[0])
    sent_ref[half : half + 8, :] = jnp.concatenate([jnp.broadcast_to(line, (8, 128))] * (states // 128), axis=1)


def frames_pass(lengths, vs, init, other, pre, e, top, th, tl):
    frames, states = top.shape[0], th.shape[0]
    half = frames // 2
    out = jax.ShapeDtypeStruct
    return pl.pallas_call(
        functools.partial(frames_kernel, frames, len(vs) + 1),
        out_shape=(out((half, states), F32), out((half + 8, states), F32), out((1, 128), F32)),
        in_specs=[smem()] + [vmem()] * (len(vs) + 7),
        out_specs=[vmem()] * 3,
        scratch_shapes=[pltpu.VMEM((states // 128, frames, 128), F32)],
        compiler_params=pltpu.CompilerParams(vmem_limit_bytes=40 << 20),
        name="frames",
    )(lengths, *vs, init[None, :], other, pre, e, top, th, tl)


def join_kernel(kept_ref, gain_ref, got_ref, log_ref, out_gain_ref):
    half = kept_ref.shape[0]
    core = lax.axis_index("tm") % 2
    log_ref[core] = kept_ref[...]
    log_ref[1 - core] = got_ref[0:half, :]
    own = gain_ref[0:1, 0:half]
    got = got_ref[half : half + 1, 0:half]
    out_gain_ref[0:1, :] = jnp.where(core == 0, own, got)
    out_gain_ref[1:2, :] = jnp.where(core == 0, got, own)


def join(kept, gain, got):
    half, states = kept.shape
    out = jax.ShapeDtypeStruct
    return pl.pallas_call(
        join_kernel,
        out_shape=(out((2, half, states), F32), out((2, half), F32)),
        in_specs=[vmem()] * 3,
        out_specs=[vmem()] * 2,
        name="join",
    )(kept, gain, got)


def shards(size, loglik, trans_weight, block_mask, init_weight, lengths, pdf_map):
    utts, total, local = loglik.shape
    chips = size // 2
    frames = total // chips
    planes = chips // 2
    x = jnp.transpose(loglik, (0, 2, 1)).reshape(utts, local, chips, frames)
    x = jnp.transpose(x, (2, 0, 1, 3)).reshape(size, local, frames)
    cols = lax.all_to_all(x, "tm", 0, 0, tiled=True).reshape(size * local, frames)
    chip, pre, e, top, th, tl = transfer(cols, trans_weight, block_mask, lengths, pdf_map)
    other = lax.ppermute(chip, "tm", [(i, i ^ 2) for i in range(size)])
    dh, dl, v = plane_product(chip, other, init_weight)
    vs = []
    for g in range(1, planes):
        got = lax.ppermute(v, "tm", [(4 * (g - 1) + i, 4 * g + i) for i in range(4)])
        vs.append(got)
        if g < planes - 1:
            v = hop(got, dh, dl)
    kept, sent, gain = frames_pass(lengths, vs, init_weight, other, pre, e, top, th, tl)
    got = lax.ppermute(sent, "tm", [(i, i ^ 1) for i in range(size)])
    return join(kept, gain, got)


def solution(mesh):
    return jax.shard_map(
        functools.partial(shards, mesh.shape["tm"]),
        mesh=mesh,
        in_specs=(P("groups", None, "tm"), P(), P(), P(), P("groups"), P()),
        out_specs=(P("groups", "tm", None), P("groups", "tm")),
        check_vma=False,
    )
```

```python
import functools
import jax
import jax.numpy as jnp
from jax import lax
from jax.experimental import pallas as pl
from jax.experimental.pallas import tpu as pltpu
from jax.sharding import PartitionSpec as P

F32 = jnp.float32
BF16 = jnp.bfloat16
SUB = 8


def halves(x):
    high = x.astype(BF16)
    return high, (x - high.astype(F32)).astype(BF16)


def dot(a, b):
    return jnp.dot(a, b, preferred_element_type=F32)


def dot3(a_high, a_low, b_high, b_low):
    return dot(a_high, b_high) + dot(a_low, b_high) + dot(a_high, b_low)


def transfer_kernel(
    frames,
    lengths_hbm,
    mask_hbm,
    weight_hbm,
    map_hbm,
    cols_ref,
    chip_ref,
    pre_ref,
    e_ref,
    top_ref,
    th_ref,
    tl_ref,
    g_scr,
    e_scr,
    t_scr,
    ah,
    al,
    bh,
    bl,
    lengths_ref,
    mask_ref,
    weight_ref,
    map_ref,
    sems,
):
    copies = [
        pltpu.make_async_copy(src, dst, sems.at[i])
        for i, (src, dst) in enumerate(
            (
                (map_hbm, map_ref),
                (weight_hbm, weight_ref),
                (mask_hbm, mask_ref),
                (lengths_hbm, lengths_ref),
            )
        )
    ]
    for copy in copies:
        copy.start()
    states = weight_ref.shape[0]
    half = frames // 2
    rows = states // 2
    blocks = half // SUB
    core = lax.axis_index("tm") % 2
    first_frame = (lax.axis_index("tm") // 2) * frames
    cols = cols_ref[...].T
    copies[0].wait()
    pick = (lax.broadcasted_iota(jnp.int32, (cols.shape[1], states), 0) == map_ref[...]).astype(F32).astype(BF16)
    p1 = cols.astype(BF16)
    rest = cols - p1.astype(F32)
    p2, p3 = halves(rest)
    depth = 256
    pieces = cols.shape[1] // depth

    def gather(*accs):
        for k in range(pieces):
            cut = slice(k * depth, (k + 1) * depth)
            pltpu.matmul_push_rhs(pick[cut, :], 0, k % 2)
            pltpu.matmul_acc_lhs(accs[k % 2], p1[:, cut], 0)
            pltpu.matmul_acc_lhs(accs[k % 2], p2[:, cut], None)
            pltpu.matmul_acc_lhs(accs[k % 2], p3[:, cut], None)
        g_scr[...] = pltpu.matmul_pop(accs[0]) + pltpu.matmul_pop(accs[1])

    pl.run_scoped(gather, pltpu.ACC(0)((frames, states), F32), pltpu.ACC(1)((frames, states), F32))
    g = g_scr[...]
    top = jnp.max(g, axis=1, keepdims=True)
    e = jnp.exp(g - top)
    e_scr[...] = e
    for k in range(states // 128):
        e_ref[k] = e[:, k * 128 : (k + 1) * 128]
    top_ref[...] = jnp.broadcast_to(top, (frames, 128))

    for copy in copies[1:]:
        copy.wait()
    alive = lengths_ref[core] - first_frame

    nb = mask_ref.shape[0]
    width = states // nb
    lane = lax.broadcasted_iota(jnp.int32, (1, states), 1) // width
    for r in range(nb):
        row = jnp.zeros((1, states), F32)
        for c in range(nb):
            row = jnp.where(lane == c, mask_ref[r, c].astype(F32), row)
        part = weight_ref[r * width : (r + 1) * width, :] * row
        t_scr[r * width : (r + 1) * width, :] = part / jnp.sum(part, axis=1, keepdims=True)
    th, tl = halves(t_scr[...])
    th_ref[...] = th
    tl_ref[...] = tl

    eye = (
        lax.broadcasted_iota(jnp.int32, (states, states), 0) == lax.broadcasted_iota(jnp.int32, (states, states), 1)
    ).astype(F32)
    for mh, ml, off in ((ah, al, 0), (bh, bl, half)):
        h, l = halves(jnp.where(alive > off, t_scr[...] * e_scr[off : off + 1, :], eye))
        mh[0:states, :] = h
        ml[0:states, :] = l

    def body(a0, a1, b0, b1):
        accs = ((a0, a1), (b0, b1))
        mats = ((ah, al), (bh, bl))

        def issue_a(high_loaded):
            for m in range(2):
                sl = pl.ds(m * rows, rows)
                pltpu.matmul_acc_lhs(accs[0][m], ah[sl, :], high_loaded)
                pltpu.matmul_acc_lhs(accs[0][m], al[sl, :], None)
            for m in range(2):
                pltpu.matmul_push_rhs(tl_ref[...], 1, m)
            for m in range(2):
                pltpu.matmul_acc_lhs(accs[0][m], ah[pl.ds(m * rows, rows), :], 1)

        def issue_b():
            for m in range(2):
                pltpu.matmul_acc_lhs(accs[1][m], bh[pl.ds(m * rows, rows), :], None)
            for m in range(2):
                pltpu.matmul_push_rhs(th_ref[...], 0, m)
            for m in range(2):
                sl = pl.ds(m * rows, rows)
                pltpu.matmul_acc_lhs(accs[1][m], bh[sl, :], 0)
                pltpu.matmul_acc_lhs(accs[1][m], bl[sl, :], None)

        def post(k, s, peak):
            mh, ml = mats[k]
            frame = s + k * half
            er = e_scr[pl.ds(frame, 1), :] * (1.0 / jnp.max(peak.astype(F32), keepdims=True)[:, :1])
            base = jnp.where(frame < alive, 0, states)
            new = None
            for m in range(2):
                x = pltpu.matmul_pop(accs[k][m]) * er
                h, l = halves(x)
                at = pl.multiple_of(base + m * rows, rows)
                mh[pl.ds(at, rows), :] = h
                ml[pl.ds(at, rows), :] = l
                y = jnp.max(h.reshape(rows // 16, 16, states), axis=0)
                new = y if new is None else jnp.maximum(new, y)
            return new

        def keep(j):
            for k in range(2):
                for i in range(2):
                    pre_ref[k, j, i] = mats[k][i][0:states, :]

        for m in range(2):
            pltpu.matmul_push_rhs(th_ref[...], 0, m)
        issue_a(0)
        one = jnp.ones((16, states), BF16)

        def step(s, peaks, last=False):
            pa, pb = peaks
            issue_b()
            pa = post(0, s, pa)
            if not last:
                issue_a(None)
            pb = post(1, s, pb)
            return pa, pb

        def block(j, peaks):
            for r in range(1, SUB):
                peaks = step(j * SUB + r, peaks)
            keep(j)
            return step(j * SUB + SUB, peaks)

        peaks = lax.fori_loop(0, blocks - 1, block, (one, one))
        for r in range(1, SUB):
            peaks = step((blocks - 1) * SUB + r, peaks, r == SUB - 1)
        keep(blocks - 1)
        for m in range(2):
            sl = pl.ds(m * rows, rows)
            pltpu.matmul_push_rhs(bh[0:states, :], 0, m)
            pltpu.matmul_acc_lhs(accs[0][m], ah[sl, :], 0)
            pltpu.matmul_acc_lhs(accs[0][m], al[sl, :], None)
            pltpu.matmul_push_rhs(bl[0:states, :], 1, m)
            pltpu.matmul_acc_lhs(accs[0][m], ah[sl, :], 1)
        c = jnp.concatenate([pltpu.matmul_pop(accs[0][m]) for m in range(2)], axis=0)
        chip_ref[...] = c * (1.0 / jnp.max(c, keepdims=True)[:, :1])

    shape = (rows, states)
    pl.run_scoped(
        body,
        pltpu.ACC(0)(shape, F32),
        pltpu.ACC(1)(shape, F32),
        pltpu.ACC(0)(shape, F32),
        pltpu.ACC(1)(shape, F32),
    )


def vmem():
    return pl.BlockSpec(memory_space=pltpu.VMEM)


def hbm():
    return pl.BlockSpec(memory_space=pltpu.MemorySpace.HBM)


def pinned(x):
    return pltpu.with_memory_space_constraint(x, pltpu.MemorySpace.HBM)


def transfer(cols, weight, mask, lengths, pdf_map):
    columns, frames = cols.shape
    states = weight.shape[0]
    blocks = frames // 2 // SUB
    out = jax.ShapeDtypeStruct
    return pl.pallas_call(
        functools.partial(transfer_kernel, frames),
        out_shape=(
            out((states, states), F32),
            out((2, blocks, 2, states, states), BF16),
            out((states // 128, frames, 128), F32),
            out((frames, 128), F32),
            out((states, states), BF16),
            out((states, states), BF16),
        ),
        in_specs=[hbm()] * 4 + [vmem()],
        out_specs=[vmem()] * 6,
        scratch_shapes=[pltpu.VMEM((frames, states), F32)] * 2
        + [pltpu.VMEM((states, states), F32)]
        + [pltpu.VMEM((2 * states, states), BF16)] * 4
        + [
            pltpu.SMEM(lengths.shape, jnp.int32),
            pltpu.SMEM(mask.shape, jnp.int32),
            pltpu.VMEM(weight.shape, F32),
            pltpu.VMEM((1, states), jnp.int32),
            pltpu.SemaphoreType.DMA((4,)),
        ],
        compiler_params=pltpu.CompilerParams(vmem_limit_bytes=6 << 20),
        name="transfer",
    )(*map(pinned, (lengths, mask, weight, pdf_map[None, :])), cols)


def row_dot(v, matrix_high, matrix_low):
    n = v.shape[0]
    vh, vl = halves(v)
    both = jnp.concatenate([vh, vl], axis=0)
    x = dot(both, matrix_high)
    return x[0:n] + x[n:] + dot(vh, matrix_low)


def unit(v):
    return v / jnp.sum(v, axis=1, keepdims=True)


def plane_kernel(init_hbm, own_ref, other_ref, dh_ref, dl_ref, v_ref, start_ref, init_ref, sem):
    copy = pltpu.make_async_copy(init_hbm, init_ref, sem)
    copy.start()
    chip = lax.axis_index("tm") // 2
    plane = chip // 2

    def product(left, right):
        d = dot3(*halves(left[...]), *halves(right[...]))
        h, l = halves(d * (1.0 / jnp.max(d, keepdims=True)[:, :1]))
        dh_ref[...] = h
        dl_ref[...] = l

    @pl.when(chip % 2 == 0)
    def _():
        product(own_ref, other_ref)

    @pl.when(chip % 2 == 1)
    def _():
        product(other_ref, own_ref)

    copy.wait()
    start = jnp.broadcast_to(unit(init_ref[...]), v_ref.shape)
    start_ref[...] = start
    v_ref[...] = unit(row_dot(start, dh_ref[...], dl_ref[...]))


def plane_product(own, other, init):
    states = own.shape[0]
    out = jax.ShapeDtypeStruct
    return pl.pallas_call(
        plane_kernel,
        out_shape=(out((states, states), BF16),) * 2 + (out((8, states), F32),) * 2,
        in_specs=[hbm()] + [vmem()] * 2,
        out_specs=[vmem()] * 4,
        scratch_shapes=[pltpu.VMEM((1, states), F32), pltpu.SemaphoreType.DMA],
        compiler_params=pltpu.CompilerParams(vmem_limit_bytes=4 << 20),
        name="plane",
    )(pinned(init[None, :]), own, other)


def hop_kernel(v_ref, dh_ref, dl_ref, out_ref):
    out_ref[...] = unit(row_dot(v_ref[...], dh_ref[...], dl_ref[...]))


def hop(v, dh, dl):
    return pl.pallas_call(
        hop_kernel,
        out_shape=jax.ShapeDtypeStruct(v.shape, F32),
        in_specs=[vmem()] * 3,
        out_specs=vmem(),
        compiler_params=pltpu.CompilerParams(vmem_limit_bytes=4 << 20),
        name="hop",
    )(v, dh, dl)


def frames_kernel(
    frames,
    planes,
    lengths_hbm,
    *refs,
):
    v_refs = refs[: planes - 1]
    start_ref, other_ref, pre_ref, e_ref, top_ref, th_ref, tl_ref, kept_ref, sent_ref, gain_ref, *scratch = refs[
        planes - 1 :
    ]
    alpha_scr, lengths_ref, sem = scratch
    copy = pltpu.make_async_copy(lengths_hbm, lengths_ref, sem)
    copy.start()
    states = th_ref.shape[0]
    half = frames // 2
    blocks = half // SUB
    subs = 2 * blocks
    index = lax.axis_index("tm")
    core = index % 2
    chip = index // 2
    v = start_ref[...]
    for g in range(1, planes):
        v = jnp.where(chip // 2 == g, v_refs[g - 1][...], v)
    oh, ol = halves(other_ref[...])
    v = jnp.where(chip % 2 == 1, unit(row_dot(v, oh, ol)), v)
    mid = unit(row_dot(v, pre_ref[0, blocks - 1, 0], pre_ref[0, blocks - 1, 1]))
    rows = [v[0:1]]
    for j in range(blocks - 1):
        rows.append(row_dot(v, pre_ref[0, j, 0], pre_ref[0, j, 1])[0:1])
    rows.append(mid[0:1])
    for j in range(blocks - 1):
        rows.append(row_dot(mid, pre_ref[1, j, 0], pre_ref[1, j, 1])[0:1])
    alpha = unit(jnp.concatenate(rows, axis=0))
    th, tl = th_ref[...], tl_ref[...]
    lane = lax.broadcasted_iota(jnp.int32, (subs, 128), 1)
    sub = lax.broadcasted_iota(jnp.int32, (subs, 128), 0)
    gains = jnp.zeros((subs, 128), F32)
    copy.wait()
    alive = lengths_ref[core] - chip * frames
    tiles = range(states // 128)
    for r in range(SUB):
        every = pl.ds(r, subs, stride=SUB)
        x = row_dot(alpha, th, tl) * jnp.concatenate([e_ref[k, every, :] for k in tiles], axis=1)
        total = jnp.sum(x, axis=1, keepdims=True)
        alpha = x / total
        for k in tiles:
            alpha_scr[k, every, :] = alpha[:, k * 128 : (k + 1) * 128]
        live = sub * SUB + r < alive
        gain = jnp.where(live, jnp.log(total) + top_ref[every, :], 0.0)
        gains = jnp.where(lane % SUB == r, gain, gains)
    end = pl.ds(jnp.clip(alive - 1, 0, frames - 1), 1)
    for which, ref in ((core, kept_ref), (1 - core, sent_ref)):
        at = pl.multiple_of(which * half, half)
        frame = at + lax.broadcasted_iota(jnp.int32, (half, 128), 0)
        for k in tiles:
            cut = slice(k * 128, (k + 1) * 128)
            final = jnp.where(alive > 0, alpha_scr[k, end, :], v[0:1, cut])
            ref[0:half, cut] = jnp.log(jnp.where(frame < alive, alpha_scr[k, pl.ds(at, half), :], final))
    picked = jnp.where(lane // SUB == sub % blocks, gains, 0.0)
    lines = [jnp.sum(picked[k * blocks : (k + 1) * blocks], axis=0, keepdims=True) for k in range(2)]
    gain_ref[...] = jnp.where(core == 0, lines[0], lines[1])
    line = jnp.where(core == 0, lines[1], lines[0])
    sent_ref[half : half + 8, :] = jnp.concatenate([jnp.broadcast_to(line, (8, 128))] * (states // 128), axis=1)


def frames_pass(lengths, vs, start, other, pre, e, top, th, tl):
    frames, states = top.shape[0], th.shape[0]
    half = frames // 2
    out = jax.ShapeDtypeStruct
    return pl.pallas_call(
        functools.partial(frames_kernel, frames, len(vs) + 1),
        out_shape=(out((half, states), F32), out((half + 8, states), F32), out((1, 128), F32)),
        in_specs=[hbm()] + [vmem()] * (len(vs) + 7),
        out_specs=[vmem()] * 3,
        scratch_shapes=[
            pltpu.VMEM((states // 128, frames, 128), F32),
            pltpu.SMEM(lengths.shape, jnp.int32),
            pltpu.SemaphoreType.DMA,
        ],
        compiler_params=pltpu.CompilerParams(vmem_limit_bytes=6 << 20),
        name="frames",
    )(pinned(lengths), *vs, start, other, pre, e, top, th, tl)


def join_kernel(kept_ref, gain_ref, got_ref, log_ref, out_gain_ref):
    half = kept_ref.shape[0]
    core = lax.axis_index("tm") % 2
    log_ref[core] = kept_ref[...]
    log_ref[1 - core] = got_ref[0:half, :]
    own = gain_ref[0:1, 0:half]
    got = got_ref[half : half + 1, 0:half]
    out_gain_ref[0:1, :] = jnp.where(core == 0, own, got)
    out_gain_ref[1:2, :] = jnp.where(core == 0, got, own)


def join(kept, gain, got):
    half, states = kept.shape
    out = jax.ShapeDtypeStruct
    return pl.pallas_call(
        join_kernel,
        out_shape=(out((2, half, states), F32), out((2, half), F32)),
        in_specs=[vmem()] * 3,
        out_specs=[vmem()] * 2,
        compiler_params=pltpu.CompilerParams(vmem_limit_bytes=4 << 20),
        name="join",
    )(kept, gain, got)


def shards(size, loglik, trans_weight, block_mask, init_weight, lengths, pdf_map):
    utts, total, local = loglik.shape
    chips = size // 2
    frames = total // chips
    planes = chips // 2
    x = jnp.transpose(loglik, (0, 2, 1)).reshape(utts, local, chips, frames)
    x = jnp.transpose(x, (2, 0, 1, 3)).reshape(size, local, frames)
    cols = lax.all_to_all(x, "tm", 0, 0, tiled=True).reshape(size * local, frames)
    chip, pre, e, top, th, tl = transfer(cols, trans_weight, block_mask, lengths, pdf_map)
    other = lax.ppermute(chip, "tm", [(i, i ^ 2) for i in range(size)])
    dh, dl, v, start = plane_product(chip, other, init_weight)
    vs = []
    for g in range(1, planes):
        got = lax.ppermute(v, "tm", [(4 * (g - 1) + i, 4 * g + i) for i in range(4)])
        vs.append(got)
        if g < planes - 1:
            v = hop(got, dh, dl)
    kept, sent, gain = frames_pass(lengths, vs, start, other, pre, e, top, th, tl)
    got = lax.ppermute(sent, "tm", [(i, i ^ 1) for i in range(size)])
    return join(kept, gain, got)


def solution(mesh):
    return jax.shard_map(
        functools.partial(shards, mesh.shape["tm"]),
        mesh=mesh,
        in_specs=(P("groups", None, "tm"), P(), P(), P(), P("groups"), P()),
        out_specs=(P("groups", "tm", None), P("groups", "tm")),
        check_vma=False,
    )
```

```python
import functools
import jax
import jax.numpy as jnp
from jax import lax
from jax.experimental import pallas as pl
from jax.experimental.pallas import tpu as pltpu
from jax.sharding import PartitionSpec as P

F32 = jnp.float32
BF16 = jnp.bfloat16
SUB = 8
LEAD = 4


def halves(x):
    high = x.astype(BF16)
    return high, (x - high.astype(F32)).astype(BF16)


def dot(a, b):
    return jnp.dot(a, b, preferred_element_type=F32)


def dot3(a_high, a_low, b_high, b_low):
    return dot(a_high, b_high) + dot(a_low, b_high) + dot(a_high, b_low)


def transfer_kernel(
    frames,
    lengths_hbm,
    mask_hbm,
    weight_hbm,
    map_hbm,
    cols_ref,
    chip_ref,
    pre_ref,
    e_ref,
    top_ref,
    th_ref,
    tl_ref,
    g_scr,
    e_scr,
    t_scr,
    ah,
    al,
    bh,
    bl,
    lengths_ref,
    mask_ref,
    weight_ref,
    map_ref,
    sems,
):
    copies = [
        pltpu.make_async_copy(src, dst, sems.at[i])
        for i, (src, dst) in enumerate(
            (
                (map_hbm, map_ref),
                (weight_hbm, weight_ref),
                (mask_hbm, mask_ref),
                (lengths_hbm, lengths_ref),
            )
        )
    ]
    for copy in copies:
        copy.start()
    states = weight_ref.shape[0]
    half = frames // 2
    rows = states // 2
    blocks = half // SUB
    core = lax.axis_index("tm") % 2
    first_frame = (lax.axis_index("tm") // 2) * frames
    cols = cols_ref[...].T
    copies[0].wait()
    pick = (lax.broadcasted_iota(jnp.int32, (cols.shape[1], states), 0) == map_ref[...]).astype(F32).astype(BF16)
    p1 = cols.astype(BF16)
    rest = cols - p1.astype(F32)
    p2, p3 = halves(rest)
    depth = 256
    pieces = cols.shape[1] // depth

    def gather(*accs):
        for k in range(pieces):
            cut = slice(k * depth, (k + 1) * depth)
            pltpu.matmul_push_rhs(pick[cut, :], 0, k % 2)
            pltpu.matmul_acc_lhs(accs[k % 2], p1[:, cut], 0)
            pltpu.matmul_acc_lhs(accs[k % 2], p2[:, cut], None)
            pltpu.matmul_acc_lhs(accs[k % 2], p3[:, cut], None)
        g_scr[...] = pltpu.matmul_pop(accs[0]) + pltpu.matmul_pop(accs[1])

    pl.run_scoped(gather, pltpu.ACC(0)((frames, states), F32), pltpu.ACC(1)((frames, states), F32))
    g = g_scr[...]
    top = jnp.max(g, axis=1, keepdims=True)
    e = jnp.exp(g - top)
    e_scr[...] = e
    for k in range(states // 128):
        e_ref[k] = e[:, k * 128 : (k + 1) * 128]
    top_ref[...] = jnp.broadcast_to(top, (frames, 128))

    for copy in copies[1:]:
        copy.wait()
    alive = lengths_ref[core] - first_frame

    nb = mask_ref.shape[0]
    width = states // nb
    lane = lax.broadcasted_iota(jnp.int32, (1, states), 1) // width
    for r in range(nb):
        row = jnp.zeros((1, states), F32)
        for c in range(nb):
            row = jnp.where(lane == c, mask_ref[r, c].astype(F32), row)
        part = weight_ref[r * width : (r + 1) * width, :] * row
        t_scr[r * width : (r + 1) * width, :] = part / jnp.sum(part, axis=1, keepdims=True)
    th, tl = halves(t_scr[...])
    th_ref[...] = th
    tl_ref[...] = tl

    eye = (
        lax.broadcasted_iota(jnp.int32, (states, states), 0) == lax.broadcasted_iota(jnp.int32, (states, states), 1)
    ).astype(F32)
    for mh, ml, off in ((ah, al, 0), (bh, bl, half)):
        h, l = halves(jnp.where(alive > off, t_scr[...] * e_scr[off : off + 1, :], eye))
        mh[0:states, :] = h
        ml[0:states, :] = l

    def body(a0, a1, b0, b1):
        accs = ((a0, a1), (b0, b1))
        mats = ((ah, al), (bh, bl))

        def issue_a(high_loaded):
            for m in range(2):
                sl = pl.ds(m * rows, rows)
                pltpu.matmul_acc_lhs(accs[0][m], ah[sl, :], high_loaded)
                pltpu.matmul_acc_lhs(accs[0][m], al[sl, :], None)
            for m in range(2):
                pltpu.matmul_push_rhs(tl_ref[...], 1, m)
            for m in range(2):
                pltpu.matmul_acc_lhs(accs[0][m], ah[pl.ds(m * rows, rows), :], 1)

        def issue_b():
            for m in range(2):
                pltpu.matmul_acc_lhs(accs[1][m], bh[pl.ds(m * rows, rows), :], None)
            for m in range(2):
                pltpu.matmul_push_rhs(th_ref[...], 0, m)
            for m in range(2):
                sl = pl.ds(m * rows, rows)
                pltpu.matmul_acc_lhs(accs[1][m], bh[sl, :], 0)
                pltpu.matmul_acc_lhs(accs[1][m], bl[sl, :], None)

        def post(k, s, peak):
            mh, ml = mats[k]
            frame = s + k * half
            er = e_scr[pl.ds(frame, 1), :] * (1.0 / jnp.max(peak.astype(F32), keepdims=True)[:, :1])
            base = jnp.where(frame < alive, 0, states)
            new = None
            for m in range(2):
                x = pltpu.matmul_pop(accs[k][m]) * er
                h, l = halves(x)
                at = pl.multiple_of(base + m * rows, rows)
                mh[pl.ds(at, rows), :] = h
                ml[pl.ds(at, rows), :] = l
                y = jnp.max(h.reshape(rows // 16, 16, states), axis=0)
                new = y if new is None else jnp.maximum(new, y)
            return new

        def keep(j):
            for k in range(2):
                for i in range(2):
                    pre_ref[k, j, i] = mats[k][i][0:states, :]

        for m in range(2):
            pltpu.matmul_push_rhs(th_ref[...], 0, m)
        issue_a(0)
        one = jnp.ones((16, states), BF16)

        def step(s, peaks, last=False):
            pa, pb = peaks
            issue_b()
            pa = post(0, s, pa)
            if not last:
                issue_a(None)
            pb = post(1, s, pb)
            return pa, pb

        def block(j, peaks):
            for r in range(1, SUB):
                peaks = step(j * SUB + r, peaks)
            keep(j)
            return step(j * SUB + SUB, peaks)

        peaks = lax.fori_loop(0, blocks - 1, block, (one, one))
        for r in range(1, SUB):
            peaks = step((blocks - 1) * SUB + r, peaks, r == SUB - 1)
        keep(blocks - 1)
        for m in range(2):
            sl = pl.ds(m * rows, rows)
            pltpu.matmul_push_rhs(bh[0:states, :], 0, m)
            pltpu.matmul_acc_lhs(accs[0][m], ah[sl, :], 0)
            pltpu.matmul_acc_lhs(accs[0][m], al[sl, :], None)
            pltpu.matmul_push_rhs(bl[0:states, :], 1, m)
            pltpu.matmul_acc_lhs(accs[0][m], ah[sl, :], 1)
        c = jnp.concatenate([pltpu.matmul_pop(accs[0][m]) for m in range(2)], axis=0)
        chip_ref[...] = c * (1.0 / jnp.max(c, keepdims=True)[:, :1])

    shape = (rows, states)
    pl.run_scoped(
        body,
        pltpu.ACC(0)(shape, F32),
        pltpu.ACC(1)(shape, F32),
        pltpu.ACC(0)(shape, F32),
        pltpu.ACC(1)(shape, F32),
    )


def vmem():
    return pl.BlockSpec(memory_space=pltpu.VMEM)


def hbm():
    return pl.BlockSpec(memory_space=pltpu.MemorySpace.HBM)


def pinned(x):
    return pltpu.with_memory_space_constraint(x, pltpu.MemorySpace.HBM)


def transfer(cols, weight, mask, lengths, pdf_map):
    columns, frames = cols.shape
    states = weight.shape[0]
    blocks = frames // 2 // SUB
    out = jax.ShapeDtypeStruct
    return pl.pallas_call(
        functools.partial(transfer_kernel, frames),
        out_shape=(
            out((states, states), F32),
            out((2, blocks, 2, states, states), BF16),
            out((states // 128, frames, 128), F32),
            out((frames, 128), F32),
            out((states, states), BF16),
            out((states, states), BF16),
        ),
        in_specs=[hbm()] * 4 + [vmem()],
        out_specs=[vmem()] * 6,
        scratch_shapes=[pltpu.VMEM((frames, states), F32)] * 2
        + [pltpu.VMEM((states, states), F32)]
        + [pltpu.VMEM((2 * states, states), BF16)] * 4
        + [
            pltpu.SMEM(lengths.shape, jnp.int32),
            pltpu.SMEM(mask.shape, jnp.int32),
            pltpu.VMEM(weight.shape, F32),
            pltpu.VMEM((1, states), jnp.int32),
            pltpu.SemaphoreType.DMA((4,)),
        ],
        compiler_params=pltpu.CompilerParams(vmem_limit_bytes=6 << 20),
        name="transfer",
    )(*map(pinned, (lengths, mask, weight, pdf_map[None, :])), cols)


def row_dot(v, matrix_high, matrix_low):
    n = v.shape[0]
    vh, vl = halves(v)
    both = jnp.concatenate([vh, vl], axis=0)
    x = dot(both, matrix_high)
    return x[0:n] + x[n:] + dot(vh, matrix_low)


def unit(v):
    return v / jnp.sum(v, axis=1, keepdims=True)


def first_kernel(init_hbm, own_ref, v_ref, start_ref, init_ref, sem):
    copy = pltpu.make_async_copy(init_hbm, init_ref, sem)
    copy.start()
    high, low = halves(own_ref[...])
    copy.wait()
    start = jnp.broadcast_to(unit(init_ref[...]), v_ref.shape)
    start_ref[...] = start
    v_ref[...] = unit(row_dot(start, high, low))


def first(init, own):
    states = own.shape[0]
    return pl.pallas_call(
        first_kernel,
        out_shape=(jax.ShapeDtypeStruct((8, states), F32),) * 2,
        in_specs=[hbm(), vmem()],
        out_specs=[vmem()] * 2,
        scratch_shapes=[pltpu.VMEM((1, states), F32), pltpu.SemaphoreType.DMA],
        compiler_params=pltpu.CompilerParams(vmem_limit_bytes=4 << 20),
        name="first",
    )(pinned(init[None, :]), own)


def plane_kernel(own_ref, other_ref, d_ref):
    chip = lax.axis_index("tm") // 2

    def product(left, right):
        d = dot3(*halves(left[...]), *halves(right[...]))
        d_ref[...] = d * (1.0 / jnp.max(d, keepdims=True)[:, :1])

    @pl.when(jnp.logical_and(chip >= LEAD, chip % 2 == 0))
    def _():
        product(own_ref, other_ref)

    @pl.when(jnp.logical_and(chip >= LEAD, chip % 2 == 1))
    def _():
        product(other_ref, own_ref)

    @pl.when(chip < LEAD)
    def _():
        d_ref[...] = own_ref[...]


def plane_product(own, other):
    return pl.pallas_call(
        plane_kernel,
        out_shape=jax.ShapeDtypeStruct(own.shape, F32),
        in_specs=[vmem()] * 2,
        out_specs=vmem(),
        compiler_params=pltpu.CompilerParams(vmem_limit_bytes=4 << 20),
        name="plane",
    )(own, other)


def hop_kernel(m_ref, *refs):
    *v_refs, out_ref = refs
    v = v_refs[0][...]
    for ref in v_refs[1:]:
        v = v + ref[...]
    out_ref[...] = unit(row_dot(v, *halves(m_ref[...])))


def hop(m, *vs):
    return pl.pallas_call(
        hop_kernel,
        out_shape=jax.ShapeDtypeStruct(vs[0].shape, F32),
        in_specs=[vmem()] * (len(vs) + 1),
        out_specs=vmem(),
        compiler_params=pltpu.CompilerParams(vmem_limit_bytes=4 << 20),
        name="hop",
    )(m, *vs)


def frames_kernel(
    frames,
    chips_of,
    lengths_hbm,
    *refs,
):
    v_refs = refs[: len(chips_of)]
    start_ref, other_ref, pre_ref, e_ref, top_ref, th_ref, tl_ref, kept_ref, sent_ref, gain_ref, *scratch = refs[
        len(chips_of) :
    ]
    alpha_scr, lengths_ref, sem = scratch
    copy = pltpu.make_async_copy(lengths_hbm, lengths_ref, sem)
    copy.start()
    states = th_ref.shape[0]
    half = frames // 2
    blocks = half // SUB
    subs = 2 * blocks
    index = lax.axis_index("tm")
    core = index % 2
    chip = index // 2
    v = start_ref[...]
    for low, high, ref in ((*pair, ref) for pair, ref in zip(chips_of, v_refs)):
        v = jnp.where(jnp.logical_and(chip >= low, chip < high), ref[...], v)
    oh, ol = halves(other_ref[...])
    v = jnp.where(jnp.logical_and(chip >= LEAD, chip % 2 == 1), unit(row_dot(v, oh, ol)), v)
    mid = unit(row_dot(v, pre_ref[0, blocks - 1, 0], pre_ref[0, blocks - 1, 1]))
    rows = [v[0:1]]
    for j in range(blocks - 1):
        rows.append(row_dot(v, pre_ref[0, j, 0], pre_ref[0, j, 1])[0:1])
    rows.append(mid[0:1])
    for j in range(blocks - 1):
        rows.append(row_dot(mid, pre_ref[1, j, 0], pre_ref[1, j, 1])[0:1])
    alpha = unit(jnp.concatenate(rows, axis=0))
    th, tl = th_ref[...], tl_ref[...]
    lane = lax.broadcasted_iota(jnp.int32, (subs, 128), 1)
    sub = lax.broadcasted_iota(jnp.int32, (subs, 128), 0)
    gains = jnp.zeros((subs, 128), F32)
    copy.wait()
    alive = lengths_ref[core] - chip * frames
    tiles = range(states // 128)
    for r in range(SUB):
        every = pl.ds(r, subs, stride=SUB)
        x = row_dot(alpha, th, tl) * jnp.concatenate([e_ref[k, every, :] for k in tiles], axis=1)
        total = jnp.sum(x, axis=1, keepdims=True)
        alpha = x / total
        for k in tiles:
            alpha_scr[k, every, :] = alpha[:, k * 128 : (k + 1) * 128]
        live = sub * SUB + r < alive
        gain = jnp.where(live, jnp.log(total) + top_ref[every, :], 0.0)
        gains = jnp.where(lane % SUB == r, gain, gains)
    end = pl.ds(jnp.clip(alive - 1, 0, frames - 1), 1)
    for which, ref in ((core, kept_ref), (1 - core, sent_ref)):
        at = pl.multiple_of(which * half, half)
        frame = at + lax.broadcasted_iota(jnp.int32, (half, 128), 0)
        for k in tiles:
            cut = slice(k * 128, (k + 1) * 128)
            final = jnp.where(alive > 0, alpha_scr[k, end, :], v[0:1, cut])
            ref[0:half, cut] = jnp.log(jnp.where(frame < alive, alpha_scr[k, pl.ds(at, half), :], final))
    picked = jnp.where(lane // SUB == sub % blocks, gains, 0.0)
    lines = [jnp.sum(picked[k * blocks : (k + 1) * blocks], axis=0, keepdims=True) for k in range(2)]
    gain_ref[...] = jnp.where(core == 0, lines[0], lines[1])
    line = jnp.where(core == 0, lines[1], lines[0])
    sent_ref[half : half + 8, :] = jnp.concatenate([jnp.broadcast_to(line, (8, 128))] * (states // 128), axis=1)


def frames_pass(lengths, chips_of, vs, start, other, pre, e, top, th, tl):
    frames, states = top.shape[0], th.shape[0]
    half = frames // 2
    out = jax.ShapeDtypeStruct
    return pl.pallas_call(
        functools.partial(frames_kernel, frames, chips_of),
        out_shape=(out((half, states), F32), out((half + 8, states), F32), out((1, 128), F32)),
        in_specs=[hbm()] + [vmem()] * (len(vs) + 7),
        out_specs=[vmem()] * 3,
        scratch_shapes=[
            pltpu.VMEM((states // 128, frames, 128), F32),
            pltpu.SMEM(lengths.shape, jnp.int32),
            pltpu.SemaphoreType.DMA,
        ],
        compiler_params=pltpu.CompilerParams(vmem_limit_bytes=6 << 20),
        name="frames",
    )(pinned(lengths), *vs, start, other, pre, e, top, th, tl)


def join_kernel(kept_ref, gain_ref, got_ref, log_ref, out_gain_ref):
    half = kept_ref.shape[0]
    core = lax.axis_index("tm") % 2
    log_ref[core] = kept_ref[...]
    log_ref[1 - core] = got_ref[0:half, :]
    own = gain_ref[0:1, 0:half]
    got = got_ref[half : half + 1, 0:half]
    out_gain_ref[0:1, :] = jnp.where(core == 0, own, got)
    out_gain_ref[1:2, :] = jnp.where(core == 0, got, own)


def join(kept, gain, got):
    half, states = kept.shape
    out = jax.ShapeDtypeStruct
    return pl.pallas_call(
        join_kernel,
        out_shape=(out((2, half, states), F32), out((2, half), F32)),
        in_specs=[vmem()] * 3,
        out_specs=[vmem()] * 2,
        compiler_params=pltpu.CompilerParams(vmem_limit_bytes=4 << 20),
        name="join",
    )(kept, gain, got)


def shards(size, loglik, trans_weight, block_mask, init_weight, lengths, pdf_map):
    utts, total, local = loglik.shape
    chips = size // 2
    frames = total // chips
    x = jnp.transpose(loglik, (0, 2, 1)).reshape(utts, local, chips, frames)
    x = jnp.transpose(x, (2, 0, 1, 3)).reshape(size, local, frames)
    cols = lax.all_to_all(x, "tm", 0, 0, tiled=True).reshape(size * local, frames)
    chip, pre, e, top, th, tl = transfer(cols, trans_weight, block_mask, lengths, pdf_map)
    other = lax.ppermute(chip, "tm", [(i, i ^ 2) for i in range(2 * LEAD, size)])
    v, start = first(init_weight, chip)
    chips_of, vs = [], []

    def send(v, source, target, count=1):
        got = lax.ppermute(v, "tm", [(2 * source + i, 2 * target + i) for i in range(2 * count)])
        chips_of.append((target, target + count))
        vs.append(got)
        return got

    for c in range(1, LEAD):
        v = hop(chip, send(v, c - 1, c))
    plane = plane_product(chip, other)
    last = [send(v, LEAD - 1, LEAD), send(v, LEAD - 1, LEAD + 1)]
    for c in range(LEAD + 2, chips, 2):
        v = hop(plane, *last)
        last = [send(v, c - 2, c, 2)]
    kept, sent, gain = frames_pass(lengths, chips_of, vs, start, other, pre, e, top, th, tl)
    got = lax.ppermute(sent, "tm", [(i, i ^ 1) for i in range(size)])
    return join(kept, gain, got)


def solution(mesh):
    return jax.shard_map(
        functools.partial(shards, mesh.shape["tm"]),
        mesh=mesh,
        in_specs=(P("groups", None, "tm"), P(), P(), P(), P("groups"), P()),
        out_specs=(P("groups", "tm", None), P("groups", "tm")),
        check_vma=False,
    )
```

```python
import functools
import jax
import jax.numpy as jnp
from jax import lax
from jax.experimental import pallas as pl
from jax.experimental.pallas import tpu as pltpu
from jax.sharding import PartitionSpec as P

F32 = jnp.float32
BF16 = jnp.bfloat16
SUB = 8


def place(half):
    index = lax.axis_index("tm")
    first = (index // 4) * 4 * half + (index % 2) * half
    return (index // 2) % 2, (first, first + 2 * half)


def halves(x):
    high = x.astype(BF16)
    return high, (x - high.astype(F32)).astype(BF16)


def dot(a, b):
    return jnp.dot(a, b, preferred_element_type=F32)


def dot3(a_high, a_low, b_high, b_low):
    return dot(a_high, b_high) + dot(a_low, b_high) + dot(a_high, b_low)


def transfer_kernel(
    frames,
    lengths_hbm,
    mask_hbm,
    weight_hbm,
    map_hbm,
    init_hbm,
    cols_ref,
    mats_ref,
    pre_ref,
    e_ref,
    top_ref,
    th_ref,
    tl_ref,
    start_ref,
    g_scr,
    e_scr,
    t_scr,
    ah,
    al,
    bh,
    bl,
    lengths_ref,
    mask_ref,
    weight_ref,
    map_ref,
    init_ref,
    sems,
):
    copies = [
        pltpu.make_async_copy(src, dst, sems.at[i])
        for i, (src, dst) in enumerate(
            (
                (map_hbm, map_ref),
                (weight_hbm, weight_ref),
                (mask_hbm, mask_ref),
                (lengths_hbm, lengths_ref),
                (init_hbm, init_ref),
            )
        )
    ]
    for copy in copies:
        copy.start()
    states = weight_ref.shape[0]
    half = frames // 2
    rows = states // 2
    blocks = half // SUB
    utt, slots = place(half)
    cols = cols_ref[...].T
    copies[0].wait()
    pick = (lax.broadcasted_iota(jnp.int32, (cols.shape[1], states), 0) == map_ref[...]).astype(F32).astype(BF16)
    p1 = cols.astype(BF16)
    rest = cols - p1.astype(F32)
    p2, p3 = halves(rest)
    depth = 256
    pieces = cols.shape[1] // depth

    def gather(*accs):
        for k in range(pieces):
            cut = slice(k * depth, (k + 1) * depth)
            pltpu.matmul_push_rhs(pick[cut, :], 0, k % 2)
            pltpu.matmul_acc_lhs(accs[k % 2], p1[:, cut], 0)
            pltpu.matmul_acc_lhs(accs[k % 2], p2[:, cut], None)
            pltpu.matmul_acc_lhs(accs[k % 2], p3[:, cut], None)
        g_scr[...] = pltpu.matmul_pop(accs[0]) + pltpu.matmul_pop(accs[1])

    pl.run_scoped(gather, pltpu.ACC(0)((frames, states), F32), pltpu.ACC(1)((frames, states), F32))
    g = g_scr[...]
    top = jnp.max(g, axis=1, keepdims=True)
    e = jnp.exp(g - top)
    e_scr[...] = e
    for k in range(states // 128):
        e_ref[k] = e[:, k * 128 : (k + 1) * 128]
    top_ref[...] = jnp.broadcast_to(top, (frames, 128))

    for copy in copies[1:]:
        copy.wait()
    alive = [lengths_ref[utt] - slot for slot in slots]
    start_ref[...] = jnp.broadcast_to(unit(init_ref[...]), start_ref.shape)

    nb = mask_ref.shape[0]
    width = states // nb
    lane = lax.broadcasted_iota(jnp.int32, (1, states), 1) // width
    for r in range(nb):
        row = jnp.zeros((1, states), F32)
        for c in range(nb):
            row = jnp.where(lane == c, mask_ref[r, c].astype(F32), row)
        part = weight_ref[r * width : (r + 1) * width, :] * row
        t_scr[r * width : (r + 1) * width, :] = part / jnp.sum(part, axis=1, keepdims=True)
    th, tl = halves(t_scr[...])
    th_ref[...] = th
    tl_ref[...] = tl

    eye = (
        lax.broadcasted_iota(jnp.int32, (states, states), 0) == lax.broadcasted_iota(jnp.int32, (states, states), 1)
    ).astype(F32)
    for k, (mh, ml) in enumerate(((ah, al), (bh, bl))):
        off = k * half
        h, l = halves(jnp.where(alive[k] > 0, t_scr[...] * e_scr[off : off + 1, :], eye))
        mh[0:states, :] = h
        ml[0:states, :] = l

    def body(a0, a1, b0, b1):
        accs = ((a0, a1), (b0, b1))
        mats = ((ah, al), (bh, bl))

        def issue_a(high_loaded):
            for m in range(2):
                sl = pl.ds(m * rows, rows)
                pltpu.matmul_acc_lhs(accs[0][m], ah[sl, :], high_loaded)
                pltpu.matmul_acc_lhs(accs[0][m], al[sl, :], None)
            for m in range(2):
                pltpu.matmul_push_rhs(tl_ref[...], 1, m)
            for m in range(2):
                pltpu.matmul_acc_lhs(accs[0][m], ah[pl.ds(m * rows, rows), :], 1)

        def issue_b():
            for m in range(2):
                pltpu.matmul_acc_lhs(accs[1][m], bh[pl.ds(m * rows, rows), :], None)
            for m in range(2):
                pltpu.matmul_push_rhs(th_ref[...], 0, m)
            for m in range(2):
                sl = pl.ds(m * rows, rows)
                pltpu.matmul_acc_lhs(accs[1][m], bh[sl, :], 0)
                pltpu.matmul_acc_lhs(accs[1][m], bl[sl, :], None)

        def post(k, s, peak):
            mh, ml = mats[k]
            er = e_scr[pl.ds(s + k * half, 1), :] * (1.0 / jnp.max(peak.astype(F32), keepdims=True)[:, :1])
            base = jnp.where(s < alive[k], 0, states)
            new = None
            for m in range(2):
                x = pltpu.matmul_pop(accs[k][m]) * er
                h, l = halves(x)
                at = pl.multiple_of(base + m * rows, rows)
                mh[pl.ds(at, rows), :] = h
                ml[pl.ds(at, rows), :] = l
                y = jnp.max(h.reshape(rows // 16, 16, states), axis=0)
                new = y if new is None else jnp.maximum(new, y)
            return new

        def keep(j):
            for k in range(2):
                for i in range(2):
                    pre_ref[k, j, i] = mats[k][i][0:states, :]

        for m in range(2):
            pltpu.matmul_push_rhs(th_ref[...], 0, m)
        issue_a(0)
        one = jnp.ones((16, states), BF16)

        def step(s, peaks, last=False):
            pa, pb = peaks
            issue_b()
            pa = post(0, s, pa)
            if not last:
                issue_a(None)
            pb = post(1, s, pb)
            return pa, pb

        def block(j, peaks):
            for r in range(1, SUB):
                peaks = step(j * SUB + r, peaks)
            keep(j)
            return step(j * SUB + SUB, peaks)

        peaks = lax.fori_loop(0, blocks - 1, block, (one, one))
        for r in range(1, SUB):
            peaks = step((blocks - 1) * SUB + r, peaks, r == SUB - 1)
        keep(blocks - 1)
        for i, (mh, ml) in enumerate(mats):
            mats_ref[i] = mh[0:states, :].astype(F32) + ml[0:states, :].astype(F32)

    shape = (rows, states)
    pl.run_scoped(
        body,
        pltpu.ACC(0)(shape, F32),
        pltpu.ACC(1)(shape, F32),
        pltpu.ACC(0)(shape, F32),
        pltpu.ACC(1)(shape, F32),
    )


def vmem():
    return pl.BlockSpec(memory_space=pltpu.VMEM)


def hbm():
    return pl.BlockSpec(memory_space=pltpu.MemorySpace.HBM)


def pinned(x):
    return pltpu.with_memory_space_constraint(x, pltpu.MemorySpace.HBM)


def transfer(cols, weight, mask, lengths, pdf_map, init):
    columns, frames = cols.shape
    states = weight.shape[0]
    blocks = frames // 2 // SUB
    out = jax.ShapeDtypeStruct
    return pl.pallas_call(
        functools.partial(transfer_kernel, frames),
        out_shape=(
            out((2, states, states), F32),
            out((2, blocks, 2, states, states), BF16),
            out((states // 128, frames, 128), F32),
            out((frames, 128), F32),
            out((states, states), BF16),
            out((states, states), BF16),
            out((8, states), F32),
        ),
        in_specs=[hbm()] * 5 + [vmem()],
        out_specs=[vmem()] * 7,
        scratch_shapes=[pltpu.VMEM((frames, states), F32)] * 2
        + [pltpu.VMEM((states, states), F32)]
        + [pltpu.VMEM((2 * states, states), BF16)] * 4
        + [
            pltpu.SMEM(lengths.shape, jnp.int32),
            pltpu.SMEM(mask.shape, jnp.int32),
            pltpu.VMEM(weight.shape, F32),
            pltpu.VMEM((1, states), jnp.int32),
            pltpu.VMEM((1, states), F32),
            pltpu.SemaphoreType.DMA((5,)),
        ],
        compiler_params=pltpu.CompilerParams(vmem_limit_bytes=6 << 20),
        name="transfer",
    )(*map(pinned, (lengths, mask, weight, pdf_map[None, :], init[None, :])), cols)


def row_dot(v, matrix_high, matrix_low):
    n = v.shape[0]
    vh, vl = halves(v)
    both = jnp.concatenate([vh, vl], axis=0)
    x = dot(both, matrix_high)
    return x[0:n] + x[n:] + dot(vh, matrix_low)


def unit(v):
    return v / jnp.sum(v, axis=1, keepdims=True)


def pass_on(v, matrix):
    return row_dot(v, *halves(matrix)) * (1.0 / jnp.sum(v, axis=1, keepdims=True))


def in_order(own_ref, other_ref, do):
    core = lax.axis_index("tm") % 2

    @pl.when(core == 0)
    def _():
        do(own_ref.at[0], other_ref.at[0], own_ref.at[1], other_ref.at[1])

    @pl.when(core == 1)
    def _():
        do(other_ref.at[0], own_ref.at[0], other_ref.at[1], own_ref.at[1])


def first_kernel(start_ref, own_ref, other_ref, v_ref):
    def do(*mats):
        v = start_ref[...]
        for m in mats:
            v = pass_on(v, m[...])
        v_ref[...] = v

    in_order(own_ref, other_ref, do)


def group_kernel(own_ref, other_ref, all_ref, mid_ref):
    def times(left, right):
        d = dot3(*halves(left), *halves(right))
        return d * (1.0 / jnp.max(d, keepdims=True)[:, :1])

    def do(*mats):
        mid_ref[...] = times(mats[0][...], mats[1][...])
        all_ref[...] = times(mid_ref[...], times(mats[2][...], mats[3][...]))

    in_order(own_ref, other_ref, do)

    @pl.when(lax.axis_index("tm") % 2 == 1)
    def _():
        mid_ref[...] = times(mid_ref[...], other_ref[1])


def hop_kernel(v_ref, m_ref, out_ref):
    out_ref[...] = pass_on(v_ref[...], m_ref[...])


def small(kernel, name, outs, *args):
    return pl.pallas_call(
        kernel,
        out_shape=tuple(jax.ShapeDtypeStruct(shape, F32) for shape in outs),
        in_specs=[vmem()] * len(args),
        out_specs=[vmem()] * len(outs),
        compiler_params=pltpu.CompilerParams(vmem_limit_bytes=4 << 20),
        name=name,
    )(*args)


def pack_kernel(x_hbm, out_ref, x_ref, sem):
    copy = pltpu.make_async_copy(x_hbm, x_ref, sem)
    copy.start()
    copy.wait()
    groups = out_ref.shape[0]
    local = out_ref.shape[2]
    low = lax.broadcasted_iota(jnp.int32, (local, 128), 1) < 64
    for g in range(groups):
        for u in range(2):
            early = x_ref[u, :, g * 256 : g * 256 + 128]
            late = x_ref[u, :, g * 256 + 128 : g * 256 + 256]
            out_ref[g, 2 * u] = jnp.where(low, early, pltpu.roll(late, 64, 1))
            out_ref[g, 2 * u + 1] = jnp.where(low, pltpu.roll(early, 64, 1), late)


def pack(x, groups):
    local = x.shape[1]
    return pl.pallas_call(
        pack_kernel,
        out_shape=jax.ShapeDtypeStruct((groups, 4, local, 128), F32),
        in_specs=[hbm()],
        out_specs=vmem(),
        scratch_shapes=[pltpu.VMEM(x.shape, F32), pltpu.SemaphoreType.DMA],
        compiler_params=pltpu.CompilerParams(vmem_limit_bytes=4 << 20),
        name="pack",
    )(pinned(x))


def frames_kernel(frames, lengths_hbm, *refs):
    start_ref, *v_refs = refs[:-13]
    other_ref, mid_ref, pre_ref, e_ref, top_ref, th_ref, tl_ref, kept_ref, sent_ref, gain_ref, *scratch = refs[
        len(v_refs) + 1 :
    ]
    alpha_scr, lengths_ref, sem = scratch
    copy = pltpu.make_async_copy(lengths_hbm, lengths_ref, sem)
    copy.start()
    states = th_ref.shape[0]
    half = frames // 2
    blocks = half // SUB
    subs = 2 * blocks
    index = lax.axis_index("tm")
    utt, slots = place(half)
    v = start_ref[...]
    for g, ref in enumerate(v_refs):
        v = jnp.where(index // 4 == g + 1, ref[...], v)
    mid = unit(pass_on(v, mid_ref[...]))
    v = unit(jnp.where(index % 2 == 1, pass_on(v, other_ref[0]), v))
    rows = [v[0:1]]
    for j in range(blocks - 1):
        rows.append(row_dot(v, pre_ref[0, j, 0], pre_ref[0, j, 1])[0:1])
    rows.append(mid[0:1])
    for j in range(blocks - 1):
        rows.append(row_dot(mid, pre_ref[1, j, 0], pre_ref[1, j, 1])[0:1])
    alpha = unit(jnp.concatenate(rows, axis=0))
    th, tl = th_ref[...], tl_ref[...]
    lane = lax.broadcasted_iota(jnp.int32, (subs, 128), 1)
    sub = lax.broadcasted_iota(jnp.int32, (subs, 128), 0)
    gains = jnp.zeros((subs, 128), F32)
    copy.wait()
    alive = [lengths_ref[utt] - slot for slot in slots]
    tiles = range(states // 128)
    for r in range(SUB):
        every = pl.ds(r, subs, stride=SUB)
        x = row_dot(alpha, th, tl) * jnp.concatenate([e_ref[k, every, :] for k in tiles], axis=1)
        total = jnp.sum(x, axis=1, keepdims=True)
        alpha = x / total
        for k in tiles:
            alpha_scr[k, every, :] = alpha[:, k * 128 : (k + 1) * 128]
        live = (sub % blocks) * SUB + r < jnp.where(sub < blocks, alive[0], alive[1])
        gain = jnp.where(live, jnp.log(total) + top_ref[every, :], 0.0)
        gains = jnp.where(lane % SUB == r, gain, gains)
    for which, ref in ((utt, kept_ref), (1 - utt, sent_ref)):
        at = pl.multiple_of(which * half, half)
        left = jnp.where(which == 0, alive[0], alive[1])
        frame = lax.broadcasted_iota(jnp.int32, (half, 128), 0)
        end = pl.ds(at + jnp.clip(left - 1, 0, half - 1), 1)
        before = jnp.where(which == 0, v[0:1], mid[0:1])
        for k in tiles:
            cut = slice(k * 128, (k + 1) * 128)
            final = jnp.where(left > 0, alpha_scr[k, end, :], before[:, cut])
            ref[0:half, cut] = jnp.log(jnp.where(frame < left, alpha_scr[k, pl.ds(at, half), :], final))
    picked = jnp.where(lane // SUB == sub % blocks, gains, 0.0)
    lines = [jnp.sum(picked[k * blocks : (k + 1) * blocks], axis=0, keepdims=True) for k in range(2)]
    gain_ref[...] = jnp.where(utt == 0, lines[0], lines[1])
    line = jnp.where(utt == 0, lines[1], lines[0])
    sent_ref[half : half + 8, :] = jnp.concatenate([jnp.broadcast_to(line, (8, 128))] * (states // 128), axis=1)


def frames_pass(lengths, vs, other, mid, pre, e, top, th, tl):
    frames, states = top.shape[0], th.shape[0]
    half = frames // 2
    out = jax.ShapeDtypeStruct
    return pl.pallas_call(
        functools.partial(frames_kernel, frames),
        out_shape=(out((half, states), F32), out((half + 8, states), F32), out((1, 128), F32)),
        in_specs=[hbm()] + [vmem()] * (len(vs) + 7),
        out_specs=[vmem()] * 3,
        scratch_shapes=[
            pltpu.VMEM((states // 128, frames, 128), F32),
            pltpu.SMEM(lengths.shape, jnp.int32),
            pltpu.SemaphoreType.DMA,
        ],
        compiler_params=pltpu.CompilerParams(vmem_limit_bytes=6 << 20),
        name="frames",
    )(pinned(lengths), *vs, other, mid, pre, e, top, th, tl)


def join_kernel(kept_ref, gain_ref, got_ref, log_ref, out_gain_ref):
    half = kept_ref.shape[0]
    utt = (lax.axis_index("tm") // 2) % 2
    log_ref[utt] = kept_ref[...]
    log_ref[1 - utt] = got_ref[0:half, :]
    own = gain_ref[0:1, 0:half]
    got = got_ref[half : half + 1, 0:half]
    out_gain_ref[0:1, :] = jnp.where(utt == 0, own, got)
    out_gain_ref[1:2, :] = jnp.where(utt == 0, got, own)


def join(kept, gain, got):
    half, states = kept.shape
    out = jax.ShapeDtypeStruct
    return pl.pallas_call(
        join_kernel,
        out_shape=(out((2, half, states), F32), out((2, half), F32)),
        in_specs=[vmem()] * 3,
        out_specs=[vmem()] * 2,
        compiler_params=pltpu.CompilerParams(vmem_limit_bytes=4 << 20),
        name="join",
    )(kept, gain, got)


def shards(size, loglik, trans_weight, block_mask, init_weight, lengths, pdf_map):
    local = loglik.shape[2]
    groups = size // 4
    x = pack(jnp.transpose(loglik, (0, 2, 1)), groups)
    frames = x.shape[3]
    x = x.reshape(size, local, frames)
    cols = lax.all_to_all(x, "tm", 0, 0, tiled=True).reshape(size * local, frames)
    own, pre, e, top, th, tl, start = transfer(cols, trans_weight, block_mask, lengths, pdf_map, init_weight)
    other = lax.ppermute(own, "tm", [(i, i ^ 1) for i in range(size)])
    (v,) = small(first_kernel, "first", [start.shape], start, own, other)
    square = own.shape[1:]
    whole, mid = small(group_kernel, "group", [square, square], own, other)
    vs = [start]
    for g in range(1, groups):
        pairs = [(i, 4 * pair_of(i // 4, g, groups) + i % 4) for i in range(size)]
        vs.append(lax.ppermute(v, "tm", pairs))
        if g < groups - 1:
            (v,) = small(hop_kernel, "hop", [v.shape], vs[-1], whole)
    kept, sent, gain = frames_pass(lengths, vs, other, mid, pre, e, top, th, tl)
    got = lax.ppermute(sent, "tm", [(i, i ^ 2) for i in range(size)])
    return join(kept, gain, got)


def pair_of(group, turn, groups):
    if turn % 2:
        return group ^ 1
    return (group - 1 if group % 2 == 0 else group + 1) % groups


def solution(mesh):
    return jax.shard_map(
        functools.partial(shards, mesh.shape["tm"]),
        mesh=mesh,
        in_specs=(P("groups", None, "tm"), P(), P(), P(), P("groups"), P()),
        out_specs=(P("groups", "tm", None), P("groups", "tm")),
        check_vma=False,
    )
```

```python
import functools
import jax
import jax.numpy as jnp
from jax import lax
from jax.experimental import pallas as pl
from jax.experimental.pallas import tpu as pltpu
from jax.sharding import PartitionSpec as P

F32 = jnp.float32
BF16 = jnp.bfloat16
SUB = 8


def place(half):
    index = lax.axis_index("tm")
    first = (index // 4) * 4 * half + (index % 2) * half
    return (index // 2) % 2, (first, first + 2 * half)


def halves(x):
    high = x.astype(BF16)
    return high, (x - high.astype(F32)).astype(BF16)


def dot(a, b):
    return jnp.dot(a, b, preferred_element_type=F32)


def dot3(a_high, a_low, b_high, b_low):
    return dot(a_high, b_high) + dot(a_low, b_high) + dot(a_high, b_low)


def transfer_kernel(
    frames,
    lengths_hbm,
    mask_hbm,
    weight_hbm,
    map_hbm,
    init_hbm,
    cols_ref,
    mats_ref,
    pre_ref,
    e_ref,
    top_ref,
    th_ref,
    tl_ref,
    start_ref,
    g_scr,
    e_scr,
    t_scr,
    ah,
    al,
    bh,
    bl,
    lengths_ref,
    mask_ref,
    weight_ref,
    map_ref,
    init_ref,
    sems,
):
    copies = [
        pltpu.make_async_copy(src, dst, sems.at[i])
        for i, (src, dst) in enumerate(
            (
                (map_hbm, map_ref),
                (weight_hbm, weight_ref),
                (mask_hbm, mask_ref),
                (lengths_hbm, lengths_ref),
                (init_hbm, init_ref),
            )
        )
    ]
    for copy in copies:
        copy.start()
    states = weight_ref.shape[0]
    half = frames // 2
    rows = states // 2
    blocks = half // SUB
    utt, slots = place(half)
    cols = cols_ref[...].T
    copies[0].wait()
    pick = (lax.broadcasted_iota(jnp.int32, (cols.shape[1], states), 0) == map_ref[...]).astype(F32).astype(BF16)
    p1 = cols.astype(BF16)
    rest = cols - p1.astype(F32)
    p2, p3 = halves(rest)
    depth = 256
    pieces = cols.shape[1] // depth

    def gather(*accs):
        for k in range(pieces):
            cut = slice(k * depth, (k + 1) * depth)
            pltpu.matmul_push_rhs(pick[cut, :], 0, k % 2)
            pltpu.matmul_acc_lhs(accs[k % 2], p1[:, cut], 0)
            pltpu.matmul_acc_lhs(accs[k % 2], p2[:, cut], None)
            pltpu.matmul_acc_lhs(accs[k % 2], p3[:, cut], None)
        g_scr[...] = pltpu.matmul_pop(accs[0]) + pltpu.matmul_pop(accs[1])

    pl.run_scoped(gather, pltpu.ACC(0)((frames, states), F32), pltpu.ACC(1)((frames, states), F32))
    g = g_scr[...]
    top = jnp.max(g, axis=1, keepdims=True)
    e = jnp.exp(g - top)
    e_scr[...] = e
    for k in range(states // 128):
        e_ref[k] = e[:, k * 128 : (k + 1) * 128]
    top_ref[...] = jnp.broadcast_to(top, (frames, 128))

    for copy in copies[1:]:
        copy.wait()
    alive = [lengths_ref[utt] - slot for slot in slots]
    start_ref[...] = jnp.broadcast_to(unit(init_ref[...]), start_ref.shape)

    nb = mask_ref.shape[0]
    width = states // nb
    lane = lax.broadcasted_iota(jnp.int32, (1, states), 1) // width
    for r in range(nb):
        row = jnp.zeros((1, states), F32)
        for c in range(nb):
            row = jnp.where(lane == c, mask_ref[r, c].astype(F32), row)
        part = weight_ref[r * width : (r + 1) * width, :] * row
        t_scr[r * width : (r + 1) * width, :] = part / jnp.sum(part, axis=1, keepdims=True)
    th, tl = halves(t_scr[...])
    th_ref[...] = th
    tl_ref[...] = tl

    eye = (
        lax.broadcasted_iota(jnp.int32, (states, states), 0) == lax.broadcasted_iota(jnp.int32, (states, states), 1)
    ).astype(F32)
    for k, (mh, ml) in enumerate(((ah, al), (bh, bl))):
        off = k * half
        h, l = halves(jnp.where(alive[k] > 0, t_scr[...] * e_scr[off : off + 1, :], eye))
        mh[0:states, :] = h
        ml[0:states, :] = l

    def body(a0, a1, b0, b1):
        accs = ((a0, a1), (b0, b1))
        mats = ((ah, al), (bh, bl))

        def issue_a(high_loaded):
            for m in range(2):
                sl = pl.ds(m * rows, rows)
                pltpu.matmul_acc_lhs(accs[0][m], ah[sl, :], high_loaded)
                pltpu.matmul_acc_lhs(accs[0][m], al[sl, :], None)
            for m in range(2):
                pltpu.matmul_push_rhs(tl_ref[...], 1, m)
            for m in range(2):
                pltpu.matmul_acc_lhs(accs[0][m], ah[pl.ds(m * rows, rows), :], 1)

        def issue_b():
            for m in range(2):
                pltpu.matmul_acc_lhs(accs[1][m], bh[pl.ds(m * rows, rows), :], None)
            for m in range(2):
                pltpu.matmul_push_rhs(th_ref[...], 0, m)
            for m in range(2):
                sl = pl.ds(m * rows, rows)
                pltpu.matmul_acc_lhs(accs[1][m], bh[sl, :], 0)
                pltpu.matmul_acc_lhs(accs[1][m], bl[sl, :], None)

        def post(k, s, peak, look):
            mh, ml = mats[k]
            er = e_scr[pl.ds(s + k * half, 1), :]
            if not look:
                er = er * (1.0 / jnp.max(peak.astype(F32), keepdims=True)[:, :1])
            live = s < alive[k]
            new = None
            for m in range(2):
                x = pltpu.matmul_pop(accs[k][m]) * er
                h, l = halves(x)
                sl = pl.ds(m * rows, rows)
                mh[sl, :] = jnp.where(live, h, mh[sl, :])
                ml[sl, :] = jnp.where(live, l, ml[sl, :])
                if look:
                    y = jnp.max(h.reshape(rows // 16, 16, states), axis=0)
                    new = y if new is None else jnp.maximum(new, y)
            return new if look else peak

        def keep(j):
            for k in range(2):
                for i in range(2):
                    pre_ref[k, j, i] = mats[k][i][0:states, :]

        for m in range(2):
            pltpu.matmul_push_rhs(th_ref[...], 0, m)
        issue_a(0)
        one = jnp.ones((16, states), BF16)

        def step(s, r, peaks, last=False):
            pa, pb = peaks
            odd = r % 2 == 1
            issue_b()
            pa = post(0, s, pa, odd)
            if not last:
                issue_a(None)
            pb = post(1, s, pb, not odd)
            return pa, pb

        def block(j, peaks):
            for r in range(1, SUB):
                peaks = step(j * SUB + r, r, peaks)
            keep(j)
            return step(j * SUB + SUB, SUB, peaks)

        peaks = lax.fori_loop(0, blocks - 1, block, (one, one))
        for r in range(1, SUB):
            peaks = step((blocks - 1) * SUB + r, r, peaks, r == SUB - 1)
        keep(blocks - 1)
        for i, (mh, ml) in enumerate(mats):
            mats_ref[i] = mh[0:states, :].astype(F32) + ml[0:states, :].astype(F32)

    shape = (rows, states)
    pl.run_scoped(
        body,
        pltpu.ACC(0)(shape, F32),
        pltpu.ACC(1)(shape, F32),
        pltpu.ACC(0)(shape, F32),
        pltpu.ACC(1)(shape, F32),
    )


def vmem():
    return pl.BlockSpec(memory_space=pltpu.VMEM)


def hbm():
    return pl.BlockSpec(memory_space=pltpu.MemorySpace.HBM)


def pinned(x):
    return pltpu.with_memory_space_constraint(x, pltpu.MemorySpace.HBM)


def transfer(cols, weight, mask, lengths, pdf_map, init):
    columns, frames = cols.shape
    states = weight.shape[0]
    blocks = frames // 2 // SUB
    out = jax.ShapeDtypeStruct
    return pl.pallas_call(
        functools.partial(transfer_kernel, frames),
        out_shape=(
            out((2, states, states), F32),
            out((2, blocks, 2, states, states), BF16),
            out((states // 128, frames, 128), F32),
            out((frames, 128), F32),
            out((states, states), BF16),
            out((states, states), BF16),
            out((8, states), F32),
        ),
        in_specs=[hbm()] * 5 + [vmem()],
        out_specs=[vmem()] * 7,
        scratch_shapes=[pltpu.VMEM((frames, states), F32)] * 2
        + [pltpu.VMEM((states, states), F32)]
        + [pltpu.VMEM((states, states), BF16)] * 4
        + [
            pltpu.SMEM(lengths.shape, jnp.int32),
            pltpu.SMEM(mask.shape, jnp.int32),
            pltpu.VMEM(weight.shape, F32),
            pltpu.VMEM((1, states), jnp.int32),
            pltpu.VMEM((1, states), F32),
            pltpu.SemaphoreType.DMA((5,)),
        ],
        compiler_params=pltpu.CompilerParams(vmem_limit_bytes=6 << 20),
        name="transfer",
    )(*map(pinned, (lengths, mask, weight, pdf_map[None, :], init[None, :])), cols)


def row_dot(v, matrix_high, matrix_low):
    n = v.shape[0]
    vh, vl = halves(v)
    both = jnp.concatenate([vh, vl], axis=0)
    x = dot(both, matrix_high)
    return x[0:n] + x[n:] + dot(vh, matrix_low)


def unit(v):
    return v / jnp.sum(v, axis=1, keepdims=True)


def pass_on(v, matrix):
    return row_dot(v, *halves(matrix)) * (1.0 / jnp.sum(v, axis=1, keepdims=True))


def in_order(own_ref, other_ref, do):
    core = lax.axis_index("tm") % 2

    @pl.when(core == 0)
    def _():
        do(own_ref.at[0], other_ref.at[0], own_ref.at[1], other_ref.at[1])

    @pl.when(core == 1)
    def _():
        do(other_ref.at[0], own_ref.at[0], other_ref.at[1], own_ref.at[1])


def first_kernel(start_ref, own_ref, other_ref, v_ref):
    def do(*mats):
        v = start_ref[...]
        for m in mats:
            v = pass_on(v, m[...])
        v_ref[...] = v

    in_order(own_ref, other_ref, do)


def group_kernel(own_ref, other_ref, all_ref, mid_ref):
    def times(left, right):
        d = dot3(*halves(left), *halves(right))
        return d * (1.0 / jnp.max(d, keepdims=True)[:, :1])

    def do(*mats):
        mid_ref[...] = times(mats[0][...], mats[1][...])
        all_ref[...] = times(mid_ref[...], times(mats[2][...], mats[3][...]))

    in_order(own_ref, other_ref, do)

    @pl.when(lax.axis_index("tm") % 2 == 1)
    def _():
        mid_ref[...] = times(mid_ref[...], other_ref[1])


def hop_kernel(v_ref, m_ref, out_ref):
    out_ref[...] = pass_on(v_ref[...], m_ref[...])


def small(kernel, name, outs, *args):
    return pl.pallas_call(
        kernel,
        out_shape=tuple(jax.ShapeDtypeStruct(shape, F32) for shape in outs),
        in_specs=[vmem()] * len(args),
        out_specs=[vmem()] * len(outs),
        compiler_params=pltpu.CompilerParams(vmem_limit_bytes=4 << 20),
        name=name,
    )(*args)


def pack_kernel(x_hbm, out_ref, x_ref, sem):
    copy = pltpu.make_async_copy(x_hbm, x_ref, sem)
    copy.start()
    copy.wait()
    groups = out_ref.shape[0]
    local = out_ref.shape[2]
    low = lax.broadcasted_iota(jnp.int32, (local, 128), 1) < 64
    for g in range(groups):
        for u in range(2):
            early = x_ref[u, :, g * 256 : g * 256 + 128]
            late = x_ref[u, :, g * 256 + 128 : g * 256 + 256]
            out_ref[g, 2 * u] = jnp.where(low, early, pltpu.roll(late, 64, 1))
            out_ref[g, 2 * u + 1] = jnp.where(low, pltpu.roll(early, 64, 1), late)


def pack(x, groups):
    local = x.shape[1]
    return pl.pallas_call(
        pack_kernel,
        out_shape=jax.ShapeDtypeStruct((groups, 4, local, 128), F32),
        in_specs=[hbm()],
        out_specs=vmem(),
        scratch_shapes=[pltpu.VMEM(x.shape, F32), pltpu.SemaphoreType.DMA],
        compiler_params=pltpu.CompilerParams(vmem_limit_bytes=4 << 20),
        name="pack",
    )(pinned(x))


def frames_kernel(frames, lengths_hbm, *refs):
    start_ref, *v_refs = refs[:-13]
    other_ref, mid_ref, pre_ref, e_ref, top_ref, th_ref, tl_ref, kept_ref, sent_ref, gain_ref, *scratch = refs[
        len(v_refs) + 1 :
    ]
    alpha_scr, lengths_ref, sem = scratch
    copy = pltpu.make_async_copy(lengths_hbm, lengths_ref, sem)
    copy.start()
    states = th_ref.shape[0]
    half = frames // 2
    blocks = half // SUB
    subs = 2 * blocks
    index = lax.axis_index("tm")
    utt, slots = place(half)
    v = start_ref[...]
    for g, ref in enumerate(v_refs):
        v = jnp.where(index // 4 == g + 1, ref[...], v)
    mid = pass_on(v, mid_ref[...])
    v = jnp.where(index % 2 == 1, pass_on(v, other_ref[0]), v)
    rows = [v[0:1]]
    for j in range(blocks - 1):
        rows.append(row_dot(v, pre_ref[0, j, 0], pre_ref[0, j, 1])[0:1])
    rows.append(mid[0:1])
    for j in range(blocks - 1):
        rows.append(row_dot(mid, pre_ref[1, j, 0], pre_ref[1, j, 1])[0:1])
    x = jnp.concatenate(rows, axis=0)
    total = jnp.sum(x, axis=1, keepdims=True)
    v, mid = unit(v), unit(mid)
    th, tl = th_ref[...], tl_ref[...]
    lane = lax.broadcasted_iota(jnp.int32, (subs, 128), 1)
    sub = lax.broadcasted_iota(jnp.int32, (subs, 128), 0)
    gains = jnp.zeros((subs, 128), F32)
    copy.wait()
    alive = [lengths_ref[utt] - slot for slot in slots]
    tiles = range(states // 128)
    for r in range(SUB):
        every = pl.ds(r, subs, stride=SUB)
        factor = jnp.concatenate([e_ref[k, every, :] for k in tiles], axis=1) * (1.0 / total)
        x = row_dot(x, th, tl) * factor
        total = jnp.sum(x, axis=1, keepdims=True)
        alpha = x * (1.0 / total)
        for k in tiles:
            alpha_scr[k, every, :] = alpha[:, k * 128 : (k + 1) * 128]
        live = (sub % blocks) * SUB + r < jnp.where(sub < blocks, alive[0], alive[1])
        gain = jnp.where(live, jnp.log(total) + top_ref[every, :], 0.0)
        gains = jnp.where(lane % SUB == r, gain, gains)
    for which, ref in ((utt, kept_ref), (1 - utt, sent_ref)):
        at = pl.multiple_of(which * half, half)
        left = jnp.where(which == 0, alive[0], alive[1])
        frame = lax.broadcasted_iota(jnp.int32, (half, 128), 0)
        end = pl.ds(at + jnp.clip(left - 1, 0, half - 1), 1)
        before = jnp.where(which == 0, v[0:1], mid[0:1])
        for k in tiles:
            cut = slice(k * 128, (k + 1) * 128)
            final = jnp.where(left > 0, alpha_scr[k, end, :], before[:, cut])
            ref[0:half, cut] = jnp.log(jnp.where(frame < left, alpha_scr[k, pl.ds(at, half), :], final))
    picked = jnp.where(lane // SUB == sub % blocks, gains, 0.0)
    lines = [jnp.sum(picked[k * blocks : (k + 1) * blocks], axis=0, keepdims=True) for k in range(2)]
    gain_ref[...] = jnp.where(utt == 0, lines[0], lines[1])
    line = jnp.where(utt == 0, lines[1], lines[0])
    sent_ref[half : half + 8, :] = jnp.concatenate([jnp.broadcast_to(line, (8, 128))] * (states // 128), axis=1)


def frames_pass(lengths, vs, other, mid, pre, e, top, th, tl):
    frames, states = top.shape[0], th.shape[0]
    half = frames // 2
    out = jax.ShapeDtypeStruct
    return pl.pallas_call(
        functools.partial(frames_kernel, frames),
        out_shape=(out((half, states), F32), out((half + 8, states), F32), out((1, 128), F32)),
        in_specs=[hbm()] + [vmem()] * (len(vs) + 7),
        out_specs=[vmem()] * 3,
        scratch_shapes=[
            pltpu.VMEM((states // 128, frames, 128), F32),
            pltpu.SMEM(lengths.shape, jnp.int32),
            pltpu.SemaphoreType.DMA,
        ],
        compiler_params=pltpu.CompilerParams(vmem_limit_bytes=6 << 20),
        name="frames",
    )(pinned(lengths), *vs, other, mid, pre, e, top, th, tl)


def join_kernel(kept_ref, gain_ref, got_ref, log_ref, out_gain_ref):
    half = kept_ref.shape[0]
    utt = (lax.axis_index("tm") // 2) % 2
    log_ref[utt] = kept_ref[...]
    log_ref[1 - utt] = got_ref[0:half, :]
    own = gain_ref[0:1, 0:half]
    got = got_ref[half : half + 1, 0:half]
    out_gain_ref[0:1, :] = jnp.where(utt == 0, own, got)
    out_gain_ref[1:2, :] = jnp.where(utt == 0, got, own)


def join(kept, gain, got):
    half, states = kept.shape
    out = jax.ShapeDtypeStruct
    return pl.pallas_call(
        join_kernel,
        out_shape=(out((2, half, states), F32), out((2, half), F32)),
        in_specs=[vmem()] * 3,
        out_specs=[vmem()] * 2,
        compiler_params=pltpu.CompilerParams(vmem_limit_bytes=4 << 20),
        name="join",
    )(kept, gain, got)


def shards(size, loglik, trans_weight, block_mask, init_weight, lengths, pdf_map):
    local = loglik.shape[2]
    groups = size // 4
    x = pack(jnp.transpose(loglik, (0, 2, 1)), groups)
    frames = x.shape[3]
    x = x.reshape(size, local, frames)
    cols = lax.all_to_all(x, "tm", 0, 0, tiled=True).reshape(size * local, frames)
    own, pre, e, top, th, tl, start = transfer(cols, trans_weight, block_mask, lengths, pdf_map, init_weight)
    other = lax.ppermute(own, "tm", [(i, i ^ 1) for i in range(size)])
    (v,) = small(first_kernel, "first", [start.shape], start, own, other)
    square = own.shape[1:]
    whole, mid = small(group_kernel, "group", [square, square], own, other)
    vs = [start]
    for g in range(1, groups):
        pairs = [(i, partner(i, g, groups)) for i in range(size)]
        vs.append(lax.ppermute(v, "tm", pairs))
        if g < groups - 1:
            (v,) = small(hop_kernel, "hop", [v.shape], vs[-1], whole)
    kept, sent, gain = frames_pass(lengths, vs, other, mid, pre, e, top, th, tl)
    got = lax.ppermute(sent, "tm", [(i, i ^ 2) for i in range(size)])
    return join(kept, gain, got)


def partner(index, turn, groups):
    group = index // 4
    other = group ^ 1 if turn % 2 else (group - 1 if group % 2 == 0 else group + 1)
    if 0 <= other < groups:
        return 4 * other + index % 4
    return index ^ 2


def solution(mesh):
    return jax.shard_map(
        functools.partial(shards, mesh.shape["tm"]),
        mesh=mesh,
        in_specs=(P("groups", None, "tm"), P(), P(), P(), P("groups"), P()),
        out_specs=(P("groups", "tm", None), P("groups", "tm")),
        check_vma=False,
    )
```

```python
import functools
import jax
import jax.numpy as jnp
from jax import lax
from jax.experimental import pallas as pl
from jax.experimental.pallas import tpu as pltpu
from jax.sharding import PartitionSpec as P

F32 = jnp.float32
BF16 = jnp.bfloat16
SUB = 8


def place(half):
    index = lax.axis_index("tm")
    first = (index // 4) * 4 * half + (index % 2) * half
    return (index // 2) % 2, (first, first + 2 * half)


def halves(x):
    high = x.astype(BF16)
    return high, (x - high.astype(F32)).astype(BF16)


def dot(a, b):
    return jnp.dot(a, b, preferred_element_type=F32)


def dot3(a_high, a_low, b_high, b_low):
    return dot(a_high, b_high) + dot(a_low, b_high) + dot(a_high, b_low)


def transfer_kernel(
    frames,
    lengths_hbm,
    mask_hbm,
    weight_hbm,
    map_hbm,
    init_hbm,
    cols_ref,
    mats_ref,
    pre_ref,
    e_ref,
    top_ref,
    th_ref,
    tl_ref,
    start_ref,
    g_scr,
    e_scr,
    t_scr,
    ah,
    al,
    bh,
    bl,
    lengths_ref,
    mask_ref,
    weight_ref,
    map_ref,
    init_ref,
    sems,
):
    copies = [
        pltpu.make_async_copy(src, dst, sems.at[i])
        for i, (src, dst) in enumerate(
            (
                (map_hbm, map_ref),
                (weight_hbm, weight_ref),
                (mask_hbm, mask_ref),
                (lengths_hbm, lengths_ref),
                (init_hbm, init_ref),
            )
        )
    ]
    for copy in copies:
        copy.start()
    states = weight_ref.shape[0]
    half = frames // 2
    rows = states // 2
    blocks = half // SUB
    utt, slots = place(half)
    cols = cols_ref[...].T
    copies[0].wait()
    pick = (lax.broadcasted_iota(jnp.int32, (cols.shape[1], states), 0) == map_ref[...]).astype(F32).astype(BF16)
    p1 = cols.astype(BF16)
    rest = cols - p1.astype(F32)
    p2, p3 = halves(rest)
    depth = 256
    pieces = cols.shape[1] // depth

    def gather(*accs):
        for k in range(pieces):
            cut = slice(k * depth, (k + 1) * depth)
            pltpu.matmul_push_rhs(pick[cut, :], 0, k % 2)
            pltpu.matmul_acc_lhs(accs[k % 2], p1[:, cut], 0)
            pltpu.matmul_acc_lhs(accs[k % 2], p2[:, cut], None)
            pltpu.matmul_acc_lhs(accs[k % 2], p3[:, cut], None)
        g_scr[...] = pltpu.matmul_pop(accs[0]) + pltpu.matmul_pop(accs[1])

    pl.run_scoped(gather, pltpu.ACC(0)((frames, states), F32), pltpu.ACC(1)((frames, states), F32))
    g = g_scr[...]
    top = jnp.max(g, axis=1, keepdims=True)
    e = jnp.exp(g - top)
    e_scr[...] = e
    for i in range(2):
        for k in range(states // 128):
            e_ref[i, k] = e[i * half : (i + 1) * half, k * 128 : (k + 1) * 128]
        top_ref[i] = jnp.broadcast_to(top[i * half : (i + 1) * half], (half, 128))

    for copy in copies[1:]:
        copy.wait()
    alive = [lengths_ref[utt] - slot for slot in slots]
    start_ref[...] = jnp.broadcast_to(unit(init_ref[...]), start_ref.shape)

    nb = mask_ref.shape[0]
    width = states // nb
    lane = lax.broadcasted_iota(jnp.int32, (1, states), 1) // width
    for r in range(nb):
        row = jnp.zeros((1, states), F32)
        for c in range(nb):
            row = jnp.where(lane == c, mask_ref[r, c].astype(F32), row)
        part = weight_ref[r * width : (r + 1) * width, :] * row
        t_scr[r * width : (r + 1) * width, :] = part / jnp.sum(part, axis=1, keepdims=True)
    th, tl = halves(t_scr[...])
    th_ref[...] = th
    tl_ref[...] = tl

    eye = (
        lax.broadcasted_iota(jnp.int32, (states, states), 0) == lax.broadcasted_iota(jnp.int32, (states, states), 1)
    ).astype(F32)
    for k, (mh, ml) in enumerate(((ah, al), (bh, bl))):
        off = k * half
        h, l = halves(jnp.where(alive[k] > 0, t_scr[...] * e_scr[off : off + 1, :], eye))
        mh[0:states, :] = h
        ml[0:states, :] = l

    def body(a0, a1, b0, b1):
        accs = ((a0, a1), (b0, b1))
        mats = ((ah, al), (bh, bl))

        def issue_a(high_loaded):
            for m in range(2):
                sl = pl.ds(m * rows, rows)
                pltpu.matmul_acc_lhs(accs[0][m], ah[sl, :], high_loaded)
                pltpu.matmul_acc_lhs(accs[0][m], al[sl, :], None)
            for m in range(2):
                pltpu.matmul_push_rhs(tl_ref[...], 1, m)
            for m in range(2):
                pltpu.matmul_acc_lhs(accs[0][m], ah[pl.ds(m * rows, rows), :], 1)

        def issue_b():
            for m in range(2):
                pltpu.matmul_acc_lhs(accs[1][m], bh[pl.ds(m * rows, rows), :], None)
            for m in range(2):
                pltpu.matmul_push_rhs(th_ref[...], 0, m)
            for m in range(2):
                sl = pl.ds(m * rows, rows)
                pltpu.matmul_acc_lhs(accs[1][m], bh[sl, :], 0)
                pltpu.matmul_acc_lhs(accs[1][m], bl[sl, :], None)

        def post(k, s, r, peak, freeze):
            look, use = r % 4 == 1 + 2 * k, r % 4 == (2 + 2 * k) % 4
            mh, ml = mats[k]
            er = e_scr[pl.ds(s + k * half, 1), :]
            if use:
                er = er * (1.0 / jnp.max(peak.astype(F32), keepdims=True)[:, :1])
            live = s < alive[k]
            new = None
            for m in range(2):
                x = pltpu.matmul_pop(accs[k][m]) * er
                h, l = halves(x)
                sl = pl.ds(m * rows, rows)
                if freeze:
                    h = jnp.where(live, h, mh[sl, :])
                    l = jnp.where(live, l, ml[sl, :])
                mh[sl, :] = h
                ml[sl, :] = l
                if look:
                    y = jnp.max(h.reshape(rows // 16, 16, states), axis=0)
                    new = y if new is None else jnp.maximum(new, y)
            return new if look else peak

        def keep(j):
            for k in range(2):
                for i in range(2):
                    pre_ref[k, j, i] = mats[k][i][0:states, :]

        for m in range(2):
            pltpu.matmul_push_rhs(th_ref[...], 0, m)
        issue_a(0)
        one = jnp.ones((16, states), BF16)

        def step(s, r, peaks, freeze, last=False):
            pa, pb = peaks
            issue_b()
            pa = post(0, s, r, pa, freeze)
            if not last:
                issue_a(None)
            pb = post(1, s, r, pb, freeze)
            return pa, pb

        def eight(j, peaks, freeze):
            for r in range(1, SUB):
                peaks = step(j * SUB + r, r, peaks, freeze)
            keep(j)
            return step(j * SUB + SUB, SUB, peaks, freeze)

        def block(j, peaks):
            full = jnp.minimum(alive[0], alive[1]) > j * SUB + SUB
            return lax.cond(full, lambda p: eight(j, p, False), lambda p: eight(j, p, True), peaks)

        peaks = lax.fori_loop(0, blocks - 1, block, (one, one))
        for r in range(1, SUB):
            peaks = step((blocks - 1) * SUB + r, r, peaks, True, r == SUB - 1)
        keep(blocks - 1)
        for i, (mh, ml) in enumerate(mats):
            mats_ref[i] = mh[0:states, :].astype(F32) + ml[0:states, :].astype(F32)

    shape = (rows, states)
    pl.run_scoped(
        body,
        pltpu.ACC(0)(shape, F32),
        pltpu.ACC(1)(shape, F32),
        pltpu.ACC(0)(shape, F32),
        pltpu.ACC(1)(shape, F32),
    )


def vmem():
    return pl.BlockSpec(memory_space=pltpu.VMEM)


def hbm():
    return pl.BlockSpec(memory_space=pltpu.MemorySpace.HBM)


def pinned(x):
    return pltpu.with_memory_space_constraint(x, pltpu.MemorySpace.HBM)


def transfer(cols, weight, mask, lengths, pdf_map, init):
    columns, frames = cols.shape
    states = weight.shape[0]
    blocks = frames // 2 // SUB
    out = jax.ShapeDtypeStruct
    return pl.pallas_call(
        functools.partial(transfer_kernel, frames),
        out_shape=(
            out((2, states, states), F32),
            out((2, blocks, 2, states, states), BF16),
            out((2, states // 128, frames // 2, 128), F32),
            out((2, frames // 2, 128), F32),
            out((states, states), BF16),
            out((states, states), BF16),
            out((8, states), F32),
        ),
        in_specs=[hbm()] * 5 + [vmem()],
        out_specs=[vmem()] * 7,
        scratch_shapes=[pltpu.VMEM((frames, states), F32)] * 2
        + [pltpu.VMEM((states, states), F32)]
        + [pltpu.VMEM((states, states), BF16)] * 4
        + [
            pltpu.SMEM(lengths.shape, jnp.int32),
            pltpu.SMEM(mask.shape, jnp.int32),
            pltpu.VMEM(weight.shape, F32),
            pltpu.VMEM((1, states), jnp.int32),
            pltpu.VMEM((1, states), F32),
            pltpu.SemaphoreType.DMA((5,)),
        ],
        compiler_params=pltpu.CompilerParams(vmem_limit_bytes=6 << 20),
        name="transfer",
    )(*map(pinned, (lengths, mask, weight, pdf_map[None, :], init[None, :])), cols)


def row_dot(v, matrix_high, matrix_low):
    n = v.shape[0]
    vh, vl = halves(v)
    both = jnp.concatenate([vh, vl], axis=0)
    x = dot(both, matrix_high)
    return x[0:n] + x[n:] + dot(vh, matrix_low)


def unit(v):
    return v / jnp.sum(v, axis=1, keepdims=True)


def pass_on(v, matrix):
    return row_dot(v, *halves(matrix)) * (1.0 / jnp.sum(v, axis=1, keepdims=True))


def in_order(own_ref, other_ref, do):
    core = lax.axis_index("tm") % 2

    @pl.when(core == 0)
    def _():
        do(own_ref.at[0], other_ref.at[0], own_ref.at[1], other_ref.at[1])

    @pl.when(core == 1)
    def _():
        do(other_ref.at[0], own_ref.at[0], other_ref.at[1], own_ref.at[1])


def first_kernel(start_ref, own_ref, other_ref, v_ref):
    def do(*mats):
        v = start_ref[...]
        for m in mats:
            v = pass_on(v, m[...])
        v_ref[...] = v

    in_order(own_ref, other_ref, do)


def group_kernel(own_ref, other_ref, all_ref, mid_ref):
    def times(left, right):
        d = dot3(*halves(left), *halves(right))
        return d * (1.0 / jnp.max(d, keepdims=True)[:, :1])

    def do(*mats):
        mid_ref[...] = times(mats[0][...], mats[1][...])
        all_ref[...] = times(mid_ref[...], times(mats[2][...], mats[3][...]))

    in_order(own_ref, other_ref, do)

    @pl.when(lax.axis_index("tm") % 2 == 1)
    def _():
        mid_ref[...] = times(mid_ref[...], other_ref[1])


def hop_kernel(v_ref, m_ref, out_ref):
    out_ref[...] = pass_on(v_ref[...], m_ref[...])


def small(kernel, name, outs, *args):
    return pl.pallas_call(
        kernel,
        out_shape=tuple(jax.ShapeDtypeStruct(shape, F32) for shape in outs),
        in_specs=[vmem()] * len(args),
        out_specs=[vmem()] * len(outs),
        compiler_params=pltpu.CompilerParams(vmem_limit_bytes=4 << 20),
        name=name,
    )(*args)


def pack_kernel(x_hbm, out_ref, x_ref, sem):
    copy = pltpu.make_async_copy(x_hbm, x_ref, sem)
    copy.start()
    copy.wait()
    groups = out_ref.shape[0]
    local = out_ref.shape[2]
    low = lax.broadcasted_iota(jnp.int32, (local, 128), 1) < 64
    for g in range(groups):
        for u in range(2):
            early = x_ref[u, :, g * 256 : g * 256 + 128]
            late = x_ref[u, :, g * 256 + 128 : g * 256 + 256]
            out_ref[g, 2 * u] = jnp.where(low, early, pltpu.roll(late, 64, 1))
            out_ref[g, 2 * u + 1] = jnp.where(low, pltpu.roll(early, 64, 1), late)


def pack(x, groups):
    local = x.shape[1]
    return pl.pallas_call(
        pack_kernel,
        out_shape=jax.ShapeDtypeStruct((groups, 4, local, 128), F32),
        in_specs=[hbm()],
        out_specs=vmem(),
        scratch_shapes=[pltpu.VMEM(x.shape, F32), pltpu.SemaphoreType.DMA],
        compiler_params=pltpu.CompilerParams(vmem_limit_bytes=4 << 20),
        name="pack",
    )(pinned(x))


def slot_kernel(sent, lengths_hbm, *refs):
    start_ref, *v_refs = refs[:-11]
    other_ref, mid_ref, pre_ref, e_ref, top_ref, th_ref, tl_ref, out_ref, *scratch = refs[len(v_refs) + 1 :]
    alpha_scr, lengths_ref, sem = scratch
    copy = pltpu.make_async_copy(lengths_hbm, lengths_ref, sem)
    copy.start()
    states = th_ref.shape[0]
    half = top_ref.shape[1]
    blocks = half // SUB
    index = lax.axis_index("tm")
    utt, slots = place(half)
    slot = 1 - utt if sent else utt

    v = start_ref[...]
    for g, ref in enumerate(v_refs):
        v = jnp.where(index // 4 == g + 1, ref[...], v)
    before = jnp.where(index % 2 == 1, pass_on(v, other_ref[0]), v)
    v = jnp.where(slot == 1, pass_on(v, mid_ref[...]), before)
    rows = [v[0:1]]
    for j in range(blocks - 1):
        rows.append(row_dot(v, pre_ref[slot, j, 0], pre_ref[slot, j, 1])[0:1])
    x = jnp.concatenate(rows, axis=0)
    total = jnp.sum(x, axis=1, keepdims=True)
    th, tl = th_ref[...], tl_ref[...]
    lane = lax.broadcasted_iota(jnp.int32, (blocks, 128), 1)
    sub = lax.broadcasted_iota(jnp.int32, (blocks, 128), 0)
    gains = jnp.zeros((blocks, 128), F32)
    copy.wait()
    left = lengths_ref[utt] - jnp.where(slot == 0, slots[0], slots[1])
    tiles = range(states // 128)
    for r in range(SUB):
        every = pl.ds(r, blocks, stride=SUB)
        factor = jnp.concatenate([e_ref[slot, k, every, :] for k in tiles], axis=1) * (1.0 / total)
        x = row_dot(x, th, tl) * factor
        total = jnp.sum(x, axis=1, keepdims=True)
        alpha = x * (1.0 / total)
        for k in tiles:
            alpha_scr[k, every, :] = alpha[:, k * 128 : (k + 1) * 128]
        live = sub * SUB + r < left
        gain = jnp.where(live, jnp.log(total) + top_ref[slot, every, :], 0.0)
        gains = jnp.where(lane % SUB == r, gain, gains)
    v = unit(v)
    frame = lax.broadcasted_iota(jnp.int32, (half, 128), 0)
    end = pl.ds(jnp.clip(left - 1, 0, half - 1), 1)
    for k in tiles:
        cut = slice(k * 128, (k + 1) * 128)
        final = jnp.where(left > 0, alpha_scr[k, end, :], v[0:1, cut])
        out_ref[0:half, cut] = jnp.log(jnp.where(frame < left, alpha_scr[k], final))
    line = jnp.sum(jnp.where(lane // SUB == sub, gains, 0.0), axis=0, keepdims=True)
    out_ref[half : half + 8, :] = jnp.concatenate([jnp.broadcast_to(line, (8, 128))] * (states // 128), axis=1)


def slot_pass(sent, lengths, vs, other, mid, pre, e, top, th, tl):
    half, states = top.shape[1], th.shape[0]
    return pl.pallas_call(
        functools.partial(slot_kernel, sent),
        out_shape=jax.ShapeDtypeStruct((half + 8, states), F32),
        in_specs=[hbm()] + [vmem()] * (len(vs) + 7),
        out_specs=vmem(),
        scratch_shapes=[
            pltpu.VMEM((states // 128, half, 128), F32),
            pltpu.SMEM(lengths.shape, jnp.int32),
            pltpu.SemaphoreType.DMA,
        ],
        compiler_params=pltpu.CompilerParams(vmem_limit_bytes=6 << 20),
        name="sent" if sent else "kept",
    )(pinned(lengths), *vs, other, mid, pre, e, top, th, tl)


def join_kernel(kept_ref, got_ref, log_ref, gain_ref):
    half = log_ref.shape[1]
    utt = (lax.axis_index("tm") // 2) % 2
    log_ref[utt] = kept_ref[0:half, :]
    log_ref[1 - utt] = got_ref[0:half, :]
    own = kept_ref[half : half + 1, 0:half]
    got = got_ref[half : half + 1, 0:half]
    gain_ref[0:1, :] = jnp.where(utt == 0, own, got)
    gain_ref[1:2, :] = jnp.where(utt == 0, got, own)


def shards(size, loglik, trans_weight, block_mask, init_weight, lengths, pdf_map):
    local = loglik.shape[2]
    groups = size // 4
    x = pack(jnp.transpose(loglik, (0, 2, 1)), groups)
    frames = x.shape[3]
    x = x.reshape(size, local, frames)
    cols = lax.all_to_all(x, "tm", 0, 0, tiled=True).reshape(size * local, frames)
    own, pre, e, top, th, tl, start = transfer(cols, trans_weight, block_mask, lengths, pdf_map, init_weight)
    other = lax.ppermute(own, "tm", [(i, i ^ 1) for i in range(size)])
    (v,) = small(first_kernel, "first", [start.shape], start, own, other)
    square = own.shape[1:]
    whole, mid = small(group_kernel, "group", [square, square], own, other)
    vs = [start]
    for g in range(1, groups):
        pairs = [(i, partner(i, g, groups)) for i in range(size)]
        vs.append(lax.ppermute(v, "tm", pairs))
        if g < groups - 1:
            (v,) = small(hop_kernel, "hop", [v.shape], vs[-1], whole)
    given = (lengths, vs, other, mid, pre, e, top, th, tl)
    sent = slot_pass(True, *given)
    got = lax.ppermute(sent, "tm", [(i, i ^ 2) for i in range(size)])
    kept = slot_pass(False, *given)
    half, states = kept.shape[0] - 8, kept.shape[1]
    return small(join_kernel, "join", [(2, half, states), (2, half)], kept, got)


def partner(index, turn, groups):
    group = index // 4
    other = group ^ 1 if turn % 2 else (group - 1 if group % 2 == 0 else group + 1)
    if 0 <= other < groups:
        return (4 * other + index % 4) ^ 1
    return index ^ 3


def solution(mesh):
    return jax.shard_map(
        functools.partial(shards, mesh.shape["tm"]),
        mesh=mesh,
        in_specs=(P("groups", None, "tm"), P(), P(), P(), P("groups"), P()),
        out_specs=(P("groups", "tm", None), P("groups", "tm")),
        check_vma=False,
    )
```

```python
import functools
import jax
import jax.numpy as jnp
from jax import lax
from jax.experimental import pallas as pl
from jax.experimental.pallas import tpu as pltpu
from jax.sharding import PartitionSpec as P

F32 = jnp.float32
BF16 = jnp.bfloat16
SUB = 8


def place(half):
    index = lax.axis_index("tm")
    first = (index // 4) * 4 * half + (index % 2) * half
    return (index // 2) % 2, (first, first + 2 * half)


def halves(x):
    high = x.astype(BF16)
    return high, (x - high.astype(F32)).astype(BF16)


def dot(a, b):
    return jnp.dot(a, b, preferred_element_type=F32)


def dot3(a_high, a_low, b_high, b_low):
    return dot(a_high, b_high) + dot(a_low, b_high) + dot(a_high, b_low)


def transfer_kernel(
    frames,
    lengths_hbm,
    mask_hbm,
    weight_hbm,
    init_hbm,
    cols_ref,
    map_ref,
    mats_ref,
    pre_ref,
    e_ref,
    top_ref,
    th_ref,
    tl_ref,
    start_ref,
    g_scr,
    e_scr,
    t_scr,
    ah,
    al,
    bh,
    bl,
    lengths_ref,
    mask_ref,
    weight_ref,
    init_ref,
    sems,
):
    copies = [
        pltpu.make_async_copy(src, dst, sems.at[i])
        for i, (src, dst) in enumerate(
            (
                (weight_hbm, weight_ref),
                (mask_hbm, mask_ref),
                (lengths_hbm, lengths_ref),
                (init_hbm, init_ref),
            )
        )
    ]
    for copy in copies:
        copy.start()
    states = weight_ref.shape[0]
    half = frames // 2
    rows = states // 2
    blocks = half // SUB
    utt, slots = place(half)
    cols = cols_ref[...].T
    pick = (lax.broadcasted_iota(jnp.int32, (cols.shape[1], states), 0) == map_ref[...]).astype(F32).astype(BF16)
    p1 = cols.astype(BF16)
    rest = cols - p1.astype(F32)
    p2, p3 = halves(rest)
    depth = 256
    pieces = cols.shape[1] // depth

    def gather(*accs):
        for k in range(pieces):
            cut = slice(k * depth, (k + 1) * depth)
            pltpu.matmul_push_rhs(pick[cut, :], 0, k % 2)
            pltpu.matmul_acc_lhs(accs[k % 2], p1[:, cut], 0)
            pltpu.matmul_acc_lhs(accs[k % 2], p2[:, cut], None)
            pltpu.matmul_acc_lhs(accs[k % 2], p3[:, cut], None)
        g_scr[...] = pltpu.matmul_pop(accs[0]) + pltpu.matmul_pop(accs[1])

    pl.run_scoped(gather, pltpu.ACC(0)((frames, states), F32), pltpu.ACC(1)((frames, states), F32))
    g = g_scr[...]
    top = jnp.max(g, axis=1, keepdims=True)
    e = jnp.exp(g - top)
    e_scr[...] = e
    for i in range(2):
        for k in range(states // 128):
            e_ref[i, k] = e[i * half : (i + 1) * half, k * 128 : (k + 1) * 128]
        top_ref[i] = jnp.broadcast_to(top[i * half : (i + 1) * half], (half, 128))

    for copy in copies:
        copy.wait()
    alive = [lengths_ref[utt] - slot for slot in slots]
    start_ref[...] = jnp.broadcast_to(unit(init_ref[...]), start_ref.shape)

    nb = mask_ref.shape[0]
    width = states // nb
    lane = lax.broadcasted_iota(jnp.int32, (1, states), 1) // width
    for r in range(nb):
        row = jnp.zeros((1, states), F32)
        for c in range(nb):
            row = jnp.where(lane == c, mask_ref[r, c].astype(F32), row)
        part = weight_ref[r * width : (r + 1) * width, :] * row
        t_scr[r * width : (r + 1) * width, :] = part / jnp.sum(part, axis=1, keepdims=True)
    th, tl = halves(t_scr[...])
    th_ref[...] = th
    tl_ref[...] = tl

    eye = (
        lax.broadcasted_iota(jnp.int32, (states, states), 0) == lax.broadcasted_iota(jnp.int32, (states, states), 1)
    ).astype(F32)
    for k, (mh, ml) in enumerate(((ah, al), (bh, bl))):
        off = k * half
        h, l = halves(jnp.where(alive[k] > 0, t_scr[...] * e_scr[off : off + 1, :], eye))
        mh[0:states, :] = h
        ml[0:states, :] = l

    def body(a0, a1, b0, b1):
        accs = ((a0, a1), (b0, b1))
        mats = ((ah, al), (bh, bl))

        def issue_a(high_loaded):
            for m in range(2):
                sl = pl.ds(m * rows, rows)
                pltpu.matmul_acc_lhs(accs[0][m], ah[sl, :], high_loaded)
                pltpu.matmul_acc_lhs(accs[0][m], al[sl, :], None)
            for m in range(2):
                pltpu.matmul_push_rhs(tl_ref[...], 1, m)
            for m in range(2):
                pltpu.matmul_acc_lhs(accs[0][m], ah[pl.ds(m * rows, rows), :], 1)

        def issue_b():
            for m in range(2):
                pltpu.matmul_acc_lhs(accs[1][m], bh[pl.ds(m * rows, rows), :], None)
            for m in range(2):
                pltpu.matmul_push_rhs(th_ref[...], 0, m)
            for m in range(2):
                sl = pl.ds(m * rows, rows)
                pltpu.matmul_acc_lhs(accs[1][m], bh[sl, :], 0)
                pltpu.matmul_acc_lhs(accs[1][m], bl[sl, :], None)

        def post(k, s, r, peak, freeze):
            look, use = r % 4 == 1 + 2 * k, r % 4 == (2 + 2 * k) % 4
            mh, ml = mats[k]
            er = e_scr[pl.ds(s + k * half, 1), :]
            if use:
                er = er * (1.0 / jnp.max(peak.astype(F32), keepdims=True)[:, :1])
            live = s < alive[k]
            new = None
            for m in range(2):
                x = pltpu.matmul_pop(accs[k][m]) * er
                h, l = halves(x)
                sl = pl.ds(m * rows, rows)
                if freeze:
                    h = jnp.where(live, h, mh[sl, :])
                    l = jnp.where(live, l, ml[sl, :])
                mh[sl, :] = h
                ml[sl, :] = l
                if look:
                    y = jnp.max(h.reshape(rows // 16, 16, states), axis=0)
                    new = y if new is None else jnp.maximum(new, y)
            return new if look else peak

        def keep(j):
            for k in range(2):
                for i in range(2):
                    pre_ref[k, j, i] = mats[k][i][0:states, :]

        for m in range(2):
            pltpu.matmul_push_rhs(th_ref[...], 0, m)
        issue_a(0)
        one = jnp.ones((16, states), BF16)

        def step(s, r, peaks, freeze, last=False):
            pa, pb = peaks
            issue_b()
            pa = post(0, s, r, pa, freeze)
            if not last:
                issue_a(None)
            pb = post(1, s, r, pb, freeze)
            return pa, pb

        def eight(j, peaks, freeze):
            for r in range(1, SUB):
                peaks = step(j * SUB + r, r, peaks, freeze)
            keep(j)
            return step(j * SUB + SUB, SUB, peaks, freeze)

        def block(j, peaks):
            full = jnp.minimum(alive[0], alive[1]) > j * SUB + SUB
            return lax.cond(full, lambda p: eight(j, p, False), lambda p: eight(j, p, True), peaks)

        peaks = lax.fori_loop(0, blocks - 1, block, (one, one))
        for r in range(1, SUB):
            peaks = step((blocks - 1) * SUB + r, r, peaks, True, r == SUB - 1)
        keep(blocks - 1)
        for i, (mh, ml) in enumerate(mats):
            mats_ref[i] = mh[0:states, :].astype(F32) + ml[0:states, :].astype(F32)

    shape = (rows, states)
    pl.run_scoped(
        body,
        pltpu.ACC(0)(shape, F32),
        pltpu.ACC(1)(shape, F32),
        pltpu.ACC(0)(shape, F32),
        pltpu.ACC(1)(shape, F32),
    )


def vmem():
    return pl.BlockSpec(memory_space=pltpu.VMEM)


def hbm():
    return pl.BlockSpec(memory_space=pltpu.MemorySpace.HBM)


def pinned(x):
    return pltpu.with_memory_space_constraint(x, pltpu.MemorySpace.HBM)


def transfer(cols, columns_of, weight, mask, lengths, init):
    columns, frames = cols.shape
    states = weight.shape[0]
    blocks = frames // 2 // SUB
    out = jax.ShapeDtypeStruct
    return pl.pallas_call(
        functools.partial(transfer_kernel, frames),
        out_shape=(
            out((2, states, states), F32),
            out((2, blocks, 2, states, states), BF16),
            out((2, states // 128, frames // 2, 128), F32),
            out((2, frames // 2, 128), F32),
            out((states, states), BF16),
            out((states, states), BF16),
            out((8, states), F32),
        ),
        in_specs=[hbm()] * 4 + [vmem()] * 2,
        out_specs=[vmem()] * 7,
        scratch_shapes=[pltpu.VMEM((frames, states), F32)] * 2
        + [pltpu.VMEM((states, states), F32)]
        + [pltpu.VMEM((states, states), BF16)] * 4
        + [
            pltpu.SMEM(lengths.shape, jnp.int32),
            pltpu.SMEM(mask.shape, jnp.int32),
            pltpu.VMEM(weight.shape, F32),
            pltpu.VMEM((1, states), F32),
            pltpu.SemaphoreType.DMA((4,)),
        ],
        compiler_params=pltpu.CompilerParams(vmem_limit_bytes=6 << 20),
        name="transfer",
    )(*map(pinned, (lengths, mask, weight, init[None, :])), cols, columns_of)


def row_dot(v, matrix_high, matrix_low):
    n = v.shape[0]
    vh, vl = halves(v)
    both = jnp.concatenate([vh, vl], axis=0)
    x = dot(both, matrix_high)
    return x[0:n] + x[n:] + dot(vh, matrix_low)


def unit(v):
    return v / jnp.sum(v, axis=1, keepdims=True)


def pass_on(v, matrix):
    return row_dot(v, *halves(matrix)) * (1.0 / jnp.sum(v, axis=1, keepdims=True))


def in_order(own_ref, other_ref, do):
    core = lax.axis_index("tm") % 2

    @pl.when(core == 0)
    def _():
        do(own_ref.at[0], other_ref.at[0], own_ref.at[1], other_ref.at[1])

    @pl.when(core == 1)
    def _():
        do(other_ref.at[0], own_ref.at[0], other_ref.at[1], own_ref.at[1])


def first_kernel(start_ref, own_ref, other_ref, v_ref):
    def do(*mats):
        v = start_ref[...]
        for m in mats:
            v = pass_on(v, m[...])
        v_ref[...] = v

    in_order(own_ref, other_ref, do)


def group_kernel(own_ref, other_ref, all_ref, mid_ref):
    def times(left, right):
        d = dot3(*halves(left), *halves(right))
        return d * (1.0 / jnp.max(d, keepdims=True)[:, :1])

    def do(*mats):
        mid_ref[...] = times(mats[0][...], mats[1][...])
        all_ref[...] = times(mid_ref[...], times(mats[2][...], mats[3][...]))

    in_order(own_ref, other_ref, do)

    @pl.when(lax.axis_index("tm") % 2 == 1)
    def _():
        mid_ref[...] = times(mid_ref[...], other_ref[1])


def hop_kernel(v_ref, m_ref, out_ref):
    out_ref[...] = pass_on(v_ref[...], m_ref[...])


def small(kernel, name, outs, *args):
    return pl.pallas_call(
        kernel,
        out_shape=tuple(jax.ShapeDtypeStruct(shape, F32) for shape in outs),
        in_specs=[vmem()] * len(args),
        out_specs=[vmem()] * len(outs),
        compiler_params=pltpu.CompilerParams(vmem_limit_bytes=4 << 20),
        name=name,
    )(*args)


def pack_kernel(x_hbm, map_hbm, out_ref, map_ref, x_ref, sems):
    map_copy = pltpu.make_async_copy(map_hbm, map_ref, sems.at[1])
    copy = pltpu.make_async_copy(x_hbm, x_ref, sems.at[0])
    copy.start()
    map_copy.start()
    copy.wait()
    map_copy.wait()
    groups = out_ref.shape[0]
    local = out_ref.shape[2]
    low = lax.broadcasted_iota(jnp.int32, (local, 128), 1) < 64
    for g in range(groups):
        for u in range(2):
            early = x_ref[u, :, g * 256 : g * 256 + 128]
            late = x_ref[u, :, g * 256 + 128 : g * 256 + 256]
            out_ref[g, 2 * u] = jnp.where(low, early, pltpu.roll(late, 64, 1))
            out_ref[g, 2 * u + 1] = jnp.where(low, pltpu.roll(early, 64, 1), late)


def pack(x, pdf_map, groups):
    local = x.shape[1]
    return pl.pallas_call(
        pack_kernel,
        out_shape=(
            jax.ShapeDtypeStruct((groups, 4, local, 128), F32),
            jax.ShapeDtypeStruct((1, pdf_map.shape[0]), jnp.int32),
        ),
        in_specs=[hbm()] * 2,
        out_specs=[vmem()] * 2,
        scratch_shapes=[pltpu.VMEM(x.shape, F32), pltpu.SemaphoreType.DMA((2,))],
        compiler_params=pltpu.CompilerParams(vmem_limit_bytes=4 << 20),
        name="pack",
    )(pinned(x), pinned(pdf_map[None, :]))


def slot_kernel(sent, lengths_hbm, *refs):
    start_ref, *v_refs = refs[:-11]
    other_ref, mid_ref, pre_ref, e_ref, top_ref, th_ref, tl_ref, out_ref, *scratch = refs[len(v_refs) + 1 :]
    alpha_scr, lengths_ref, sem = scratch
    copy = pltpu.make_async_copy(lengths_hbm, lengths_ref, sem)
    copy.start()
    states = th_ref.shape[0]
    half = top_ref.shape[1]
    blocks = half // SUB
    index = lax.axis_index("tm")
    utt, slots = place(half)
    slot = 1 - utt if sent else utt

    def body(acc_high, acc_low):
        def stacked(v):
            return jnp.concatenate(halves(v), axis=0)

        def load(high, low):
            pltpu.matmul_push_rhs(high, 0, 0)
            pltpu.matmul_push_rhs(low, 0, 1)

        def times(v, fresh):
            both = stacked(v)
            stage = 0 if fresh else None
            pltpu.matmul_acc_lhs(acc_high, both, stage)
            pltpu.matmul_acc_lhs(acc_low, both, stage)
            y = pltpu.matmul_pop(acc_high) + pltpu.matmul_pop(acc_low)
            return y[0:8] + y[8:16]

        def passed(v, matrix):
            load(*halves(matrix))
            return times(v, True) * (1.0 / jnp.sum(v, axis=1, keepdims=True))

        v = start_ref[...]
        for g, ref in enumerate(v_refs):
            v = jnp.where(index // 4 == g + 1, ref[...], v)
        before = jnp.where(index % 2 == 1, passed(v, other_ref[0]), v)
        v = jnp.where(slot == 1, passed(v, mid_ref[...]), before)
        rows = [v[0:1]]
        for j in range(blocks - 1):
            load(pre_ref[slot, j, 0], pre_ref[slot, j, 1])
            rows.append(times(v, True)[0:1])
        x = jnp.concatenate(rows, axis=0)
        total = jnp.sum(x, axis=1, keepdims=True)
        load(th_ref[...], tl_ref[...])
        lane = lax.broadcasted_iota(jnp.int32, (blocks, 128), 1)
        sub = lax.broadcasted_iota(jnp.int32, (blocks, 128), 0)
        gains = jnp.zeros((blocks, 128), F32)
        copy.wait()
        left = lengths_ref[utt] - jnp.where(slot == 0, slots[0], slots[1])
        tiles = range(states // 128)
        for r in range(SUB):
            every = pl.ds(r, blocks, stride=SUB)
            factor = jnp.concatenate([e_ref[slot, k, every, :] for k in tiles], axis=1) * (1.0 / total)
            x = times(x, r == 0) * factor
            total = jnp.sum(x, axis=1, keepdims=True)
            alpha = x * (1.0 / total)
            for k in tiles:
                alpha_scr[k, every, :] = alpha[:, k * 128 : (k + 1) * 128]
            live = sub * SUB + r < left
            gain = jnp.where(live, jnp.log(total) + top_ref[slot, every, :], 0.0)
            gains = jnp.where(lane % SUB == r, gain, gains)
        v = unit(v)
        frame = lax.broadcasted_iota(jnp.int32, (half, 128), 0)
        end = pl.ds(jnp.clip(left - 1, 0, half - 1), 1)
        for k in tiles:
            cut = slice(k * 128, (k + 1) * 128)
            final = jnp.where(left > 0, alpha_scr[k, end, :], v[0:1, cut])
            out_ref[0:half, cut] = jnp.log(jnp.where(frame < left, alpha_scr[k], final))
        line = jnp.sum(jnp.where(lane // SUB == sub, gains, 0.0), axis=0, keepdims=True)
        out_ref[half : half + 8, :] = jnp.concatenate([jnp.broadcast_to(line, (8, 128))] * (states // 128), axis=1)

    shape = (16, states)
    pl.run_scoped(body, pltpu.ACC(0)(shape, F32), pltpu.ACC(1)(shape, F32))


def slot_pass(sent, lengths, vs, other, mid, pre, e, top, th, tl):
    half, states = top.shape[1], th.shape[0]
    return pl.pallas_call(
        functools.partial(slot_kernel, sent),
        out_shape=jax.ShapeDtypeStruct((half + 8, states), F32),
        in_specs=[hbm()] + [vmem()] * (len(vs) + 7),
        out_specs=vmem(),
        scratch_shapes=[
            pltpu.VMEM((states // 128, half, 128), F32),
            pltpu.SMEM(lengths.shape, jnp.int32),
            pltpu.SemaphoreType.DMA,
        ],
        compiler_params=pltpu.CompilerParams(vmem_limit_bytes=6 << 20),
        name="sent" if sent else "kept",
    )(pinned(lengths), *vs, other, mid, pre, e, top, th, tl)


def join_kernel(kept_ref, got_ref, log_ref, gain_ref):
    half = log_ref.shape[1]
    utt = (lax.axis_index("tm") // 2) % 2
    log_ref[utt] = kept_ref[0:half, :]
    log_ref[1 - utt] = got_ref[0:half, :]
    own = kept_ref[half : half + 1, 0:half]
    got = got_ref[half : half + 1, 0:half]
    gain_ref[0:1, :] = jnp.where(utt == 0, own, got)
    gain_ref[1:2, :] = jnp.where(utt == 0, got, own)


def shards(size, loglik, trans_weight, block_mask, init_weight, lengths, pdf_map):
    local = loglik.shape[2]
    groups = size // 4
    x, columns_of = pack(jnp.transpose(loglik, (0, 2, 1)), pdf_map, groups)
    frames = x.shape[3]
    x = x.reshape(size, local, frames)
    cols = lax.all_to_all(x, "tm", 0, 0, tiled=True).reshape(size * local, frames)
    own, pre, e, top, th, tl, start = transfer(cols, columns_of, trans_weight, block_mask, lengths, init_weight)
    other = lax.ppermute(own, "tm", [(i, i ^ 1) for i in range(size)])
    (v,) = small(first_kernel, "first", [start.shape], start, own, other)
    square = own.shape[1:]
    whole, mid = small(group_kernel, "group", [square, square], own, other)
    vs = [start]
    for g in range(1, groups):
        pairs = [(i, partner(i, g, groups)) for i in range(size)]
        vs.append(lax.ppermute(v, "tm", pairs))
        if g < groups - 1:
            (v,) = small(hop_kernel, "hop", [v.shape], vs[-1], whole)
    given = (lengths, vs, other, mid, pre, e, top, th, tl)
    sent = slot_pass(True, *given)
    got = lax.ppermute(sent, "tm", [(i, i ^ 2) for i in range(size)])
    kept = slot_pass(False, *given)
    half, states = kept.shape[0] - 8, kept.shape[1]
    return small(join_kernel, "join", [(2, half, states), (2, half)], kept, got)


def partner(index, turn, groups):
    group = index // 4
    other = group ^ 1 if turn % 2 else (group - 1 if group % 2 == 0 else group + 1)
    if 0 <= other < groups:
        return (4 * other + index % 4) ^ 1
    return index ^ 3


def solution(mesh):
    return jax.shard_map(
        functools.partial(shards, mesh.shape["tm"]),
        mesh=mesh,
        in_specs=(P("groups", None, "tm"), P(), P(), P(), P("groups"), P()),
        out_specs=(P("groups", "tm", None), P("groups", "tm")),
        check_vma=False,
    )
```

```python
import functools
import jax
import jax.numpy as jnp
from jax import lax
from jax.experimental import pallas as pl
from jax.experimental.pallas import tpu as pltpu
from jax.sharding import PartitionSpec as P

F32 = jnp.float32
BF16 = jnp.bfloat16
SUB = 8


def place(half):
    index = lax.axis_index("tm")
    first = (index // 4) * 4 * half + (index % 2) * half
    return (index // 2) % 2, (first, first + 2 * half)


def halves(x):
    high = x.astype(BF16)
    return high, (x - high.astype(F32)).astype(BF16)


def dot(a, b):
    return jnp.dot(a, b, preferred_element_type=F32)


def dot3(a_high, a_low, b_high, b_low):
    return dot(a_high, b_high) + dot(a_low, b_high) + dot(a_high, b_low)


def transfer_kernel(
    frames,
    lengths_hbm,
    init_hbm,
    cols_ref,
    map_ref,
    weight_ref,
    mask_ref,
    mats_ref,
    pre_ref,
    e_ref,
    top_ref,
    th_ref,
    tl_ref,
    start_ref,
    g_scr,
    e_scr,
    t_scr,
    ah,
    al,
    bh,
    bl,
    lengths_ref,
    init_ref,
    sems,
):
    copies = [
        pltpu.make_async_copy(src, dst, sems.at[i])
        for i, (src, dst) in enumerate(
            (
                (lengths_hbm, lengths_ref),
                (init_hbm, init_ref),
            )
        )
    ]
    for copy in copies:
        copy.start()
    states = weight_ref.shape[0]
    half = frames // 2
    rows = states // 2
    blocks = half // SUB
    utt, slots = place(half)
    cols = cols_ref[...].T
    pick = (lax.broadcasted_iota(jnp.int32, (cols.shape[1], states), 0) == map_ref[...]).astype(F32).astype(BF16)
    p1 = cols.astype(BF16)
    rest = cols - p1.astype(F32)
    p2, p3 = halves(rest)
    depth = 256
    pieces = cols.shape[1] // depth

    def gather(*accs):
        for k in range(pieces):
            cut = slice(k * depth, (k + 1) * depth)
            pltpu.matmul_push_rhs(pick[cut, :], 0, k % 2)
            pltpu.matmul_acc_lhs(accs[k % 2], p1[:, cut], 0)
            pltpu.matmul_acc_lhs(accs[k % 2], p2[:, cut], None)
            pltpu.matmul_acc_lhs(accs[k % 2], p3[:, cut], None)
        g_scr[...] = pltpu.matmul_pop(accs[0]) + pltpu.matmul_pop(accs[1])

    pl.run_scoped(gather, pltpu.ACC(0)((frames, states), F32), pltpu.ACC(1)((frames, states), F32))
    g = g_scr[...]
    top = jnp.max(g, axis=1, keepdims=True)
    e = jnp.exp(g - top)
    e_scr[...] = e
    for i in range(2):
        for k in range(states // 128):
            e_ref[i, k] = e[i * half : (i + 1) * half, k * 128 : (k + 1) * 128]
        top_ref[i] = jnp.broadcast_to(top[i * half : (i + 1) * half], (half, 128))


    nb = mask_ref.shape[0]
    mask = mask_ref[...].astype(F32)
    width = states // nb
    lane = lax.broadcasted_iota(jnp.int32, (1, states), 1) // width
    for r in range(nb):
        row = jnp.zeros((1, states), F32)
        for c in range(nb):
            row = jnp.where(lane == c, mask[r : r + 1, c : c + 1], row)
        part = weight_ref[r * width : (r + 1) * width, :] * row
        t_scr[r * width : (r + 1) * width, :] = part / jnp.sum(part, axis=1, keepdims=True)
    th, tl = halves(t_scr[...])
    th_ref[...] = th
    tl_ref[...] = tl

    for copy in copies:
        copy.wait()
    alive = [lengths_ref[utt] - slot for slot in slots]
    eye = (
        lax.broadcasted_iota(jnp.int32, (states, states), 0) == lax.broadcasted_iota(jnp.int32, (states, states), 1)
    ).astype(F32)
    for k, (mh, ml) in enumerate(((ah, al), (bh, bl))):
        off = k * half
        h, l = halves(jnp.where(alive[k] > 0, t_scr[...] * e_scr[off : off + 1, :], eye))
        mh[0:states, :] = h
        ml[0:states, :] = l

    def body(a0, a1, b0, b1):
        accs = ((a0, a1), (b0, b1))
        mats = ((ah, al), (bh, bl))

        def issue_a(high_loaded):
            for m in range(2):
                sl = pl.ds(m * rows, rows)
                pltpu.matmul_acc_lhs(accs[0][m], ah[sl, :], high_loaded)
                pltpu.matmul_acc_lhs(accs[0][m], al[sl, :], None)
            for m in range(2):
                pltpu.matmul_push_rhs(tl_ref[...], 1, m)
            for m in range(2):
                pltpu.matmul_acc_lhs(accs[0][m], ah[pl.ds(m * rows, rows), :], 1)

        def issue_b():
            for m in range(2):
                pltpu.matmul_acc_lhs(accs[1][m], bh[pl.ds(m * rows, rows), :], None)
            for m in range(2):
                pltpu.matmul_push_rhs(th_ref[...], 0, m)
            for m in range(2):
                sl = pl.ds(m * rows, rows)
                pltpu.matmul_acc_lhs(accs[1][m], bh[sl, :], 0)
                pltpu.matmul_acc_lhs(accs[1][m], bl[sl, :], None)

        def post(k, s, r, peak, freeze):
            look, use = r % 4 == 1 + 2 * k, r % 4 == (2 + 2 * k) % 4
            mh, ml = mats[k]
            er = e_scr[pl.ds(s + k * half, 1), :]
            if use:
                er = er * (1.0 / jnp.max(peak.astype(F32), keepdims=True)[:, :1])
            live = s < alive[k]
            new = None
            for m in range(2):
                x = pltpu.matmul_pop(accs[k][m]) * er
                h, l = halves(x)
                sl = pl.ds(m * rows, rows)
                if freeze:
                    h = jnp.where(live, h, mh[sl, :])
                    l = jnp.where(live, l, ml[sl, :])
                mh[sl, :] = h
                ml[sl, :] = l
                if look:
                    y = jnp.max(h.reshape(rows // 16, 16, states), axis=0)
                    new = y if new is None else jnp.maximum(new, y)
            return new if look else peak

        def keep(j):
            for k in range(2):
                for i in range(2):
                    pre_ref[k, j, i] = mats[k][i][0:states, :]

        for m in range(2):
            pltpu.matmul_push_rhs(th_ref[...], 0, m)
        issue_a(0)
        one = jnp.ones((16, states), BF16)

        def step(s, r, peaks, freeze, last=False):
            pa, pb = peaks
            issue_b()
            pa = post(0, s, r, pa, freeze)
            if not last:
                issue_a(None)
            pb = post(1, s, r, pb, freeze)
            return pa, pb

        def eight(j, peaks, freeze):
            for r in range(1, SUB):
                peaks = step(j * SUB + r, r, peaks, freeze)
            keep(j)
            return step(j * SUB + SUB, SUB, peaks, freeze)

        def block(j, peaks):
            full = jnp.minimum(alive[0], alive[1]) > j * SUB + SUB
            return lax.cond(full, lambda p: eight(j, p, False), lambda p: eight(j, p, True), peaks)

        peaks = lax.fori_loop(0, blocks - 1, block, (one, one))
        for r in range(1, SUB):
            peaks = step((blocks - 1) * SUB + r, r, peaks, True, r == SUB - 1)
        keep(blocks - 1)
        start_ref[...] = jnp.broadcast_to(unit(init_ref[...]), start_ref.shape)
        for i, (mh, ml) in enumerate(mats):
            mats_ref[i] = mh[0:states, :].astype(F32) + ml[0:states, :].astype(F32)

    shape = (rows, states)
    pl.run_scoped(
        body,
        pltpu.ACC(0)(shape, F32),
        pltpu.ACC(1)(shape, F32),
        pltpu.ACC(0)(shape, F32),
        pltpu.ACC(1)(shape, F32),
    )


def vmem():
    return pl.BlockSpec(memory_space=pltpu.VMEM)


def hbm():
    return pl.BlockSpec(memory_space=pltpu.MemorySpace.HBM)


def pinned(x):
    return pltpu.with_memory_space_constraint(x, pltpu.MemorySpace.HBM)


def transfer(cols, columns_of, weight, mask, lengths, init):
    columns, frames = cols.shape
    states = weight.shape[0]
    blocks = frames // 2 // SUB
    out = jax.ShapeDtypeStruct
    return pl.pallas_call(
        functools.partial(transfer_kernel, frames),
        out_shape=(
            out((2, states, states), F32),
            out((2, blocks, 2, states, states), BF16),
            out((2, states // 128, frames // 2, 128), F32),
            out((2, frames // 2, 128), F32),
            out((states, states), BF16),
            out((states, states), BF16),
            out((8, states), F32),
        ),
        in_specs=[hbm()] * 2 + [vmem()] * 4,
        out_specs=[vmem()] * 7,
        scratch_shapes=[pltpu.VMEM((frames, states), F32)] * 2
        + [pltpu.VMEM((states, states), F32)]
        + [pltpu.VMEM((states, states), BF16)] * 4
        + [
            pltpu.SMEM(lengths.shape, jnp.int32),
            pltpu.VMEM((1, states), F32),
            pltpu.SemaphoreType.DMA((2,)),
        ],
        compiler_params=pltpu.CompilerParams(vmem_limit_bytes=6 << 20),
        name="transfer",
    )(*map(pinned, (lengths, init[None, :])), cols, columns_of, weight, mask)


def row_dot(v, matrix_high, matrix_low):
    n = v.shape[0]
    both = jnp.concatenate(halves(v), axis=0)
    x = dot(both, matrix_high)
    y = dot(both, matrix_low)
    return x[0:n] + x[n:] + y[0:n]


def unit(v):
    return v / jnp.sum(v, axis=1, keepdims=True)


def pass_on(v, matrix):
    return row_dot(v, *halves(matrix)) * (1.0 / jnp.sum(v, axis=1, keepdims=True))


def in_order(own_ref, other_ref, do):
    core = lax.axis_index("tm") % 2

    @pl.when(core == 0)
    def _():
        do(own_ref.at[0], other_ref.at[0], own_ref.at[1], other_ref.at[1])

    @pl.when(core == 1)
    def _():
        do(other_ref.at[0], own_ref.at[0], other_ref.at[1], own_ref.at[1])


def first_kernel(start_ref, own_ref, other_ref, v_ref):
    def do(*mats):
        v = start_ref[...]
        for m in mats:
            v = pass_on(v, m[...])
        v_ref[...] = v

    in_order(own_ref, other_ref, do)


def group_kernel(own_ref, other_ref, all_ref, mid_ref):
    def times(left, right):
        d = dot3(*halves(left), *halves(right))
        return d * (1.0 / jnp.max(d, keepdims=True)[:, :1])

    def do(*mats):
        mid_ref[...] = times(mats[0][...], mats[1][...])
        all_ref[...] = times(mid_ref[...], times(mats[2][...], mats[3][...]))

    in_order(own_ref, other_ref, do)

    @pl.when(lax.axis_index("tm") % 2 == 1)
    def _():
        mid_ref[...] = times(mid_ref[...], other_ref[1])


def hop_kernel(v_ref, m_ref, out_ref):
    out_ref[...] = pass_on(v_ref[...], m_ref[...])


def small(kernel, name, outs, *args):
    return pl.pallas_call(
        kernel,
        out_shape=tuple(jax.ShapeDtypeStruct(shape, F32) for shape in outs),
        in_specs=[vmem()] * len(args),
        out_specs=[vmem()] * len(outs),
        compiler_params=pltpu.CompilerParams(vmem_limit_bytes=4 << 20),
        name=name,
    )(*args)


def pack_kernel(x_hbm, map_hbm, weight_hbm, mask_hbm, out_ref, map_ref, weight_ref, mask_ref, x_ref, sems):
    groups = out_ref.shape[0]
    pairs = [(x_hbm.at[:, :, pl.ds(g * 256, 256)], x_ref.at[:, :, pl.ds(g * 256, 256)]) for g in range(groups)]
    pairs += [(map_hbm, map_ref), (weight_hbm, weight_ref), (mask_hbm, mask_ref)]
    copies = [pltpu.make_async_copy(src, dst, sems.at[i]) for i, (src, dst) in enumerate(pairs)]
    for copy in copies:
        copy.start()
    local = out_ref.shape[2]
    low = lax.broadcasted_iota(jnp.int32, (local, 128), 1) < 64
    for g in range(groups):
        copies[g].wait()
        for u in range(2):
            early = x_ref[u, :, g * 256 : g * 256 + 128]
            late = x_ref[u, :, g * 256 + 128 : g * 256 + 256]
            out_ref[g, 2 * u] = jnp.where(low, early, pltpu.roll(late, 64, 1))
            out_ref[g, 2 * u + 1] = jnp.where(low, pltpu.roll(early, 64, 1), late)
    for copy in copies[groups:]:
        copy.wait()


def pack(x, pdf_map, weight, mask, groups):
    local = x.shape[1]
    return pl.pallas_call(
        pack_kernel,
        out_shape=(
            jax.ShapeDtypeStruct((groups, 4, local, 128), F32),
            jax.ShapeDtypeStruct((1, pdf_map.shape[0]), jnp.int32),
            jax.ShapeDtypeStruct(weight.shape, F32),
            jax.ShapeDtypeStruct(mask.shape, jnp.int32),
        ),
        in_specs=[hbm()] * 4,
        out_specs=[vmem()] * 4,
        scratch_shapes=[pltpu.VMEM(x.shape, F32), pltpu.SemaphoreType.DMA((groups + 3,))],
        compiler_params=pltpu.CompilerParams(vmem_limit_bytes=4 << 20),
        name="pack",
    )(pinned(x), pinned(pdf_map[None, :]), pinned(weight), pinned(mask))


def slot_kernel(sent, lengths_hbm, *refs):
    start_ref, *v_refs = refs[:-11]
    other_ref, mid_ref, pre_ref, e_ref, top_ref, th_ref, tl_ref, out_ref, *scratch = refs[len(v_refs) + 1 :]
    alpha_scr, lengths_ref, sem = scratch
    copy = pltpu.make_async_copy(lengths_hbm, lengths_ref, sem)
    copy.start()
    states = th_ref.shape[0]
    half = top_ref.shape[1]
    blocks = half // SUB
    index = lax.axis_index("tm")
    utt, slots = place(half)
    slot = 1 - utt if sent else utt

    v = start_ref[...]
    for g, ref in enumerate(v_refs):
        v = jnp.where(index // 4 == g + 1, ref[...], v)
    before = jnp.where(index % 2 == 1, pass_on(v, other_ref[0]), v)
    v = jnp.where(slot == 1, pass_on(v, mid_ref[...]), before)
    rows = [v[0:1]]
    for j in range(blocks - 1):
        rows.append(row_dot(v, pre_ref[slot, j, 0], pre_ref[slot, j, 1])[0:1])
    x = jnp.concatenate(rows, axis=0)
    total = jnp.sum(x, axis=1, keepdims=True)
    th, tl = th_ref[...], tl_ref[...]
    lane = lax.broadcasted_iota(jnp.int32, (blocks, 128), 1)
    sub = lax.broadcasted_iota(jnp.int32, (blocks, 128), 0)
    gains = jnp.zeros((blocks, 128), F32)
    copy.wait()
    left = lengths_ref[utt] - jnp.where(slot == 0, slots[0], slots[1])
    tiles = range(states // 128)
    for r in range(SUB):
        every = pl.ds(r, blocks, stride=SUB)
        factor = jnp.concatenate([e_ref[slot, k, every, :] for k in tiles], axis=1) * (1.0 / total)
        x = row_dot(x, th, tl) * factor
        total = jnp.sum(x, axis=1, keepdims=True)
        alpha = x * (1.0 / total)
        for k in tiles:
            alpha_scr[k, every, :] = alpha[:, k * 128 : (k + 1) * 128]
        live = sub * SUB + r < left
        gain = jnp.where(live, jnp.log(total) + top_ref[slot, every, :], 0.0)
        gains = jnp.where(lane % SUB == r, gain, gains)
    v = unit(v)
    frame = lax.broadcasted_iota(jnp.int32, (half, 128), 0)
    end = pl.ds(jnp.clip(left - 1, 0, half - 1), 1)
    for k in tiles:
        cut = slice(k * 128, (k + 1) * 128)
        final = jnp.where(left > 0, alpha_scr[k, end, :], v[0:1, cut])
        out_ref[0:half, cut] = jnp.log(jnp.where(frame < left, alpha_scr[k], final))
    line = jnp.sum(jnp.where(lane // SUB == sub, gains, 0.0), axis=0, keepdims=True)
    out_ref[half : half + 8, :] = jnp.concatenate([jnp.broadcast_to(line, (8, 128))] * (states // 128), axis=1)


def slot_pass(sent, lengths, vs, other, mid, pre, e, top, th, tl):
    half, states = top.shape[1], th.shape[0]
    return pl.pallas_call(
        functools.partial(slot_kernel, sent),
        out_shape=jax.ShapeDtypeStruct((half + 8, states), F32),
        in_specs=[hbm()] + [vmem()] * (len(vs) + 7),
        out_specs=vmem(),
        scratch_shapes=[
            pltpu.VMEM((states // 128, half, 128), F32),
            pltpu.SMEM(lengths.shape, jnp.int32),
            pltpu.SemaphoreType.DMA,
        ],
        compiler_params=pltpu.CompilerParams(vmem_limit_bytes=6 << 20),
        name="sent" if sent else "kept",
    )(pinned(lengths), *vs, other, mid, pre, e, top, th, tl)


def join_kernel(kept_ref, got_ref, log_ref, gain_ref):
    half = log_ref.shape[1]
    utt = (lax.axis_index("tm") // 2) % 2
    log_ref[utt] = kept_ref[0:half, :]
    log_ref[1 - utt] = got_ref[0:half, :]
    own = kept_ref[half : half + 1, 0:half]
    got = got_ref[half : half + 1, 0:half]
    gain_ref[0:1, :] = jnp.where(utt == 0, own, got)
    gain_ref[1:2, :] = jnp.where(utt == 0, got, own)


def shards(size, loglik, trans_weight, block_mask, init_weight, lengths, pdf_map):
    local = loglik.shape[2]
    groups = size // 4
    x, *tables = pack(jnp.transpose(loglik, (0, 2, 1)), pdf_map, trans_weight, block_mask, groups)
    frames = x.shape[3]
    x = x.reshape(size, local, frames)
    cols = lax.all_to_all(x, "tm", 0, 0, tiled=True).reshape(size * local, frames)
    own, pre, e, top, th, tl, start = transfer(cols, *tables, lengths, init_weight)
    other = lax.ppermute(own, "tm", [(i, i ^ 1) for i in range(size)])
    (v,) = small(first_kernel, "first", [start.shape], start, own, other)
    square = own.shape[1:]
    whole, mid = small(group_kernel, "group", [square, square], own, other)
    vs = [start]
    for g in range(1, groups):
        pairs = [(i, partner(i, g, groups)) for i in range(size)]
        vs.append(lax.ppermute(v, "tm", pairs))
        if g < groups - 1:
            (v,) = small(hop_kernel, "hop", [v.shape], vs[-1], whole)
    given = (lengths, vs, other, mid, pre, e, top, th, tl)
    sent = slot_pass(True, *given)
    got = lax.ppermute(sent, "tm", [(i, i ^ 2) for i in range(size)])
    kept = slot_pass(False, *given)
    half, states = kept.shape[0] - 8, kept.shape[1]
    return small(join_kernel, "join", [(2, half, states), (2, half)], kept, got)


def partner(index, turn, groups):
    group = index // 4
    other = group ^ 1 if turn % 2 else (group - 1 if group % 2 == 0 else group + 1)
    if 0 <= other < groups:
        return (4 * other + index % 4) ^ 1
    return index ^ 3


def solution(mesh):
    return jax.shard_map(
        functools.partial(shards, mesh.shape["tm"]),
        mesh=mesh,
        in_specs=(P("groups", None, "tm"), P(), P(), P(), P("groups"), P()),
        out_specs=(P("groups", "tm", None), P("groups", "tm")),
        check_vma=False,
    )
```

```python
import functools
import jax
import jax.numpy as jnp
from jax import lax
from jax.experimental import pallas as pl
from jax.experimental.pallas import tpu as pltpu
from jax.sharding import PartitionSpec as P

F32 = jnp.float32
BF16 = jnp.bfloat16
SUB = 8


def place(half):
    index = lax.axis_index("tm")
    first = (index // 4) * 4 * half + (index % 2) * half
    return (index // 2) % 2, (first, first + 2 * half)


def frames_of(lengths_ref, utt):
    row = lengths_ref[...].astype(F32)
    here = lax.broadcasted_iota(jnp.int32, row.shape, 1) == utt
    return jnp.sum(jnp.where(here, row, 0.0)).astype(jnp.int32)


def halves(x):
    high = x.astype(BF16)
    return high, (x - high.astype(F32)).astype(BF16)


def dot(a, b):
    return jnp.dot(a, b, preferred_element_type=F32)


def dot3(a_high, a_low, b_high, b_low):
    return dot(a_high, b_high) + dot(a_low, b_high) + dot(a_high, b_low)


def transfer_kernel(
    frames,
    cols_ref,
    map_ref,
    weight_ref,
    mask_ref,
    lengths_ref,
    init_ref,
    mats_ref,
    pre_ref,
    e_ref,
    top_ref,
    th_ref,
    tl_ref,
    start_ref,
    g_scr,
    e_scr,
    t_scr,
    ah,
    al,
    bh,
    bl,
):
    states = weight_ref.shape[0]
    half = frames // 2
    rows = states // 2
    blocks = half // SUB
    utt, slots = place(half)
    cols = cols_ref[...].T
    pick = (lax.broadcasted_iota(jnp.int32, (cols.shape[1], states), 0) == map_ref[...]).astype(F32).astype(BF16)
    p1 = cols.astype(BF16)
    rest = cols - p1.astype(F32)
    p2, p3 = halves(rest)
    depth = 256
    pieces = cols.shape[1] // depth

    def gather(*accs):
        for k in range(pieces):
            cut = slice(k * depth, (k + 1) * depth)
            pltpu.matmul_push_rhs(pick[cut, :], 0, k % 2)
            pltpu.matmul_acc_lhs(accs[k % 2], p1[:, cut], 0)
            pltpu.matmul_acc_lhs(accs[k % 2], p2[:, cut], None)
            pltpu.matmul_acc_lhs(accs[k % 2], p3[:, cut], None)
        g_scr[...] = pltpu.matmul_pop(accs[0]) + pltpu.matmul_pop(accs[1])

    pl.run_scoped(gather, pltpu.ACC(0)((frames, states), F32), pltpu.ACC(1)((frames, states), F32))
    g = g_scr[...]
    top = jnp.max(g, axis=1, keepdims=True)
    e = jnp.exp(g - top)
    e_scr[...] = e
    for i in range(2):
        for k in range(states // 128):
            e_ref[i, k] = e[i * half : (i + 1) * half, k * 128 : (k + 1) * 128]
        top_ref[i] = jnp.broadcast_to(top[i * half : (i + 1) * half], (half, 128))


    nb = mask_ref.shape[0]
    mask = mask_ref[...].astype(F32)
    width = states // nb
    lane = lax.broadcasted_iota(jnp.int32, (1, states), 1) // width
    for r in range(nb):
        row = jnp.zeros((1, states), F32)
        for c in range(nb):
            row = jnp.where(lane == c, mask[r : r + 1, c : c + 1], row)
        part = weight_ref[r * width : (r + 1) * width, :] * row
        t_scr[r * width : (r + 1) * width, :] = part / jnp.sum(part, axis=1, keepdims=True)
    th, tl = halves(t_scr[...])
    th_ref[...] = th
    tl_ref[...] = tl

    alive = [frames_of(lengths_ref, utt) - slot for slot in slots]
    eye = (
        lax.broadcasted_iota(jnp.int32, (states, states), 0) == lax.broadcasted_iota(jnp.int32, (states, states), 1)
    ).astype(F32)
    for k, (mh, ml) in enumerate(((ah, al), (bh, bl))):
        off = k * half
        h, l = halves(jnp.where(alive[k] > 0, t_scr[...] * e_scr[off : off + 1, :], eye))
        mh[0:states, :] = h
        ml[0:states, :] = l

    def body(a0, a1, b0, b1):
        accs = ((a0, a1), (b0, b1))
        mats = ((ah, al), (bh, bl))

        def issue_a(high_loaded):
            for m in range(2):
                sl = pl.ds(m * rows, rows)
                pltpu.matmul_acc_lhs(accs[0][m], ah[sl, :], high_loaded)
                pltpu.matmul_acc_lhs(accs[0][m], al[sl, :], None)
            for m in range(2):
                pltpu.matmul_push_rhs(tl_ref[...], 1, m)
            for m in range(2):
                pltpu.matmul_acc_lhs(accs[0][m], ah[pl.ds(m * rows, rows), :], 1)

        def issue_b():
            for m in range(2):
                pltpu.matmul_acc_lhs(accs[1][m], bh[pl.ds(m * rows, rows), :], None)
            for m in range(2):
                pltpu.matmul_push_rhs(th_ref[...], 0, m)
            for m in range(2):
                sl = pl.ds(m * rows, rows)
                pltpu.matmul_acc_lhs(accs[1][m], bh[sl, :], 0)
                pltpu.matmul_acc_lhs(accs[1][m], bl[sl, :], None)

        def post(k, j, r, peak, freeze):
            s = j * SUB + r
            look, use = r % 4 == 1 + 2 * k, r % 4 == (2 + 2 * k) % 4
            mh, ml = mats[k]
            er = e_scr[pl.ds(s + k * half, 1), :]
            if use:
                er = er * (1.0 / jnp.max(peak.astype(F32), keepdims=True)[:, :1])
            live = s < alive[k]
            new = None
            for m in range(2):
                x = pltpu.matmul_pop(accs[k][m]) * er
                h, l = halves(x)
                sl = pl.ds(m * rows, rows)
                if freeze:
                    h = jnp.where(live, h, mh[sl, :])
                    l = jnp.where(live, l, ml[sl, :])
                mh[sl, :] = h
                ml[sl, :] = l
                if r == SUB - 1:
                    pre_ref[k, j, 0, sl, :] = h
                    pre_ref[k, j, 1, sl, :] = l
                if look:
                    y = jnp.max(h.reshape(rows // 16, 16, states), axis=0)
                    new = y if new is None else jnp.maximum(new, y)
            return new if look else peak

        for m in range(2):
            pltpu.matmul_push_rhs(th_ref[...], 0, m)
        issue_a(0)
        one = jnp.ones((16, states), BF16)

        def step(j, r, peaks, freeze, last=False):
            pa, pb = peaks
            issue_b()
            pa = post(0, j, r, pa, freeze)
            if not last:
                issue_a(None)
            pb = post(1, j, r, pb, freeze)
            return pa, pb

        def eight(j, peaks, freeze):
            for r in range(1, SUB):
                peaks = step(j, r, peaks, freeze)
            return step(j, SUB, peaks, freeze)

        def block(j, peaks):
            full = jnp.minimum(alive[0], alive[1]) > j * SUB + SUB
            return lax.cond(full, lambda p: eight(j, p, False), lambda p: eight(j, p, True), peaks)

        peaks = lax.fori_loop(0, blocks - 1, block, (one, one))
        for r in range(1, SUB):
            peaks = step(blocks - 1, r, peaks, True, r == SUB - 1)
        start_ref[...] = jnp.broadcast_to(unit(init_ref[...]), start_ref.shape)
        for i, (mh, ml) in enumerate(mats):
            mats_ref[i] = mh[0:states, :].astype(F32) + ml[0:states, :].astype(F32)

    shape = (rows, states)
    pl.run_scoped(
        body,
        pltpu.ACC(0)(shape, F32),
        pltpu.ACC(1)(shape, F32),
        pltpu.ACC(0)(shape, F32),
        pltpu.ACC(1)(shape, F32),
    )


def vmem():
    return pl.BlockSpec(memory_space=pltpu.VMEM)


def hbm():
    return pl.BlockSpec(memory_space=pltpu.MemorySpace.HBM)


def pinned(x):
    return pltpu.with_memory_space_constraint(x, pltpu.MemorySpace.HBM)


def transfer(cols, columns_of, weight, mask, lengths, init):
    columns, frames = cols.shape
    states = weight.shape[0]
    blocks = frames // 2 // SUB
    out = jax.ShapeDtypeStruct
    return pl.pallas_call(
        functools.partial(transfer_kernel, frames),
        out_shape=(
            out((2, states, states), F32),
            out((2, blocks, 2, states, states), BF16),
            out((2, states // 128, frames // 2, 128), F32),
            out((2, frames // 2, 128), F32),
            out((states, states), BF16),
            out((states, states), BF16),
            out((8, states), F32),
        ),
        in_specs=[vmem()] * 6,
        out_specs=[vmem()] * 7,
        scratch_shapes=[pltpu.VMEM((frames, states), F32)] * 2
        + [pltpu.VMEM((states, states), F32)]
        + [pltpu.VMEM((states, states), BF16)] * 4,
        compiler_params=pltpu.CompilerParams(vmem_limit_bytes=6 << 20),
        name="transfer",
    )(cols, columns_of, weight, mask, lengths, init)


def row_dot(v, matrix_high, matrix_low):
    n = v.shape[0]
    both = jnp.concatenate(halves(v), axis=0)
    x = dot(both, matrix_high)
    y = dot(both, matrix_low)
    return x[0:n] + x[n:] + y[0:n]


def unit(v):
    return v / jnp.sum(v, axis=1, keepdims=True)


def pass_on(v, matrix):
    return row_dot(v, *halves(matrix)) * (1.0 / jnp.sum(v, axis=1, keepdims=True))


def in_order(own_ref, other_ref, do):
    core = lax.axis_index("tm") % 2

    @pl.when(core == 0)
    def _():
        do(own_ref.at[0], other_ref.at[0], own_ref.at[1], other_ref.at[1])

    @pl.when(core == 1)
    def _():
        do(other_ref.at[0], own_ref.at[0], other_ref.at[1], own_ref.at[1])


def first_kernel(start_ref, own_ref, other_ref, v_ref):
    def do(*mats):
        v = start_ref[...]
        for m in mats:
            v = pass_on(v, m[...])
        v_ref[...] = v

    in_order(own_ref, other_ref, do)


def group_kernel(own_ref, other_ref, all_ref, mid_ref):
    def times(left, right):
        d = dot3(*halves(left), *halves(right))
        return d * (1.0 / jnp.max(d, keepdims=True)[:, :1])

    def do(*mats):
        mid_ref[...] = times(mats[0][...], mats[1][...])
        all_ref[...] = times(mid_ref[...], times(mats[2][...], mats[3][...]))

    in_order(own_ref, other_ref, do)

    @pl.when(lax.axis_index("tm") % 2 == 1)
    def _():
        mid_ref[...] = times(mid_ref[...], other_ref[1])


def hop_kernel(v_ref, m_ref, out_ref):
    out_ref[...] = pass_on(v_ref[...], m_ref[...])


def small(kernel, name, outs, *args):
    return pl.pallas_call(
        kernel,
        out_shape=tuple(jax.ShapeDtypeStruct(shape, F32) for shape in outs),
        in_specs=[vmem()] * len(args),
        out_specs=[vmem()] * len(outs),
        compiler_params=pltpu.CompilerParams(vmem_limit_bytes=4 << 20),
        name=name,
    )(*args)


def pack_kernel(tables, x_hbm, *refs):
    table_hbms, out_ref, table_refs, (x_ref, sems) = refs[:tables], refs[tables], refs[tables + 1 : -2], refs[-2:]
    groups = out_ref.shape[0]
    pairs = [(x_hbm.at[:, :, pl.ds(g * 256, 256)], x_ref.at[:, :, pl.ds(g * 256, 256)]) for g in range(groups)]
    pairs += zip(table_hbms, table_refs)
    copies = [pltpu.make_async_copy(src, dst, sems.at[i]) for i, (src, dst) in enumerate(pairs)]
    for copy in copies:
        copy.start()
    local = out_ref.shape[2]
    low = lax.broadcasted_iota(jnp.int32, (local, 128), 1) < 64
    for g in range(groups):
        copies[g].wait()
        for u in range(2):
            early = x_ref[u, :, g * 256 : g * 256 + 128]
            late = x_ref[u, :, g * 256 + 128 : g * 256 + 256]
            out_ref[g, 2 * u] = jnp.where(low, early, pltpu.roll(late, 64, 1))
            out_ref[g, 2 * u + 1] = jnp.where(low, pltpu.roll(early, 64, 1), late)
    for copy in copies[groups:]:
        copy.wait()


def pack(x, groups, *tables):
    local = x.shape[1]
    n = len(tables)
    packed = jax.ShapeDtypeStruct((groups, 4, local, 128), F32)
    return pl.pallas_call(
        functools.partial(pack_kernel, n),
        out_shape=(packed, *(jax.ShapeDtypeStruct(t.shape, t.dtype) for t in tables)),
        in_specs=[hbm()] * (n + 1),
        out_specs=[vmem()] * (n + 1),
        scratch_shapes=[pltpu.VMEM(x.shape, F32), pltpu.SemaphoreType.DMA((groups + n,))],
        compiler_params=pltpu.CompilerParams(vmem_limit_bytes=4 << 20),
        name="pack",
    )(*map(pinned, (x, *tables)))


def slot_kernel(sent, lengths_ref, *refs):
    start_ref, *v_refs = refs[:-9]
    other_ref, mid_ref, pre_ref, e_ref, top_ref, th_ref, tl_ref, out_ref, alpha_scr = refs[len(v_refs) + 1 :]
    states = th_ref.shape[0]
    half = top_ref.shape[1]
    blocks = half // SUB
    index = lax.axis_index("tm")
    utt, slots = place(half)
    slot = 1 - utt if sent else utt

    v = start_ref[...]
    for g, ref in enumerate(v_refs):
        v = jnp.where(index // 4 == g + 1, ref[...], v)
    before = jnp.where(index % 2 == 1, pass_on(v, other_ref[0]), v)
    v = jnp.where(slot == 1, pass_on(v, mid_ref[...]), before)
    rows = [v[0:1]]
    for j in range(blocks - 1):
        rows.append(row_dot(v, pre_ref[slot, j, 0], pre_ref[slot, j, 1])[0:1])
    x = jnp.concatenate(rows, axis=0)
    total = jnp.sum(x, axis=1, keepdims=True)
    th, tl = th_ref[...], tl_ref[...]
    lane = lax.broadcasted_iota(jnp.int32, (blocks, 128), 1)
    sub = lax.broadcasted_iota(jnp.int32, (blocks, 128), 0)
    gains = jnp.zeros((blocks, 128), F32)
    left = frames_of(lengths_ref, utt) - jnp.where(slot == 0, slots[0], slots[1])
    tiles = range(states // 128)
    for r in range(SUB):
        every = pl.ds(r, blocks, stride=SUB)
        factor = jnp.concatenate([e_ref[slot, k, every, :] for k in tiles], axis=1) * (1.0 / total)
        x = row_dot(x, th, tl) * factor
        total = jnp.sum(x, axis=1, keepdims=True)
        alpha = x * (1.0 / total)
        for k in tiles:
            alpha_scr[k, every, :] = alpha[:, k * 128 : (k + 1) * 128]
        live = sub * SUB + r < left
        gain = jnp.where(live, jnp.log(total) + top_ref[slot, every, :], 0.0)
        gains = jnp.where(lane % SUB == r, gain, gains)
    v = unit(v)
    frame = lax.broadcasted_iota(jnp.int32, (half, 128), 0)
    end = pl.ds(jnp.clip(left - 1, 0, half - 1), 1)
    for k in tiles:
        cut = slice(k * 128, (k + 1) * 128)
        final = jnp.where(left > 0, alpha_scr[k, end, :], v[0:1, cut])
        out_ref[0:half, cut] = jnp.log(jnp.where(frame < left, alpha_scr[k], final))
    line = jnp.sum(jnp.where(lane // SUB == sub, gains, 0.0), axis=0, keepdims=True)
    out_ref[half : half + 8, :] = jnp.concatenate([jnp.broadcast_to(line, (8, 128))] * (states // 128), axis=1)


def slot_pass(sent, lengths, vs, other, mid, pre, e, top, th, tl):
    half, states = top.shape[1], th.shape[0]
    return pl.pallas_call(
        functools.partial(slot_kernel, sent),
        out_shape=jax.ShapeDtypeStruct((half + 8, states), F32),
        in_specs=[vmem()] * (len(vs) + 8),
        out_specs=vmem(),
        scratch_shapes=[pltpu.VMEM((states // 128, half, 128), F32)],
        compiler_params=pltpu.CompilerParams(vmem_limit_bytes=6 << 20),
        name="sent" if sent else "kept",
    )(lengths, *vs, other, mid, pre, e, top, th, tl)


def join_kernel(kept_ref, got_ref, log_ref, gain_ref):
    half = log_ref.shape[1]
    utt = (lax.axis_index("tm") // 2) % 2
    log_ref[utt] = kept_ref[0:half, :]
    log_ref[1 - utt] = got_ref[0:half, :]
    own = kept_ref[half : half + 1, 0:half]
    got = got_ref[half : half + 1, 0:half]
    gain_ref[0:1, :] = jnp.where(utt == 0, own, got)
    gain_ref[1:2, :] = jnp.where(utt == 0, got, own)


def shards(size, loglik, trans_weight, block_mask, init_weight, lengths, pdf_map):
    local = loglik.shape[2]
    groups = size // 4
    tables = (pdf_map[None, :], trans_weight, block_mask, lengths[None, :], init_weight[None, :])
    x, *tables = pack(jnp.transpose(loglik, (0, 2, 1)), groups, *tables)
    frames = x.shape[3]
    x = x.reshape(size, local, frames)
    cols = lax.all_to_all(x, "tm", 0, 0, tiled=True).reshape(size * local, frames)
    own, pre, e, top, th, tl, start = transfer(cols, *tables)
    other = lax.ppermute(own, "tm", [(i, i ^ 1) for i in range(size)])
    (v,) = small(first_kernel, "first", [start.shape], start, own, other)
    square = own.shape[1:]
    whole, mid = small(group_kernel, "group", [square, square], own, other)
    vs = [start]
    for g in range(1, groups):
        pairs = [(i, partner(i, g, groups)) for i in range(size)]
        vs.append(lax.ppermute(v, "tm", pairs))
        if g < groups - 1:
            (v,) = small(hop_kernel, "hop", [v.shape], vs[-1], whole)
    given = (tables[3], vs, other, mid, pre, e, top, th, tl)
    sent = slot_pass(True, *given)
    got = lax.ppermute(sent, "tm", [(i, i ^ 2) for i in range(size)])
    kept = slot_pass(False, *given)
    half, states = kept.shape[0] - 8, kept.shape[1]
    return small(join_kernel, "join", [(2, half, states), (2, half)], kept, got)


def partner(index, turn, groups):
    group = index // 4
    other = group ^ 1 if turn % 2 else (group - 1 if group % 2 == 0 else group + 1)
    if 0 <= other < groups:
        return (4 * other + index % 4) ^ 1
    return index ^ 3


def solution(mesh):
    return jax.shard_map(
        functools.partial(shards, mesh.shape["tm"]),
        mesh=mesh,
        in_specs=(P("groups", None, "tm"), P(), P(), P(), P("groups"), P()),
        out_specs=(P("groups", "tm", None), P("groups", "tm")),
        check_vma=False,
    )
```

```python
import functools
import jax
import jax.numpy as jnp
from jax import lax
from jax.experimental import pallas as pl
from jax.experimental.pallas import tpu as pltpu
from jax.sharding import PartitionSpec as P

F32 = jnp.float32
BF16 = jnp.bfloat16
SUB = 8


def place(half):
    index = lax.axis_index("tm")
    first = (index // 4) * 4 * half + (index % 2) * half
    return (index // 2) % 2, (first, first + 2 * half)


def frames_of(lengths_ref, utt):
    row = lengths_ref[...].astype(F32)
    here = lax.broadcasted_iota(jnp.int32, row.shape, 1) == utt
    return jnp.sum(jnp.where(here, row, 0.0)).astype(jnp.int32)


def halves(x):
    high = x.astype(BF16)
    return high, (x - high.astype(F32)).astype(BF16)


def dot(a, b):
    return jnp.dot(a, b, preferred_element_type=F32)


def dot3(a_high, a_low, b_high, b_low):
    return dot(a_high, b_high) + dot(a_low, b_high) + dot(a_high, b_low)


def transfer_kernel(
    frames,
    cols_ref,
    map_ref,
    weight_ref,
    mask_ref,
    lengths_ref,
    init_ref,
    mats_ref,
    pre_ref,
    e_ref,
    top_ref,
    th_ref,
    tl_ref,
    start_ref,
    g_scr,
    e_scr,
    t_scr,
    ah,
    al,
    bh,
    bl,
):
    states = weight_ref.shape[0]
    half = frames // 2
    rows = states // 2
    blocks = half // SUB
    utt, slots = place(half)
    cols = cols_ref[...].T
    pick = (lax.broadcasted_iota(jnp.int32, (cols.shape[1], states), 0) == map_ref[...]).astype(F32).astype(BF16)
    p1 = cols.astype(BF16)
    rest = cols - p1.astype(F32)
    p2, p3 = halves(rest)
    depth = 256
    pieces = cols.shape[1] // depth

    def gather(*accs):
        for k in range(pieces):
            cut = slice(k * depth, (k + 1) * depth)
            pltpu.matmul_push_rhs(pick[cut, :], 0, k % 2)
            pltpu.matmul_acc_lhs(accs[k % 2], p1[:, cut], 0)
            pltpu.matmul_acc_lhs(accs[k % 2], p2[:, cut], None)
            pltpu.matmul_acc_lhs(accs[k % 2], p3[:, cut], None)
        g_scr[...] = pltpu.matmul_pop(accs[0]) + pltpu.matmul_pop(accs[1])

    pl.run_scoped(gather, pltpu.ACC(0)((frames, states), F32), pltpu.ACC(1)((frames, states), F32))
    g = g_scr[...]
    top = jnp.max(g, axis=1, keepdims=True)
    e = jnp.exp(g - top)
    e_scr[...] = e
    for i in range(2):
        for k in range(states // 128):
            e_ref[i, k] = e[i * half : (i + 1) * half, k * 128 : (k + 1) * 128]
        top_ref[i] = jnp.broadcast_to(top[i * half : (i + 1) * half], (half, 128))


    nb = mask_ref.shape[0]
    mask = mask_ref[...].astype(F32)
    width = states // nb
    lane = lax.broadcasted_iota(jnp.int32, (1, states), 1) // width
    for r in range(nb):
        row = jnp.zeros((1, states), F32)
        for c in range(nb):
            row = jnp.where(lane == c, mask[r : r + 1, c : c + 1], row)
        part = weight_ref[r * width : (r + 1) * width, :] * row
        t_scr[r * width : (r + 1) * width, :] = part / jnp.sum(part, axis=1, keepdims=True)
    th, tl = halves(t_scr[...])
    th_ref[...] = th
    tl_ref[...] = tl

    alive = [frames_of(lengths_ref, utt) - slot for slot in slots]
    eye = (
        lax.broadcasted_iota(jnp.int32, (states, states), 0) == lax.broadcasted_iota(jnp.int32, (states, states), 1)
    ).astype(F32)
    for k, (mh, ml) in enumerate(((ah, al), (bh, bl))):
        off = k * half
        h, l = halves(jnp.where(alive[k] > 0, t_scr[...] * e_scr[off : off + 1, :], eye))
        mh[0:states, :] = h
        ml[0:states, :] = l

    def body(a0, a1, b0, b1):
        accs = ((a0, a1), (b0, b1))
        mats = ((ah, al), (bh, bl))

        def issue_a(high_loaded):
            for m in range(2):
                sl = pl.ds(m * rows, rows)
                pltpu.matmul_acc_lhs(accs[0][m], ah[sl, :], high_loaded)
                pltpu.matmul_acc_lhs(accs[0][m], al[sl, :], None)
            for m in range(2):
                pltpu.matmul_push_rhs(tl_ref[...], 1, m)
            for m in range(2):
                pltpu.matmul_acc_lhs(accs[0][m], ah[pl.ds(m * rows, rows), :], 1)

        def issue_b():
            for m in range(2):
                pltpu.matmul_acc_lhs(accs[1][m], bh[pl.ds(m * rows, rows), :], None)
            for m in range(2):
                pltpu.matmul_push_rhs(th_ref[...], 0, m)
            for m in range(2):
                sl = pl.ds(m * rows, rows)
                pltpu.matmul_acc_lhs(accs[1][m], bh[sl, :], 0)
                pltpu.matmul_acc_lhs(accs[1][m], bl[sl, :], None)

        def post(k, j, r, peak, freeze):
            s = j * SUB + r
            look, use = r % 4 == 1 + 2 * k, r % 4 == (2 + 2 * k) % 4
            mh, ml = mats[k]
            er = e_scr[pl.ds(s + k * half, 1), :]
            if use:
                er = er * (1.0 / jnp.max(peak.astype(F32), keepdims=True)[:, :1])
            live = s < alive[k]
            new = None
            for m in range(2):
                x = pltpu.matmul_pop(accs[k][m]) * er
                h, l = halves(x)
                sl = pl.ds(m * rows, rows)
                if freeze:
                    h = jnp.where(live, h, mh[sl, :])
                    l = jnp.where(live, l, ml[sl, :])
                mh[sl, :] = h
                ml[sl, :] = l
                if r == SUB - 1:
                    pre_ref[k, j, 0, sl, :] = h
                    pre_ref[k, j, 1, sl, :] = l
                if look:
                    y = jnp.max(h.reshape(rows // 16, 16, states), axis=0)
                    new = y if new is None else jnp.maximum(new, y)
            return new if look else peak

        for m in range(2):
            pltpu.matmul_push_rhs(th_ref[...], 0, m)
        issue_a(0)
        one = jnp.ones((16, states), BF16)

        def step(j, r, peaks, freeze, last=False):
            pa, pb = peaks
            issue_b()
            pa = post(0, j, r, pa, freeze)
            if not last:
                issue_a(None)
            pb = post(1, j, r, pb, freeze)
            return pa, pb

        def eight(j, peaks, freeze):
            for r in range(1, SUB):
                peaks = step(j, r, peaks, freeze)
            return step(j, SUB, peaks, freeze)

        def block(j, peaks):
            full = jnp.minimum(alive[0], alive[1]) > j * SUB + SUB
            return lax.cond(full, lambda p: eight(j, p, False), lambda p: eight(j, p, True), peaks)

        peaks = lax.fori_loop(0, blocks - 1, block, (one, one))
        def tail(peaks, freeze):
            for r in range(1, SUB):
                peaks = step(blocks - 1, r, peaks, freeze, r == SUB - 1)
            return peaks

        full = jnp.minimum(alive[0], alive[1]) >= half
        lax.cond(full, lambda p: tail(p, False), lambda p: tail(p, True), peaks)
        start_ref[...] = jnp.broadcast_to(unit(init_ref[...]), start_ref.shape)
        for i, (mh, ml) in enumerate(mats):
            mats_ref[i] = mh[0:states, :].astype(F32) + ml[0:states, :].astype(F32)

    shape = (rows, states)
    pl.run_scoped(
        body,
        pltpu.ACC(0)(shape, F32),
        pltpu.ACC(1)(shape, F32),
        pltpu.ACC(0)(shape, F32),
        pltpu.ACC(1)(shape, F32),
    )


def vmem():
    return pl.BlockSpec(memory_space=pltpu.VMEM)


def hbm():
    return pl.BlockSpec(memory_space=pltpu.MemorySpace.HBM)


def pinned(x):
    return pltpu.with_memory_space_constraint(x, pltpu.MemorySpace.HBM)


def transfer(cols, columns_of, weight, mask, lengths, init):
    columns, frames = cols.shape
    states = weight.shape[0]
    blocks = frames // 2 // SUB
    out = jax.ShapeDtypeStruct
    return pl.pallas_call(
        functools.partial(transfer_kernel, frames),
        out_shape=(
            out((2, states, states), F32),
            out((2, blocks, 2, states, states), BF16),
            out((2, states // 128, frames // 2, 128), F32),
            out((2, frames // 2, 128), F32),
            out((states, states), BF16),
            out((states, states), BF16),
            out((8, states), F32),
        ),
        in_specs=[vmem()] * 6,
        out_specs=[vmem()] * 7,
        scratch_shapes=[pltpu.VMEM((frames, states), F32)] * 2
        + [pltpu.VMEM((states, states), F32)]
        + [pltpu.VMEM((states, states), BF16)] * 4,
        compiler_params=pltpu.CompilerParams(vmem_limit_bytes=6 << 20),
        name="transfer",
    )(cols, columns_of, weight, mask, lengths, init)


def row_dot(v, matrix_high, matrix_low):
    n = v.shape[0]
    both = jnp.concatenate(halves(v), axis=0)
    x = dot(both, matrix_high)
    y = dot(both, matrix_low)
    return x[0:n] + x[n:] + y[0:n]


def unit(v):
    return v / jnp.sum(v, axis=1, keepdims=True)


def pass_on(v, matrix):
    return row_dot(v, *halves(matrix)) * (1.0 / jnp.sum(v, axis=1, keepdims=True))


def in_order(own_ref, other_ref, do):
    core = lax.axis_index("tm") % 2

    @pl.when(core == 0)
    def _():
        do(own_ref.at[0], other_ref.at[0], own_ref.at[1], other_ref.at[1])

    @pl.when(core == 1)
    def _():
        do(other_ref.at[0], own_ref.at[0], other_ref.at[1], own_ref.at[1])


def first_kernel(start_ref, own_ref, other_ref, v_ref):
    def do(*mats):
        v = start_ref[...]
        for m in mats:
            v = pass_on(v, m[...])
        v_ref[...] = v

    in_order(own_ref, other_ref, do)


def group_kernel(own_ref, other_ref, all_ref, mid_ref):
    def times(left, right):
        d = dot3(*halves(left), *halves(right))
        return d * (1.0 / jnp.max(d, keepdims=True)[:, :1])

    def do(*mats):
        mid_ref[...] = times(mats[0][...], mats[1][...])
        all_ref[...] = times(mid_ref[...], times(mats[2][...], mats[3][...]))

    in_order(own_ref, other_ref, do)

    @pl.when(lax.axis_index("tm") % 2 == 1)
    def _():
        mid_ref[...] = times(mid_ref[...], other_ref[1])


def hop_kernel(v_ref, m_ref, out_ref):
    out_ref[...] = pass_on(v_ref[...], m_ref[...])


def small(kernel, name, outs, *args):
    return pl.pallas_call(
        kernel,
        out_shape=tuple(jax.ShapeDtypeStruct(shape, F32) for shape in outs),
        in_specs=[vmem()] * len(args),
        out_specs=[vmem()] * len(outs),
        compiler_params=pltpu.CompilerParams(vmem_limit_bytes=4 << 20),
        name=name,
    )(*args)


def pack_kernel(tables, x_hbm, *refs):
    table_hbms, out_ref, table_refs, (x_ref, sems) = refs[:tables], refs[tables], refs[tables + 1 : -2], refs[-2:]
    groups = out_ref.shape[0]
    pairs = [(x_hbm, x_ref), *zip(table_hbms, table_refs)]
    copies = [pltpu.make_async_copy(src, dst, sems.at[i]) for i, (src, dst) in enumerate(pairs)]
    for copy in copies:
        copy.start()
    local = out_ref.shape[2]
    low = lax.broadcasted_iota(jnp.int32, (local, 128), 1) < 64
    for g in range(groups):
        if g == 0:
            copies[0].wait()
        for u in range(2):
            early = x_ref[u, :, g * 256 : g * 256 + 128]
            late = x_ref[u, :, g * 256 + 128 : g * 256 + 256]
            out_ref[g, 2 * u] = jnp.where(low, early, pltpu.roll(late, 64, 1))
            out_ref[g, 2 * u + 1] = jnp.where(low, pltpu.roll(early, 64, 1), late)
    for copy in copies[1:]:
        copy.wait()


def pack(x, groups, *tables):
    local = x.shape[1]
    n = len(tables)
    packed = jax.ShapeDtypeStruct((groups, 4, local, 128), F32)
    return pl.pallas_call(
        functools.partial(pack_kernel, n),
        out_shape=(packed, *(jax.ShapeDtypeStruct(t.shape, t.dtype) for t in tables)),
        in_specs=[hbm()] * (n + 1),
        out_specs=[vmem()] * (n + 1),
        scratch_shapes=[pltpu.VMEM(x.shape, F32), pltpu.SemaphoreType.DMA((groups + n,))],
        compiler_params=pltpu.CompilerParams(vmem_limit_bytes=4 << 20),
        name="pack",
    )(*map(pinned, (x, *tables)))


def slot_kernel(sent, lengths_ref, *refs):
    start_ref, *v_refs = refs[:-9]
    other_ref, mid_ref, pre_ref, e_ref, top_ref, th_ref, tl_ref, out_ref, alpha_scr = refs[len(v_refs) + 1 :]
    states = th_ref.shape[0]
    half = top_ref.shape[1]
    blocks = half // SUB
    index = lax.axis_index("tm")
    utt, slots = place(half)
    slot = 1 - utt if sent else utt

    v = start_ref[...]
    for g, ref in enumerate(v_refs):
        v = jnp.where(index // 4 == g + 1, ref[...], v)
    before = jnp.where(index % 2 == 1, pass_on(v, other_ref[0]), v)
    v = jnp.where(slot == 1, pass_on(v, mid_ref[...]), before)
    rows = [v[0:1]]
    for j in range(blocks - 1):
        rows.append(row_dot(v, pre_ref[slot, j, 0], pre_ref[slot, j, 1])[0:1])
    x = jnp.concatenate(rows, axis=0)
    total = jnp.sum(x, axis=1, keepdims=True)
    th, tl = th_ref[...], tl_ref[...]
    lane = lax.broadcasted_iota(jnp.int32, (blocks, 128), 1)
    sub = lax.broadcasted_iota(jnp.int32, (blocks, 128), 0)
    gains = jnp.zeros((blocks, 128), F32)
    left = frames_of(lengths_ref, utt) - jnp.where(slot == 0, slots[0], slots[1])
    tiles = range(states // 128)
    for r in range(SUB):
        every = pl.ds(r, blocks, stride=SUB)
        factor = jnp.concatenate([e_ref[slot, k, every, :] for k in tiles], axis=1) * (1.0 / total)
        x = row_dot(x, th, tl) * factor
        total = jnp.sum(x, axis=1, keepdims=True)
        alpha = x * (1.0 / total)
        for k in tiles:
            alpha_scr[k, every, :] = alpha[:, k * 128 : (k + 1) * 128]
        live = sub * SUB + r < left
        gain = jnp.where(live, jnp.log(total) + top_ref[slot, every, :], 0.0)
        gains = jnp.where(lane % SUB == r, gain, gains)
    v = unit(v)
    frame = lax.broadcasted_iota(jnp.int32, (half, 128), 0)
    end = pl.ds(jnp.clip(left - 1, 0, half - 1), 1)
    for k in tiles:
        cut = slice(k * 128, (k + 1) * 128)
        final = jnp.where(left > 0, alpha_scr[k, end, :], v[0:1, cut])
        out_ref[0:half, cut] = jnp.log(jnp.where(frame < left, alpha_scr[k], final))
    line = jnp.sum(jnp.where(lane // SUB == sub, gains, 0.0), axis=0, keepdims=True)
    out_ref[half : half + 8, :] = jnp.concatenate([jnp.broadcast_to(line, (8, 128))] * (states // 128), axis=1)


def slot_pass(sent, lengths, vs, other, mid, pre, e, top, th, tl):
    half, states = top.shape[1], th.shape[0]
    return pl.pallas_call(
        functools.partial(slot_kernel, sent),
        out_shape=jax.ShapeDtypeStruct((half + 8, states), F32),
        in_specs=[vmem()] * (len(vs) + 8),
        out_specs=vmem(),
        scratch_shapes=[pltpu.VMEM((states // 128, half, 128), F32)],
        compiler_params=pltpu.CompilerParams(vmem_limit_bytes=6 << 20),
        name="sent" if sent else "kept",
    )(lengths, *vs, other, mid, pre, e, top, th, tl)


def join_kernel(kept_ref, got_ref, log_ref, gain_ref):
    half = log_ref.shape[1]
    utt = (lax.axis_index("tm") // 2) % 2
    log_ref[utt] = kept_ref[0:half, :]
    log_ref[1 - utt] = got_ref[0:half, :]
    own = kept_ref[half : half + 1, 0:half]
    got = got_ref[half : half + 1, 0:half]
    gain_ref[0:1, :] = jnp.where(utt == 0, own, got)
    gain_ref[1:2, :] = jnp.where(utt == 0, got, own)


def shards(size, loglik, trans_weight, block_mask, init_weight, lengths, pdf_map):
    local = loglik.shape[2]
    groups = size // 4
    tables = (pdf_map[None, :], trans_weight, block_mask, lengths[None, :], init_weight[None, :])
    x, *tables = pack(jnp.transpose(loglik, (0, 2, 1)), groups, *tables)
    frames = x.shape[3]
    x = x.reshape(size, local, frames)
    cols = lax.all_to_all(x, "tm", 0, 0, tiled=True).reshape(size * local, frames)
    own, pre, e, top, th, tl, start = transfer(cols, *tables)
    other = lax.ppermute(own, "tm", [(i, i ^ 1) for i in range(size)])
    (v,) = small(first_kernel, "first", [start.shape], start, own, other)
    square = own.shape[1:]
    whole, mid = small(group_kernel, "group", [square, square], own, other)
    vs = [start]
    for g in range(1, groups):
        pairs = [(i, partner(i, g, groups)) for i in range(size)]
        vs.append(lax.ppermute(v, "tm", pairs))
        if g < groups - 1:
            (v,) = small(hop_kernel, "hop", [v.shape], vs[-1], whole)
    given = (tables[3], vs, other, mid, pre, e, top, th, tl)
    sent = slot_pass(True, *given)
    got = lax.ppermute(sent, "tm", [(i, i ^ 2) for i in range(size)])
    kept = slot_pass(False, *given)
    half, states = kept.shape[0] - 8, kept.shape[1]
    return small(join_kernel, "join", [(2, half, states), (2, half)], kept, got)


def partner(index, turn, groups):
    group = index // 4
    other = group ^ 1 if turn % 2 else (group - 1 if group % 2 == 0 else group + 1)
    if 0 <= other < groups:
        return (4 * other + index % 4) ^ 1
    return index ^ 3


def solution(mesh):
    return jax.shard_map(
        functools.partial(shards, mesh.shape["tm"]),
        mesh=mesh,
        in_specs=(P("groups", None, "tm"), P(), P(), P(), P("groups"), P()),
        out_specs=(P("groups", "tm", None), P("groups", "tm")),
        check_vma=False,
    )
```

```python
import functools
import jax
import jax.numpy as jnp
from jax import lax
from jax.experimental import pallas as pl
from jax.experimental.pallas import tpu as pltpu
from jax.sharding import PartitionSpec as P

F32 = jnp.float32
BF16 = jnp.bfloat16
SUB = 8
LARGE, LARGEST, SMALL = 2.0**100, 2.0**126, 2.0**-20


def place(half):
    index = lax.axis_index("tm")
    first = (index // 4) * 4 * half + (index % 2) * half
    return (index // 2) % 2, (first, first + 2 * half)


def frames_of(lengths_ref, utt):
    row = lengths_ref[...].astype(F32)
    here = lax.broadcasted_iota(jnp.int32, row.shape, 1) == utt
    return jnp.sum(jnp.where(here, row, 0.0)).astype(jnp.int32)


def halves(x):
    high = x.astype(BF16)
    return high, (x - high.astype(F32)).astype(BF16)


def dot(a, b):
    return jnp.dot(a, b, preferred_element_type=F32)


def dot3(a_high, a_low, b_high, b_low):
    return dot(a_high, b_high) + dot(a_low, b_high) + dot(a_high, b_low)


def transfer_kernel(
    frames,
    cols_ref,
    map_ref,
    weight_ref,
    mask_ref,
    lengths_ref,
    init_ref,
    mats_ref,
    pre_ref,
    e_ref,
    top_ref,
    th_ref,
    tl_ref,
    start_ref,
    g_scr,
    e_scr,
    t_scr,
    ah,
    al,
    bh,
    bl,
):
    states = weight_ref.shape[0]
    half = frames // 2
    rows = states // 2
    blocks = half // SUB
    utt, slots = place(half)
    cols = cols_ref[...].T
    pick = (lax.broadcasted_iota(jnp.int32, (cols.shape[1], states), 0) == map_ref[...]).astype(F32).astype(BF16)
    p1 = cols.astype(BF16)
    rest = cols - p1.astype(F32)
    p2, p3 = halves(rest)
    depth = 256
    pieces = cols.shape[1] // depth

    def gather(*accs):
        for k in range(pieces):
            cut = slice(k * depth, (k + 1) * depth)
            pltpu.matmul_push_rhs(pick[cut, :], 0, k % 2)
            pltpu.matmul_acc_lhs(accs[k % 2], p1[:, cut], 0)
            pltpu.matmul_acc_lhs(accs[k % 2], p2[:, cut], None)
            pltpu.matmul_acc_lhs(accs[k % 2], p3[:, cut], None)
        g_scr[...] = pltpu.matmul_pop(accs[0]) + pltpu.matmul_pop(accs[1])

    pl.run_scoped(gather, pltpu.ACC(0)((frames, states), F32), pltpu.ACC(1)((frames, states), F32))
    g = g_scr[...]
    top = jnp.max(g, axis=1, keepdims=True)
    e = jnp.exp(g - top)
    e_scr[...] = e
    for i in range(2):
        for k in range(states // 128):
            e_ref[i, k] = e[i * half : (i + 1) * half, k * 128 : (k + 1) * 128]
        top_ref[i] = jnp.broadcast_to(top[i * half : (i + 1) * half], (half, 128))


    nb = mask_ref.shape[0]
    mask = mask_ref[...].astype(F32)
    width = states // nb
    lane = lax.broadcasted_iota(jnp.int32, (1, states), 1) // width
    for r in range(nb):
        row = jnp.zeros((1, states), F32)
        for c in range(nb):
            row = jnp.where(lane == c, mask[r : r + 1, c : c + 1], row)
        part = weight_ref[r * width : (r + 1) * width, :] * row
        t_scr[r * width : (r + 1) * width, :] = part / jnp.sum(part, axis=1, keepdims=True)
    th, tl = halves(t_scr[...])
    th_ref[...] = th
    tl_ref[...] = tl

    alive = [frames_of(lengths_ref, utt) - slot for slot in slots]
    eye = (
        lax.broadcasted_iota(jnp.int32, (states, states), 0) == lax.broadcasted_iota(jnp.int32, (states, states), 1)
    ).astype(F32)
    def body(a0, a1, b0, b1):
        accs = ((a0, a1), (b0, b1))
        mats = ((ah, al), (bh, bl))

        def issue_a(high_loaded):
            for m in range(2):
                sl = pl.ds(m * rows, rows)
                pltpu.matmul_acc_lhs(accs[0][m], ah[sl, :], high_loaded)
                pltpu.matmul_acc_lhs(accs[0][m], al[sl, :], None)
            for m in range(2):
                pltpu.matmul_push_rhs(tl_ref[...], 1, m)
            for m in range(2):
                pltpu.matmul_acc_lhs(accs[0][m], ah[pl.ds(m * rows, rows), :], 1)

        def issue_b():
            for m in range(2):
                pltpu.matmul_acc_lhs(accs[1][m], bh[pl.ds(m * rows, rows), :], None)
            for m in range(2):
                pltpu.matmul_push_rhs(th_ref[...], 0, m)
            for m in range(2):
                sl = pl.ds(m * rows, rows)
                pltpu.matmul_acc_lhs(accs[1][m], bh[sl, :], 0)
                pltpu.matmul_acc_lhs(accs[1][m], bl[sl, :], None)

        def post(k, j, r, carried, freeze, period):
            s = j * SUB + r
            peak, low = carried
            look, use = r % period == (1 + 2 * k) % period, r % period == (2 + 2 * k) % period
            mh, ml = mats[k]
            er = e_scr[pl.ds(s + k * half, 1), :]
            if use:
                size = jnp.max(peak.astype(F32), keepdims=True)[:, :1]
                low = jnp.minimum(low, size)
                er = er * jnp.minimum(LARGE / size, LARGEST)
            live = s < alive[k]
            new = None
            for m in range(2):
                x = pltpu.matmul_pop(accs[k][m]) * er
                h, l = halves(x)
                sl = pl.ds(m * rows, rows)
                if freeze:
                    h = jnp.where(live, h, mh[sl, :])
                    l = jnp.where(live, l, ml[sl, :])
                mh[sl, :] = h
                ml[sl, :] = l
                if r == SUB - 1:
                    pre_ref[k, j, 0, sl, :] = h
                    pre_ref[k, j, 1, sl, :] = l
                if look:
                    y = jnp.max(h.reshape(rows // 16, 16, states), axis=0)
                    new = y if new is None else jnp.maximum(new, y)
            return (new if look else peak), low

        def step(j, r, peaks, freeze, period, last=False):
            pa, pb = peaks
            issue_b()
            pa = post(0, j, r, pa, freeze, period)
            if not last:
                issue_a(None)
            pb = post(1, j, r, pb, freeze, period)
            return pa, pb

        def eight(j, peaks, freeze, period):
            for r in range(1, SUB):
                peaks = step(j, r, peaks, freeze, period)
            return step(j, SUB, peaks, freeze, period)

        def run(period):
            for k, (mh, ml) in enumerate(((ah, al), (bh, bl))):
                off = k * half
                h, l = halves(jnp.where(alive[k] > 0, t_scr[...] * (e_scr[off : off + 1, :] * LARGE), eye))
                mh[0:states, :] = h
                ml[0:states, :] = l

            for m in range(2):
                pltpu.matmul_push_rhs(th_ref[...], 0, m)
            issue_a(0)
            one = jnp.full((16, states), LARGE, BF16), jnp.ones((1, 1), F32)

            def block(j, peaks):
                full = jnp.minimum(alive[0], alive[1]) > j * SUB + SUB
                return lax.cond(
                    full, lambda p: eight(j, p, False, period), lambda p: eight(j, p, True, period), peaks
                )

            def tail(peaks, freeze):
                for r in range(1, SUB):
                    peaks = step(blocks - 1, r, peaks, freeze, period, r == SUB - 1)
                return peaks

            peaks = lax.fori_loop(0, blocks - 1, block, (one, one))
            full = jnp.minimum(alive[0], alive[1]) >= half
            (_, low_a), (_, low_b) = lax.cond(full, lambda p: tail(p, False), lambda p: tail(p, True), peaks)
            low = jnp.minimum(low_a, low_b)
            for mh, _ in mats:
                low = jnp.minimum(low, jnp.max(mh[...].astype(F32), keepdims=True)[:, :1])
            return jnp.min(low)

        lowest = run(4)

        @pl.when(lowest < SMALL)
        def _():
            run(1)

        start_ref[...] = jnp.broadcast_to(unit(init_ref[...]), start_ref.shape)
        for i, (mh, ml) in enumerate(mats):
            full = mh[...].astype(F32) + ml[...].astype(F32)
            mats_ref[i] = full * (1.0 / jnp.max(full, keepdims=True)[:, :1])

    shape = (rows, states)
    pl.run_scoped(
        body,
        pltpu.ACC(0)(shape, F32),
        pltpu.ACC(1)(shape, F32),
        pltpu.ACC(0)(shape, F32),
        pltpu.ACC(1)(shape, F32),
    )


def vmem():
    return pl.BlockSpec(memory_space=pltpu.VMEM)


def hbm():
    return pl.BlockSpec(memory_space=pltpu.MemorySpace.HBM)


def pinned(x):
    return pltpu.with_memory_space_constraint(x, pltpu.MemorySpace.HBM)


def transfer(cols, columns_of, weight, mask, lengths, init):
    columns, frames = cols.shape
    states = weight.shape[0]
    blocks = frames // 2 // SUB
    out = jax.ShapeDtypeStruct
    return pl.pallas_call(
        functools.partial(transfer_kernel, frames),
        out_shape=(
            out((2, states, states), F32),
            out((2, blocks, 2, states, states), BF16),
            out((2, states // 128, frames // 2, 128), F32),
            out((2, frames // 2, 128), F32),
            out((states, states), BF16),
            out((states, states), BF16),
            out((8, states), F32),
        ),
        in_specs=[vmem()] * 6,
        out_specs=[vmem()] * 7,
        scratch_shapes=[pltpu.VMEM((frames, states), F32)] * 2
        + [pltpu.VMEM((states, states), F32)]
        + [pltpu.VMEM((states, states), BF16)] * 4,
        compiler_params=pltpu.CompilerParams(vmem_limit_bytes=6 << 20),
        name="transfer",
    )(cols, columns_of, weight, mask, lengths, init)


def row_dot(v, matrix_high, matrix_low):
    n = v.shape[0]
    both = jnp.concatenate(halves(v), axis=0)
    x = dot(both, matrix_high)
    y = dot(both, matrix_low)
    return x[0:n] + x[n:] + y[0:n]


def unit(v):
    return v / jnp.sum(v, axis=1, keepdims=True)


def pass_on(v, matrix):
    return row_dot(v, *halves(matrix)) * (1.0 / jnp.sum(v, axis=1, keepdims=True))


def in_order(own_ref, other_ref, do):
    core = lax.axis_index("tm") % 2

    @pl.when(core == 0)
    def _():
        do(own_ref.at[0], other_ref.at[0], own_ref.at[1], other_ref.at[1])

    @pl.when(core == 1)
    def _():
        do(other_ref.at[0], own_ref.at[0], other_ref.at[1], own_ref.at[1])


def first_kernel(start_ref, own_ref, other_ref, v_ref):
    def do(*mats):
        v = start_ref[...]
        for m in mats:
            v = pass_on(v, m[...])
        v_ref[...] = v

    in_order(own_ref, other_ref, do)


def group_kernel(own_ref, other_ref, all_ref, mid_ref):
    def times(left, right):
        d = dot3(*halves(left), *halves(right))
        return d * (1.0 / jnp.max(d, keepdims=True)[:, :1])

    def do(*mats):
        mid_ref[...] = times(mats[0][...], mats[1][...])
        all_ref[...] = times(mid_ref[...], times(mats[2][...], mats[3][...]))

    in_order(own_ref, other_ref, do)

    @pl.when(lax.axis_index("tm") % 2 == 1)
    def _():
        mid_ref[...] = times(mid_ref[...], other_ref[1])


def hop_kernel(v_ref, m_ref, out_ref):
    out_ref[...] = pass_on(v_ref[...], m_ref[...])


def small(kernel, name, outs, *args):
    return pl.pallas_call(
        kernel,
        out_shape=tuple(jax.ShapeDtypeStruct(shape, F32) for shape in outs),
        in_specs=[vmem()] * len(args),
        out_specs=[vmem()] * len(outs),
        compiler_params=pltpu.CompilerParams(vmem_limit_bytes=4 << 20),
        name=name,
    )(*args)


def pack_kernel(tables, x_hbm, *refs):
    table_hbms, out_ref, table_refs, (x_ref, sems) = refs[:tables], refs[tables], refs[tables + 1 : -2], refs[-2:]
    groups = out_ref.shape[0]
    pairs = [(x_hbm, x_ref), *zip(table_hbms, table_refs)]
    copies = [pltpu.make_async_copy(src, dst, sems.at[i]) for i, (src, dst) in enumerate(pairs)]
    for copy in copies:
        copy.start()
    local = out_ref.shape[2]
    low = lax.broadcasted_iota(jnp.int32, (local, 128), 1) < 64
    for g in range(groups):
        if g == 0:
            copies[0].wait()
        for u in range(2):
            early = x_ref[u, :, g * 256 : g * 256 + 128]
            late = x_ref[u, :, g * 256 + 128 : g * 256 + 256]
            out_ref[g, 2 * u] = jnp.where(low, early, pltpu.roll(late, 64, 1))
            out_ref[g, 2 * u + 1] = jnp.where(low, pltpu.roll(early, 64, 1), late)
    for copy in copies[1:]:
        copy.wait()


def pack(x, groups, *tables):
    local = x.shape[1]
    n = len(tables)
    packed = jax.ShapeDtypeStruct((groups, 4, local, 128), F32)
    return pl.pallas_call(
        functools.partial(pack_kernel, n),
        out_shape=(packed, *(jax.ShapeDtypeStruct(t.shape, t.dtype) for t in tables)),
        in_specs=[hbm()] * (n + 1),
        out_specs=[vmem()] * (n + 1),
        scratch_shapes=[pltpu.VMEM(x.shape, F32), pltpu.SemaphoreType.DMA((groups + n,))],
        compiler_params=pltpu.CompilerParams(vmem_limit_bytes=4 << 20),
        name="pack",
    )(*map(pinned, (x, *tables)))


def slot_kernel(sent, lengths_ref, *refs):
    start_ref, *v_refs = refs[:-9]
    other_ref, mid_ref, pre_ref, e_ref, top_ref, th_ref, tl_ref, out_ref, alpha_scr = refs[len(v_refs) + 1 :]
    states = th_ref.shape[0]
    half = top_ref.shape[1]
    blocks = half // SUB
    index = lax.axis_index("tm")
    utt, slots = place(half)
    slot = 1 - utt if sent else utt

    v = start_ref[...]
    for g, ref in enumerate(v_refs):
        v = jnp.where(index // 4 == g + 1, ref[...], v)
    before = jnp.where(index % 2 == 1, pass_on(v, other_ref[0]), v)
    v = jnp.where(slot == 1, pass_on(v, mid_ref[...]), before)
    rows = [v[0:1]]
    for j in range(blocks - 1):
        rows.append(row_dot(v, pre_ref[slot, j, 0], pre_ref[slot, j, 1])[0:1])
    x = unit(jnp.concatenate(rows, axis=0))
    th, tl = th_ref[...], tl_ref[...]
    lane = lax.broadcasted_iota(jnp.int32, (blocks, 128), 1)
    sub = lax.broadcasted_iota(jnp.int32, (blocks, 128), 0)
    gains = jnp.zeros((blocks, 128), F32)
    left = frames_of(lengths_ref, utt) - jnp.where(slot == 0, slots[0], slots[1])
    tiles = range(states // 128)
    for r in range(SUB):
        every = pl.ds(r, blocks, stride=SUB)
        factor = jnp.concatenate([e_ref[slot, k, every, :] for k in tiles], axis=1)
        if r:
            factor = factor * (1.0 / total)
        x = row_dot(x, th, tl) * factor
        total = jnp.sum(x, axis=1, keepdims=True)
        alpha = x * (1.0 / total)
        for k in tiles:
            alpha_scr[k, every, :] = alpha[:, k * 128 : (k + 1) * 128]
        live = sub * SUB + r < left
        gain = jnp.where(live, jnp.log(total) + top_ref[slot, every, :], 0.0)
        gains = jnp.where(lane % SUB == r, gain, gains)
    v = unit(v)
    frame = lax.broadcasted_iota(jnp.int32, (half, 128), 0)
    end = pl.ds(jnp.clip(left - 1, 0, half - 1), 1)
    for k in tiles:
        cut = slice(k * 128, (k + 1) * 128)
        final = jnp.where(left > 0, alpha_scr[k, end, :], v[0:1, cut])
        out_ref[0:half, cut] = jnp.log(jnp.where(frame < left, alpha_scr[k], final))
    line = jnp.sum(jnp.where(lane // SUB == sub, gains, 0.0), axis=0, keepdims=True)
    out_ref[half : half + 8, :] = jnp.concatenate([jnp.broadcast_to(line, (8, 128))] * (states // 128), axis=1)


def slot_pass(sent, lengths, vs, other, mid, pre, e, top, th, tl):
    half, states = top.shape[1], th.shape[0]
    return pl.pallas_call(
        functools.partial(slot_kernel, sent),
        out_shape=jax.ShapeDtypeStruct((half + 8, states), F32),
        in_specs=[vmem()] * (len(vs) + 8),
        out_specs=vmem(),
        scratch_shapes=[pltpu.VMEM((states // 128, half, 128), F32)],
        compiler_params=pltpu.CompilerParams(vmem_limit_bytes=6 << 20),
        name="sent" if sent else "kept",
    )(lengths, *vs, other, mid, pre, e, top, th, tl)


def join_kernel(kept_ref, got_ref, log_ref, gain_ref):
    half = log_ref.shape[1]
    utt = (lax.axis_index("tm") // 2) % 2
    log_ref[utt] = kept_ref[0:half, :]
    log_ref[1 - utt] = got_ref[0:half, :]
    own = kept_ref[half : half + 1, 0:half]
    got = got_ref[half : half + 1, 0:half]
    gain_ref[0:1, :] = jnp.where(utt == 0, own, got)
    gain_ref[1:2, :] = jnp.where(utt == 0, got, own)


def shards(size, loglik, trans_weight, block_mask, init_weight, lengths, pdf_map):
    local = loglik.shape[2]
    groups = size // 4
    tables = (pdf_map[None, :], trans_weight, block_mask, lengths[None, :], init_weight[None, :])
    x, *tables = pack(jnp.transpose(loglik, (0, 2, 1)), groups, *tables)
    frames = x.shape[3]
    x = x.reshape(size, local, frames)
    cols = lax.all_to_all(x, "tm", 0, 0, tiled=True).reshape(size * local, frames)
    own, pre, e, top, th, tl, start = transfer(cols, *tables)
    other = lax.ppermute(own, "tm", [(i, i ^ 1) for i in range(size)])
    (v,) = small(first_kernel, "first", [start.shape], start, own, other)
    square = own.shape[1:]
    whole, mid = small(group_kernel, "group", [square, square], own, other)
    vs = [start]
    for g in range(1, groups):
        pairs = [(i, partner(i, g, groups)) for i in range(size)]
        vs.append(lax.ppermute(v, "tm", pairs))
        if g < groups - 1:
            (v,) = small(hop_kernel, "hop", [v.shape], vs[-1], whole)
    given = (tables[3], vs, other, mid, pre, e, top, th, tl)
    sent = slot_pass(True, *given)
    got = lax.ppermute(sent, "tm", [(i, i ^ 2) for i in range(size)])
    kept = slot_pass(False, *given)
    half, states = kept.shape[0] - 8, kept.shape[1]
    return small(join_kernel, "join", [(2, half, states), (2, half)], kept, got)


def partner(index, turn, groups):
    group = index // 4
    other = group ^ 1 if turn % 2 else (group - 1 if group % 2 == 0 else group + 1)
    if 0 <= other < groups:
        return (4 * other + index % 4) ^ 1
    return index ^ 3


def solution(mesh):
    return jax.shard_map(
        functools.partial(shards, mesh.shape["tm"]),
        mesh=mesh,
        in_specs=(P("groups", None, "tm"), P(), P(), P(), P("groups"), P()),
        out_specs=(P("groups", "tm", None), P("groups", "tm")),
        check_vma=False,
    )
```

```python
import functools
import jax
import jax.numpy as jnp
from jax import lax
from jax.experimental import pallas as pl
from jax.experimental.pallas import tpu as pltpu
from jax.sharding import PartitionSpec as P

F32 = jnp.float32
BF16 = jnp.bfloat16
SUB = 8
LARGE, LARGEST, SMALL = 2.0**100, 2.0**126, 2.0**-20


def place(half):
    index = lax.axis_index("tm")
    first = (index // 4) * 4 * half + (index % 2) * half
    return (index // 2) % 2, (first, first + 2 * half)


def frames_of(lengths_ref, utt):
    row = lengths_ref[...].astype(F32)
    here = lax.broadcasted_iota(jnp.int32, row.shape, 1) == utt
    return jnp.sum(jnp.where(here, row, 0.0)).astype(jnp.int32)


def halves(x):
    high = x.astype(BF16)
    return high, (x - high.astype(F32)).astype(BF16)


def dot(a, b):
    return jnp.dot(a, b, preferred_element_type=F32)


def dot3(a_high, a_low, b_high, b_low):
    return dot(a_high, b_high) + dot(a_low, b_high) + dot(a_high, b_low)


def transfer_kernel(
    frames,
    cols_ref,
    map_ref,
    weight_ref,
    mask_ref,
    lengths_ref,
    init_ref,
    mats_ref,
    pre_ref,
    e_ref,
    top_ref,
    th_ref,
    tl_ref,
    start_ref,
    g_scr,
    e_scr,
    t_scr,
    ah,
    al,
    bh,
    bl,
):
    states = weight_ref.shape[0]
    half = frames // 2
    rows = states // 2
    blocks = half // SUB
    utt, slots = place(half)
    cols = cols_ref[...].T
    pick = (lax.broadcasted_iota(jnp.int32, (cols.shape[1], states), 0) == map_ref[...]).astype(F32).astype(BF16)
    p1 = cols.astype(BF16)
    rest = cols - p1.astype(F32)
    p2, p3 = halves(rest)
    depth = 256
    pieces = cols.shape[1] // depth

    def gather(*accs):
        for k in range(pieces):
            cut = slice(k * depth, (k + 1) * depth)
            pltpu.matmul_push_rhs(pick[cut, :], 0, k % 2)
            pltpu.matmul_acc_lhs(accs[k % 2], p1[:, cut], 0)
            pltpu.matmul_acc_lhs(accs[k % 2], p2[:, cut], None)
            pltpu.matmul_acc_lhs(accs[k % 2], p3[:, cut], None)
        g_scr[...] = pltpu.matmul_pop(accs[0]) + pltpu.matmul_pop(accs[1])

    pl.run_scoped(gather, pltpu.ACC(0)((frames, states), F32), pltpu.ACC(1)((frames, states), F32))
    g = g_scr[...]
    top = jnp.max(g, axis=1, keepdims=True)
    e = jnp.exp(g - top)
    e_scr[...] = e
    for i in range(2):
        for k in range(states // 128):
            e_ref[i, k] = e[i * half : (i + 1) * half, k * 128 : (k + 1) * 128]
        top_ref[i] = jnp.broadcast_to(top[i * half : (i + 1) * half], (half, 128))


    nb = mask_ref.shape[0]
    mask = mask_ref[...].astype(F32)
    width = states // nb
    lane = lax.broadcasted_iota(jnp.int32, (1, states), 1) // width
    for r in range(nb):
        row = jnp.zeros((1, states), F32)
        for c in range(nb):
            row = jnp.where(lane == c, mask[r : r + 1, c : c + 1], row)
        part = weight_ref[r * width : (r + 1) * width, :] * row
        t_scr[r * width : (r + 1) * width, :] = part / jnp.sum(part, axis=1, keepdims=True)
    th, tl = halves(t_scr[...])
    th_ref[...] = th
    tl_ref[...] = tl

    alive = [frames_of(lengths_ref, utt) - slot for slot in slots]
    eye = (
        lax.broadcasted_iota(jnp.int32, (states, states), 0) == lax.broadcasted_iota(jnp.int32, (states, states), 1)
    ).astype(F32)
    def body(a0, a1, b0, b1):
        accs = ((a0, a1), (b0, b1))
        mats = ((ah, al), (bh, bl))

        def issue_a(high_loaded):
            for m in range(2):
                sl = pl.ds(m * rows, rows)
                pltpu.matmul_acc_lhs(accs[0][m], ah[sl, :], high_loaded)
                pltpu.matmul_acc_lhs(accs[0][m], al[sl, :], None)
            for m in range(2):
                pltpu.matmul_push_rhs(tl_ref[...], 1, m)
            for m in range(2):
                pltpu.matmul_acc_lhs(accs[0][m], ah[pl.ds(m * rows, rows), :], 1)

        def issue_b():
            for m in range(2):
                pltpu.matmul_acc_lhs(accs[1][m], bh[pl.ds(m * rows, rows), :], None)
            for m in range(2):
                pltpu.matmul_push_rhs(th_ref[...], 0, m)
            for m in range(2):
                sl = pl.ds(m * rows, rows)
                pltpu.matmul_acc_lhs(accs[1][m], bh[sl, :], 0)
                pltpu.matmul_acc_lhs(accs[1][m], bl[sl, :], None)

        def post(k, j, r, carried, freeze, period):
            s = j * SUB + r
            peak, low = carried
            look, use = r % period == (1 + 2 * k) % period, r % period == (2 + 2 * k) % period
            mh, ml = mats[k]
            er = e_scr[pl.ds(s + k * half, 1), :]
            if use:
                size = jnp.max(peak.astype(F32), keepdims=True)[:, :1]
                low = jnp.minimum(low, size)
                er = er * jnp.minimum(LARGE / size, LARGEST)
            live = s < alive[k]
            new = None
            for m in range(2):
                x = pltpu.matmul_pop(accs[k][m]) * er
                h, l = halves(x)
                sl = pl.ds(m * rows, rows)
                if freeze:
                    h = jnp.where(live, h, mh[sl, :])
                    l = jnp.where(live, l, ml[sl, :])
                mh[sl, :] = h
                ml[sl, :] = l
                if r == SUB - 1:
                    pre_ref[k, j, 0, sl, :] = h
                    pre_ref[k, j, 1, sl, :] = l
                if look:
                    y = jnp.max(h.reshape(rows // 16, 16, states), axis=0)
                    new = y if new is None else jnp.maximum(new, y)
            return (new if look else peak), low

        def step(j, r, peaks, freeze, period, last=False):
            pa, pb = peaks
            issue_b()
            pa = post(0, j, r, pa, freeze, period)
            if not last:
                issue_a(None)
            pb = post(1, j, r, pb, freeze, period)
            return pa, pb

        def eight(j, peaks, freeze, period):
            for r in range(1, SUB):
                peaks = step(j, r, peaks, freeze, period)
            return step(j, SUB, peaks, freeze, period)

        def run(period):
            for k, (mh, ml) in enumerate(((ah, al), (bh, bl))):
                off = k * half
                h, l = halves(jnp.where(alive[k] > 0, t_scr[...] * (e_scr[off : off + 1, :] * LARGE), eye))
                mh[0:states, :] = h
                ml[0:states, :] = l

            for m in range(2):
                pltpu.matmul_push_rhs(th_ref[...], 0, m)
            issue_a(0)
            one = jnp.full((16, states), LARGE, BF16), jnp.ones((1, 1), F32)

            def block(j, peaks):
                full = jnp.minimum(alive[0], alive[1]) > j * SUB + SUB
                return lax.cond(
                    full, lambda p: eight(j, p, False, period), lambda p: eight(j, p, True, period), peaks
                )

            def tail(peaks, freeze):
                for r in range(1, SUB):
                    peaks = step(blocks - 1, r, peaks, freeze, period, r == SUB - 1)
                return peaks

            peaks = lax.fori_loop(0, blocks - 1, block, (one, one))
            full = jnp.minimum(alive[0], alive[1]) >= half
            (_, low_a), (_, low_b) = lax.cond(full, lambda p: tail(p, False), lambda p: tail(p, True), peaks)
            low = jnp.minimum(low_a, low_b)
            for i, (mh, ml) in enumerate(mats):
                both = mh[...].astype(F32) + ml[...].astype(F32)
                size = jnp.max(both, keepdims=True)[:, :1]
                mats_ref[i] = both * (1.0 / size)
                low = jnp.minimum(low, size)
            return jnp.min(low)

        start_ref[...] = jnp.broadcast_to(unit(init_ref[...]), start_ref.shape)
        lowest = run(4)

        @pl.when(lowest < SMALL)
        def _():
            run(1)


    shape = (rows, states)
    pl.run_scoped(
        body,
        pltpu.ACC(0)(shape, F32),
        pltpu.ACC(1)(shape, F32),
        pltpu.ACC(0)(shape, F32),
        pltpu.ACC(1)(shape, F32),
    )


def vmem():
    return pl.BlockSpec(memory_space=pltpu.VMEM)


def hbm():
    return pl.BlockSpec(memory_space=pltpu.MemorySpace.HBM)


def pinned(x):
    return pltpu.with_memory_space_constraint(x, pltpu.MemorySpace.HBM)


def transfer(cols, columns_of, weight, mask, lengths, init):
    columns, frames = cols.shape
    states = weight.shape[0]
    blocks = frames // 2 // SUB
    out = jax.ShapeDtypeStruct
    return pl.pallas_call(
        functools.partial(transfer_kernel, frames),
        out_shape=(
            out((2, states, states), F32),
            out((2, blocks, 2, states, states), BF16),
            out((2, states // 128, frames // 2, 128), F32),
            out((2, frames // 2, 128), F32),
            out((states, states), BF16),
            out((states, states), BF16),
            out((8, states), F32),
        ),
        in_specs=[vmem()] * 6,
        out_specs=[vmem()] * 7,
        scratch_shapes=[pltpu.VMEM((frames, states), F32)] * 2
        + [pltpu.VMEM((states, states), F32)]
        + [pltpu.VMEM((states, states), BF16)] * 4,
        compiler_params=pltpu.CompilerParams(vmem_limit_bytes=6 << 20),
        name="transfer",
    )(cols, columns_of, weight, mask, lengths, init)


def row_dot(v, matrix_high, matrix_low):
    n = v.shape[0]
    both = jnp.concatenate(halves(v), axis=0)
    x = dot(both, matrix_high)
    y = dot(both, matrix_low)
    return x[0:n] + x[n:] + y[0:n]


def unit(v):
    return v / jnp.sum(v, axis=1, keepdims=True)


def pass_on(v, matrix):
    return row_dot(v, *halves(matrix)) * (1.0 / jnp.sum(v, axis=1, keepdims=True))


def in_order(own_ref, other_ref, do):
    core = lax.axis_index("tm") % 2

    @pl.when(core == 0)
    def _():
        do(own_ref.at[0], other_ref.at[0], own_ref.at[1], other_ref.at[1])

    @pl.when(core == 1)
    def _():
        do(other_ref.at[0], own_ref.at[0], other_ref.at[1], own_ref.at[1])


def first_kernel(start_ref, own_ref, other_ref, v_ref):
    def do(*mats):
        v = start_ref[...]
        for m in mats:
            v = pass_on(v, m[...])
        v_ref[...] = v

    in_order(own_ref, other_ref, do)


def group_kernel(own_ref, other_ref, all_ref, mid_ref):
    def times(left, right):
        d = dot3(*halves(left), *halves(right))
        return d * (1.0 / jnp.max(d, keepdims=True)[:, :1])

    def do(*mats):
        mid_ref[...] = times(mats[0][...], mats[1][...])
        all_ref[...] = times(mid_ref[...], times(mats[2][...], mats[3][...]))

    in_order(own_ref, other_ref, do)

    @pl.when(lax.axis_index("tm") % 2 == 1)
    def _():
        mid_ref[...] = times(mid_ref[...], other_ref[1])


def hop_kernel(v_ref, m_ref, out_ref):
    out_ref[...] = pass_on(v_ref[...], m_ref[...])


def small(kernel, name, outs, *args):
    return pl.pallas_call(
        kernel,
        out_shape=tuple(jax.ShapeDtypeStruct(shape, F32) for shape in outs),
        in_specs=[vmem()] * len(args),
        out_specs=[vmem()] * len(outs),
        compiler_params=pltpu.CompilerParams(vmem_limit_bytes=4 << 20),
        name=name,
    )(*args)


def pack_kernel(tables, x_hbm, *refs):
    table_hbms, out_ref, table_refs, (x_ref, sems) = refs[:tables], refs[tables], refs[tables + 1 : -2], refs[-2:]
    groups = out_ref.shape[0]
    pairs = [(x_hbm, x_ref), *zip(table_hbms, table_refs)]
    copies = [pltpu.make_async_copy(src, dst, sems.at[i]) for i, (src, dst) in enumerate(pairs)]
    for copy in copies:
        copy.start()
    local = out_ref.shape[2]
    low = lax.broadcasted_iota(jnp.int32, (local, 128), 1) < 64
    for g in range(groups):
        if g == 0:
            copies[0].wait()
        for u in range(2):
            early = x_ref[u, :, g * 256 : g * 256 + 128]
            late = x_ref[u, :, g * 256 + 128 : g * 256 + 256]
            out_ref[g, 2 * u] = jnp.where(low, early, pltpu.roll(late, 64, 1))
            out_ref[g, 2 * u + 1] = jnp.where(low, pltpu.roll(early, 64, 1), late)
    for copy in copies[1:]:
        copy.wait()


def pack(x, groups, *tables):
    local = x.shape[1]
    n = len(tables)
    packed = jax.ShapeDtypeStruct((groups, 4, local, 128), F32)
    return pl.pallas_call(
        functools.partial(pack_kernel, n),
        out_shape=(packed, *(jax.ShapeDtypeStruct(t.shape, t.dtype) for t in tables)),
        in_specs=[hbm()] * (n + 1),
        out_specs=[vmem()] * (n + 1),
        scratch_shapes=[pltpu.VMEM(x.shape, F32), pltpu.SemaphoreType.DMA((groups + n,))],
        compiler_params=pltpu.CompilerParams(vmem_limit_bytes=4 << 20),
        name="pack",
    )(*map(pinned, (x, *tables)))


def slot_kernel(sent, lengths_ref, *refs):
    start_ref, *v_refs = refs[:-9]
    other_ref, mid_ref, pre_ref, e_ref, top_ref, th_ref, tl_ref, out_ref, alpha_scr = refs[len(v_refs) + 1 :]
    states = th_ref.shape[0]
    half = top_ref.shape[1]
    blocks = half // SUB
    index = lax.axis_index("tm")
    utt, slots = place(half)
    slot = 1 - utt if sent else utt

    v = start_ref[...]
    for g, ref in enumerate(v_refs):
        v = jnp.where(index // 4 == g + 1, ref[...], v)
    before = jnp.where(index % 2 == 1, pass_on(v, other_ref[0]), v)
    v = jnp.where(slot == 1, pass_on(v, mid_ref[...]), before)
    rows = [v[0:1]]
    for j in range(blocks - 1):
        rows.append(row_dot(v, pre_ref[slot, j, 0], pre_ref[slot, j, 1])[0:1])
    x = unit(jnp.concatenate(rows, axis=0))
    th, tl = th_ref[...], tl_ref[...]
    lane = lax.broadcasted_iota(jnp.int32, (blocks, 128), 1)
    sub = lax.broadcasted_iota(jnp.int32, (blocks, 128), 0)
    gains = jnp.zeros((blocks, 128), F32)
    left = frames_of(lengths_ref, utt) - jnp.where(slot == 0, slots[0], slots[1])
    tiles = range(states // 128)
    for r in range(SUB):
        every = pl.ds(r, blocks, stride=SUB)
        factor = jnp.concatenate([e_ref[slot, k, every, :] for k in tiles], axis=1)
        if r:
            factor = factor * (1.0 / total)
        x = row_dot(x, th, tl) * factor
        total = jnp.sum(x, axis=1, keepdims=True)
        alpha = x * (1.0 / total)
        for k in tiles:
            alpha_scr[k, every, :] = alpha[:, k * 128 : (k + 1) * 128]
        live = sub * SUB + r < left
        gain = jnp.where(live, jnp.log(total) + top_ref[slot, every, :], 0.0)
        gains = jnp.where(lane % SUB == r, gain, gains)
    v = unit(v)
    frame = lax.broadcasted_iota(jnp.int32, (half, 128), 0)
    end = pl.ds(jnp.clip(left - 1, 0, half - 1), 1)
    for k in tiles:
        cut = slice(k * 128, (k + 1) * 128)
        final = jnp.where(left > 0, alpha_scr[k, end, :], v[0:1, cut])
        out_ref[0:half, cut] = jnp.log(jnp.where(frame < left, alpha_scr[k], final))
    line = jnp.sum(jnp.where(lane // SUB == sub, gains, 0.0), axis=0, keepdims=True)
    out_ref[half : half + 8, :] = jnp.concatenate([jnp.broadcast_to(line, (8, 128))] * (states // 128), axis=1)


def slot_pass(sent, lengths, vs, other, mid, pre, e, top, th, tl):
    half, states = top.shape[1], th.shape[0]
    return pl.pallas_call(
        functools.partial(slot_kernel, sent),
        out_shape=jax.ShapeDtypeStruct((half + 8, states), F32),
        in_specs=[vmem()] * (len(vs) + 8),
        out_specs=vmem(),
        scratch_shapes=[pltpu.VMEM((states // 128, half, 128), F32)],
        compiler_params=pltpu.CompilerParams(vmem_limit_bytes=6 << 20),
        name="sent" if sent else "kept",
    )(lengths, *vs, other, mid, pre, e, top, th, tl)


def join_kernel(kept_ref, got_ref, log_ref, gain_ref):
    half = log_ref.shape[1]
    utt = (lax.axis_index("tm") // 2) % 2
    log_ref[utt] = kept_ref[0:half, :]
    log_ref[1 - utt] = got_ref[0:half, :]
    own = kept_ref[half : half + 1, 0:half]
    got = got_ref[half : half + 1, 0:half]
    gain_ref[0:1, :] = jnp.where(utt == 0, own, got)
    gain_ref[1:2, :] = jnp.where(utt == 0, got, own)


def shards(size, loglik, trans_weight, block_mask, init_weight, lengths, pdf_map):
    local = loglik.shape[2]
    groups = size // 4
    tables = (pdf_map[None, :], trans_weight, block_mask, lengths[None, :], init_weight[None, :])
    x, *tables = pack(jnp.transpose(loglik, (0, 2, 1)), groups, *tables)
    frames = x.shape[3]
    x = x.reshape(size, local, frames)
    cols = lax.all_to_all(x, "tm", 0, 0, tiled=True).reshape(size * local, frames)
    own, pre, e, top, th, tl, start = transfer(cols, *tables)
    other = lax.ppermute(own, "tm", [(i, i ^ 1) for i in range(size)])
    (v,) = small(first_kernel, "first", [start.shape], start, own, other)
    square = own.shape[1:]
    whole, mid = small(group_kernel, "group", [square, square], own, other)
    vs = [start]
    for g in range(1, groups):
        pairs = [(i, partner(i, g, groups)) for i in range(size)]
        vs.append(lax.ppermute(v, "tm", pairs))
        if g < groups - 1:
            (v,) = small(hop_kernel, "hop", [v.shape], vs[-1], whole)
    given = (tables[3], vs, other, mid, pre, e, top, th, tl)
    sent = slot_pass(True, *given)
    got = lax.ppermute(sent, "tm", [(i, i ^ 2) for i in range(size)])
    kept = slot_pass(False, *given)
    half, states = kept.shape[0] - 8, kept.shape[1]
    return small(join_kernel, "join", [(2, half, states), (2, half)], kept, got)


def partner(index, turn, groups):
    group = index // 4
    other = group ^ 1 if turn % 2 else (group - 1 if group % 2 == 0 else group + 1)
    if 0 <= other < groups:
        return (4 * other + index % 4) ^ 1
    return index ^ 3


def solution(mesh):
    return jax.shard_map(
        functools.partial(shards, mesh.shape["tm"]),
        mesh=mesh,
        in_specs=(P("groups", None, "tm"), P(), P(), P(), P("groups"), P()),
        out_specs=(P("groups", "tm", None), P("groups", "tm")),
        check_vma=False,
    )
```
